32 devices in a mesh: groups: 2 (over y), gx: 4 (over z), gy: 2 (over x), gz: 2 (over core).
Axes of the slice: x: 2, y: 2, z: 4, core: 2. Of those that a mesh axis runs over, the one named last changes fastest.
Arguments:
- fields: float32 [6, 16, 64, 256], P(None, ('groups', 'gx'), 'gy', 'gz'), parts along dimension 1, may hold values from -6 to 6
- adjoint: float32 [6, 16, 64, 256], P(None, ('groups', 'gx'), 'gy', 'gz'), parts along dimension 1, may hold values from -6 to 6
- inv_eps: float32 [16, 64, 256], P(('groups', 'gx'), 'gy', 'gz'), parts along dimension 0, may hold values from 0.3 to 1
- loss_level: int32 [16, 64, 256], P(('groups', 'gx'), 'gy', 'gz'), parts along dimension 0, may hold values from 0 to 3
- direction: float32 [3, 512], replicated, may hold values from -1 to 1
- pattern_weight: float32 [512], replicated, may hold values from 2 to 20
- voxel_cell: int32 [8, 2, 2, 4, 8], P(('groups', 'gx'), 'gy', 'gz'), parts along dimension 0, may hold values from 62 to 8129, as said below
- voxel_elem: int32 [8, 2, 2, 4, 8], P(('groups', 'gx'), 'gy', 'gz'), parts along dimension 0, may hold values from -1 to 255, as said below
Outputs:
- fields_out: float32 [6, 16, 64, 256], P(None, ('groups', 'gx'), 'gy', 'gz'), parts along dimension 1
- pattern: float32 [1024], P('groups'), parts along dimension 0
- elem_grad: float32 [2048], P(('groups', 'gx')), parts along dimension 0
The draws below stay inside these ranges and needn't reach their ends.
There are 2 independent parts, one for each index of `groups`. The reference program is written for one: setup_inputs(seed, part) draws one part's arguments, and reference() takes and returns one part's arrays. A program takes and returns all parts, laid end to end along the dimension named above; an argument that names none is the same for every part. Nothing has to cross between parts.
Inputs may be any that keep to these rules, and one draw needn't show every extreme that they name: `voxel_cell`: each entry is the local number of a cell whose third local index is one of 62 .. 65; the entries of one source block are all different. `voxel_elem`: in each list of 8 slots the live ones (not -1) come first. In every draw, each block's list to the owner of its own slab is full, and so are all lists to one further owner.
All inputs are finite; a program needn't handle non-finite values.
Results may differ from the reference program's by a relative error of at most 0.0003.
Values sent between devices are 32-bit elements; how exact they have to be, the bound alone decides.
No kernel may reach another device: no remote copies, remote signals or barrier semaphores. Data moves between devices by JAX's collectives and lax.ppermute only.
A program may use at most 64 MiB of HBM per device.

```python
import math
import jax
import jax.numpy as jnp
from jax import lax

CX = 2
CY = 32
CZ = 128
STEPS = 2
SLOTS = 8
NE = 1024
ND = 512
NX = 8
NY = 64
NZ = 256
N_GX = 4
N_GY = 2
N_GZ = 2


def voxel_tables(key):
    ngx = NX // CX
    ngy = NY // CY
    ngz = NZ // CZ
    layer = 4 * CX * CY
    base = jax.random.fold_in(key, 7)
    key_count, key_full, key_perm, key_elem = jax.random.split(base, 4)
    counts = jax.random.randint(key_count, (ngx, ngy, ngz, ngx), max(1, SLOTS // 3), SLOTS + 1)
    full_owner = jax.random.randint(key_full, (), 0, ngx)
    source = jnp.arange(ngx)[:, None, None, None]
    owner = jnp.arange(ngx)[None, None, None, :]
    counts = jnp.where((owner == source) | (owner == full_owner), SLOTS, counts)
    keys = jax.random.split(key_perm, ngx * ngy * ngz)
    picks = jax.vmap(lambda one: jax.random.permutation(one, layer)[:ngx * SLOTS])(keys)
    picks = picks.reshape(ngx, ngy, ngz, ngx, SLOTS)
    xpos = picks // (CY * 4)
    ypos = picks // 4 % CY
    zpos = CZ // 2 - 2 + picks % 4
    cell = (xpos * CY + ypos) * CZ + zpos
    elem = jax.random.randint(key_elem, (ngx, ngy, ngz, ngx, SLOTS), 0, NE // ngx)
    slot = jnp.arange(SLOTS)
    elem = jnp.where(slot < counts[..., None], elem, -1)
    return (cell.astype(jnp.int32), elem.astype(jnp.int32))


def draw_voxel_cell(key, part):
    return voxel_tables(key)[0]


def draw_voxel_elem(key, part):
    return jnp.transpose(voxel_tables(key)[1], (3, 1, 2, 0, 4))


def touch_ends(drawn, key, low, largest):
    dims = drawn.shape
    place = [jax.random.randint(jax.random.fold_in(key, axis), (), 0, dims[axis]) for axis in range(len(dims))]
    drawn = drawn.at[tuple(place)].set(low)
    longest = dims.index(max(dims))
    place[longest] = (place[longest] + 1) % dims[longest]
    return drawn.at[tuple(place)].set(largest)


def block_levels(own_key, extent, shards, low, top_value):
    def one(dim, blocks):
        draws = jax.random.uniform(jax.random.fold_in(jax.random.fold_in(own_key, 6), dim), (blocks,), jnp.float32, low / len(shards), top_value / len(shards))
        return jnp.repeat(jnp.exp(draws), extent[dim] // blocks).reshape((-1,) + (1,) * (len(extent) - dim - 1))

    loudness = one(*shards[0])
    for cut in shards[1:]:
        loudness = loudness * one(*cut)
    return loudness


def scatter_about(key, shape, scale, bound, cuts=(), held_as=jnp.bfloat16):
    values = scale * jax.random.normal(key, shape, jnp.float32)
    if cuts:
        values = values * block_levels(key, shape, cuts, -0.22, 0.18)
    return jnp.clip(values, -bound, bound).astype(held_as)


def setup_inputs(seed: int = 0, part: int = 0) -> dict:
    key_list = jax.random.split(jax.random.key(seed), 9)
    part_splits = jax.random.split(jax.random.fold_in(key_list[8], part), 9)
    return {
        "fields": scatter_about(part_splits[0], (6, NX, NY, NZ), 1.0, 6.0, ((1, 4), (2, 2), (3, 2)), jnp.float32),
        "adjoint": scatter_about(part_splits[1], (6, NX, NY, NZ), 1.0, 6.0, ((1, 4), (2, 2), (3, 2)), jnp.float32),
        "inv_eps": jnp.clip(jnp.exp(math.log(1.0) - 1.2039728 * jax.random.uniform(part_splits[2], (NX, NY, NZ), jnp.float32) ** block_levels(part_splits[2], (NX, NY, NZ), ((0, 4), (1, 2), (2, 2)), -0.2, 0.2)), 0.3, 1.0),
        "loss_level": touch_ends(jax.random.randint(part_splits[3], (NX, NY, NZ), 0, 4), jax.random.fold_in(part_splits[3], 1), 0, 3).astype(jnp.int32),
        "direction": jnp.clip(jax.random.uniform(key_list[4], (3, ND), jnp.float32, -1.0, 1.0), -1.0, 1.0),
        "pattern_weight": jnp.clip(jnp.exp(jax.random.uniform(key_list[5], (ND,), jnp.float32, math.log(2.0), math.log(20.0))), 2.0, 20.0),
        "voxel_cell": draw_voxel_cell(jax.random.fold_in(jax.random.fold_in(key_list[8], part), 71), part),
        "voxel_elem": draw_voxel_elem(jax.random.fold_in(jax.random.fold_in(key_list[8], part), 71), part),
    }


OMEGA = 0.9
KAPPA = 0.37
COMPS = (0, 1, 3, 4)

def coefficients(inv_eps, loss_level):
    level = 0.15 * loss_level.astype(jnp.float32)
    return ((1.0 - level) / (1.0 + level), 0.5 * inv_eps / (1.0 + level))

def ahead(a, dx, dy, dz):
    n = a.shape
    return a[dx:n[0] - 1 + dx, dy:n[1] - 1 + dy, dz:n[2] - 1 + dz]

def behind(a, dx, dy, dz):
    n = a.shape
    return a[1 - dx:n[0] - dx, 1 - dy:n[1] - dy, 1 - dz:n[2] - dz]

def curl_plus(e_pad):
    ex, ey, ez = (e_pad[0], e_pad[1], e_pad[2])
    cur_x = ahead(ez, 0, 1, 0) - ahead(ez, 0, 0, 0) - (ahead(ey, 0, 0, 1) - ahead(ey, 0, 0, 0))
    cur_y = ahead(ex, 0, 0, 1) - ahead(ex, 0, 0, 0) - (ahead(ez, 1, 0, 0) - ahead(ez, 0, 0, 0))
    cur_z = ahead(ey, 1, 0, 0) - ahead(ey, 0, 0, 0) - (ahead(ex, 0, 1, 0) - ahead(ex, 0, 0, 0))
    return jnp.stack([cur_x, cur_y, cur_z])

def curl_minus(h_pad):
    hx, hy, hz = (h_pad[0], h_pad[1], h_pad[2])
    cur_x = behind(hz, 0, 0, 0) - behind(hz, 0, 1, 0) - (behind(hy, 0, 0, 0) - behind(hy, 0, 0, 1))
    cur_y = behind(hx, 0, 0, 0) - behind(hx, 0, 0, 1) - (behind(hz, 0, 0, 0) - behind(hz, 1, 0, 0))
    cur_z = behind(hy, 0, 0, 0) - behind(hy, 1, 0, 0) - (behind(hx, 0, 0, 0) - behind(hx, 0, 1, 0))
    return jnp.stack([cur_x, cur_y, cur_z])

def yee_global(state, ca, cb):
    e_old = state[:3]
    e_pad = jnp.pad(e_old, ((0, 0), (0, 1), (0, 1), (0, 1)))
    new_h = state[3:] - 0.5 * curl_plus(e_pad)
    h_pad = jnp.pad(new_h, ((0, 0), (1, 0), (1, 0), (1, 0)))
    new_e = ca * e_old + cb * curl_minus(h_pad)
    return jnp.concatenate([new_e, new_h], axis=0)

def steering(xs, ys, zval, direction):
    phase = KAPPA * (xs[:, None, None] * direction[0] + ys[None, :, None] * direction[1] + zval * direction[2])
    phase = phase.reshape(-1, direction.shape[1])
    return jnp.concatenate([jnp.cos(phase), jnp.sin(phase)], axis=1)

def dft_rows(states, zindex):
    picks = jnp.array(COMPS, dtype=jnp.int32)
    real_part = 0.0
    imag_part = 0.0
    for step in range(1, len(states)):
        plane = states[step][picks, :, :, zindex].reshape(4, -1)
        real_part = real_part + plane * math.cos(OMEGA * step)
        imag_part = imag_part - plane * math.sin(OMEGA * step)
    return jnp.concatenate([real_part, imag_part], axis=0)

def far_field(dft, steer):
    prod = jnp.dot(dft, steer, precision=lax.Precision.HIGHEST)
    nd = steer.shape[1] // 2
    return jnp.concatenate([prod[:4, :nd] - prod[4:, nd:], prod[:4, nd:] + prod[4:, :nd]], axis=0)

def weight_rows(field, weight):
    return 2.0 * weight[:, None] * field.T

def expand_rows(rows):
    lower = jnp.concatenate([rows[:, 4:], -rows[:, :4]], axis=1)
    return jnp.concatenate([rows.T, lower.T], axis=1)

def back_project(mixing, steer):
    return lax.dot_general(mixing, steer, (((1,), (1,)), ((), ())), precision=lax.Precision.HIGHEST)

def reference(fields, adjoint, inv_eps, loss_level, direction, pattern_weight, voxel_cell, voxel_elem):
    ca, cb = coefficients(inv_eps, loss_level)
    states = [fields]
    for step in range(STEPS):
        states.append(yee_global(states[-1], ca, cb))
    zs = CZ // 2 + 2
    amp = 1.0 / math.sqrt(NX * NY * N_GZ)
    xs = jnp.arange(NX, dtype=jnp.int32).astype(jnp.float32)
    ys = jnp.arange(NY, dtype=jnp.int32).astype(jnp.float32)
    total = jnp.zeros((8, ND), jnp.float32)
    for plane in range(N_GZ):
        zindex = plane * CZ + zs
        zval = jnp.asarray(zindex, jnp.int32).astype(jnp.float32)
        total = total + far_field(dft_rows(states, zindex), steering(xs, ys, zval, direction))
    field = amp * total
    pattern = lax.optimization_barrier(jnp.sum(field * field, axis=0))
    mixing = expand_rows(weight_rows(field, pattern_weight))
    sources = []
    for plane in range(N_GZ):
        zval = jnp.asarray(plane * CZ + zs, jnp.int32).astype(jnp.float32)
        sources.append(amp * back_project(mixing, steering(xs, ys, zval, direction)))
    picks = jnp.array(COMPS, dtype=jnp.int32)
    adj = adjoint
    adj_states = []
    for tau in range(1, STEPS + 1):
        when = STEPS + 1 - tau
        for plane in range(N_GZ):
            src = sources[plane][:4] * math.cos(OMEGA * when) - sources[plane][4:] * math.sin(OMEGA * when)
            adj = adj.at[picks, :, :, plane * CZ + zs].add(src.reshape(4, NX, NY))
        adj = yee_global(adj, ca, cb)
        adj_states.append(adj)
    sens = jnp.zeros((NX, NY, NZ), jnp.float32)
    for tau in range(1, STEPS + 1):
        sens = sens + lax.optimization_barrier(jnp.sum(adj_states[tau - 1][:3] * states[STEPS + 1 - tau][:3], axis=0))
    blocks = sens.reshape(N_GX, CX, N_GY, CY, N_GZ, CZ).transpose(0, 2, 4, 1, 3, 5).reshape(N_GX, N_GY, N_GZ, CX * CY * CZ)
    values = jnp.take_along_axis(blocks, voxel_cell.reshape(N_GX, N_GY, N_GZ, N_GX * SLOTS).astype(jnp.int32), axis=3)
    sender_elem = jnp.transpose(voxel_elem, (3, 1, 2, 0, 4))
    owner = jnp.arange(N_GX, dtype=jnp.int32)[None, None, None, :, None]
    per_owner = NE // N_GX
    ids = jnp.where(sender_elem >= 0, owner * per_owner + sender_elem, NE).astype(jnp.int32)
    sums = jax.ops.segment_sum(values.reshape(-1), ids.reshape(-1), num_segments=NE + 1)[:NE]
    elem_grad = sums / math.sqrt(N_GX * N_GX * N_GY * N_GZ * SLOTS / NE)
    return (states[STEPS], pattern, elem_grad)
```

```python
import functools
import math

import jax
import jax.numpy as jnp
from jax import lax
from jax.experimental import pallas as pl
from jax.experimental.pallas import tpu as pltpu
from jax.sharding import PartitionSpec as P

STEPS = 2
NE = 1024
OMEGA = 0.9
KAPPA = 0.37
GATHER = ("gy", "gz", "gx")
HIGHEST = lax.Precision.HIGHEST

SPANS = {
    0: (-6, 2), 1: (-6, 2), 2: (-6, 1), 3: (-6, 1), 4: (-6, 1), 5: (-5, 1),
    6: (-6, 1), 7: (-6, 1), 8: (-6, 0), 9: (-6, 0), 10: (-6, 0), 11: (-5, 0),
    12: (-5, 1), 13: (-5, 1),
}
GROUPS = ((0, 1, 2), (3, 4, 6), (5, 8, 9, 10), (7, 12, 13, 11))
ROWS = 28


def extended(block, sides, width):
    for axis, dim in sides:
        count = lax.axis_size(axis)
        top = lax.slice_in_dim(block, block.shape[dim] - width, None, axis=dim)
        bottom = lax.slice_in_dim(block, 0, width, axis=dim)
        if count == 2:
            index = lax.axis_index(axis)
            other = lax.ppermute(jnp.where(index == 0, top, bottom), axis, [(0, 1), (1, 0)])
            low = jnp.where(index == 1, other, 0.0)
            high = jnp.where(index == 0, other, 0.0)
        else:
            forward = [(i, i + 1) for i in range(count - 1)]
            low = lax.ppermute(top, axis, forward)
            high = lax.ppermute(bottom, axis, [(t, s) for s, t in forward])
        block = jnp.concatenate([low, block, high], axis=dim)
    return block


def coefficients(inv_eps, level):
    level = 0.15 * level
    return ((1.0 - level) / (1.0 + level), 0.5 * inv_eps / (1.0 + level))


def ahead(a, dx, dy, dz):
    n = a.shape
    return a[dx : n[0] - 1 + dx, dy : n[1] - 1 + dy, dz : n[2] - 1 + dz]


def behind(a, dx, dy, dz):
    n = a.shape
    return a[1 - dx : n[0] - dx, 1 - dy : n[1] - dy, 1 - dz : n[2] - dz]


def curl_plus(e_pad):
    ex, ey, ez = (e_pad[0], e_pad[1], e_pad[2])
    cur_x = ahead(ez, 0, 1, 0) - ahead(ez, 0, 0, 0) - (ahead(ey, 0, 0, 1) - ahead(ey, 0, 0, 0))
    cur_y = ahead(ex, 0, 0, 1) - ahead(ex, 0, 0, 0) - (ahead(ez, 1, 0, 0) - ahead(ez, 0, 0, 0))
    cur_z = ahead(ey, 1, 0, 0) - ahead(ey, 0, 0, 0) - (ahead(ex, 0, 1, 0) - ahead(ex, 0, 0, 0))
    return jnp.stack([cur_x, cur_y, cur_z])


def curl_minus(h_pad):
    hx, hy, hz = (h_pad[0], h_pad[1], h_pad[2])
    cur_x = behind(hz, 0, 0, 0) - behind(hz, 0, 1, 0) - (behind(hy, 0, 0, 0) - behind(hy, 0, 0, 1))
    cur_y = behind(hx, 0, 0, 0) - behind(hx, 0, 0, 1) - (behind(hz, 0, 0, 0) - behind(hz, 1, 0, 0))
    cur_z = behind(hy, 0, 0, 0) - behind(hy, 1, 0, 0) - (behind(hx, 0, 0, 0) - behind(hx, 0, 1, 0))
    return jnp.stack([cur_x, cur_y, cur_z])


def window(fields, inv_eps, loss_level):
    shape = inv_eps.shape
    stack = jnp.concatenate([fields, inv_eps[None], loss_level.astype(jnp.float32)[None]])
    wide = extended(stack, (("gz", 3), ("gy", 2), ("gx", 1)), STEPS)
    ca, cb = coefficients(wide[6], wide[7])
    e, h = wide[:3], wide[3:6]
    keep = 1.0
    for dim, axis in enumerate(("gx", "gy", "gz")):
        first = jnp.arange(shape[dim] + 2 * STEPS) >= STEPS
        inside = (first | (lax.axis_index(axis) > 0)).astype(jnp.float32)
        keep = keep * inside.reshape([-1 if d == dim else 1 for d in range(3)])
    for _ in range(STEPS):
        h = (h[:, :-1, :-1, :-1] - 0.5 * curl_plus(e)) * keep[:-1, :-1, :-1]
        curl = curl_minus(h)
        e = ca[1:-1, 1:-1, 1:-1] * e[:, 1:-1, 1:-1, 1:-1] + cb[1:-1, 1:-1, 1:-1] * curl
        h = h[:, 1:, 1:, 1:]
        ca, cb, keep = (a[1:-1, 1:-1, 1:-1] for a in (ca, cb, keep))
    return jnp.concatenate([e, h])


def outgoing(fields, adjoint, inv_eps, loss_level, voxel_cell, voxel_elem):
    size_x, size_y, size_z = inv_eps.shape
    zs = size_z // 2 + 2
    arrays = [*fields, *adjoint, inv_eps, loss_level.astype(jnp.float32)]
    groups = []
    for members in GROUPS:
        planes = [
            jnp.swapaxes(arrays[m][:, :, zs + SPANS[m][0] : zs + SPANS[m][1] + 1], 1, 2) for m in members
        ]
        group = jnp.concatenate(planes, axis=1)
        groups.append(jnp.pad(group, ((0, 0), (0, ROWS - group.shape[1]), (0, 0))))
    cells = voxel_cell.astype(jnp.float32).reshape(-1)
    elems = voxel_elem.astype(jnp.float32).reshape(-1)
    tables = jnp.stack([cells, elems])
    if cells.shape[0] <= size_y:
        tables = jnp.pad(tables, ((0, 0), (0, size_y - cells.shape[0])))
        groups[0] = groups[0].at[:, ROWS - 1, :].set(tables)
        return jnp.concatenate(groups, axis=2)
    lanes = 4 * size_y
    rows = -(-cells.shape[0] // lanes)
    extra = -(-rows // 4) * 4
    tables = jnp.pad(tables, ((0, 0), (0, extra * lanes - cells.shape[0]))).reshape(2, extra, lanes)
    return jnp.concatenate([jnp.concatenate(groups, axis=2), tables], axis=1)


def steering(count_x, count_y, groups_z, size_z, direction):
    zs = size_z // 2 + 2
    xs = jnp.arange(count_x, dtype=jnp.float32)[:, None]
    ys = jnp.arange(count_y, dtype=jnp.float32)[None, :, None]
    zval = (jnp.arange(groups_z, dtype=jnp.float32) * size_z + zs)[:, None, None]
    phase_x = KAPPA * xs * direction[0]
    phase_yz = (KAPPA * (ys * direction[1] + zval * direction[2])).reshape(groups_z * count_y, -1)
    return (
        jnp.concatenate([jnp.cos(phase_x), jnp.sin(phase_x)], axis=1),
        jnp.concatenate([jnp.cos(phase_yz), jnp.sin(phase_yz)], axis=1),
    )


def main_kernel(dims, own_ref, got_ref, yz_ref, x_ref, weight_ref, pattern_ref, elem_ref):
    groups_x, groups_y, groups_z, size_x, size_y, size_z, slots, per_owner, half = dims
    count_x, count_y = groups_x * size_x, groups_y * size_y
    lanes = groups_z * count_y
    zs = size_z // 2 + 2
    per_row = 4 * size_y
    blocks = [(b, c) for c in range(groups_z) for b in range(groups_y)]

    def rows_of(row):
        out = []
        for b, c in blocks:
            start = (b * groups_z + c) * groups_x * size_x * half + row
            out.append(got_ref[pl.ds(start, count_x, stride=half), :])
        return out

    planes = {}
    for row in range(ROWS):
        loaded = rows_of(row)
        for q, members in enumerate(GROUPS):
            at = 0
            for m in members:
                size = SPANS[m][1] - SPANS[m][0] + 1
                if at <= row < at + size:
                    planes[m, SPANS[m][0] + row - at] = jnp.concatenate(
                        [p[:, q * size_y : (q + 1) * size_y] for p in loaded], axis=1
                    )
                at += size

    row_id = lax.broadcasted_iota(jnp.int32, (count_x, lanes), 0)
    lane_id = lax.broadcasted_iota(jnp.int32, (count_x, lanes), 1) % count_y
    x_up, x_low = row_id < count_x - 1, row_id > 0
    y_up, y_low = lane_id < count_y - 1, lane_id > 0

    def dxp(a):
        return jnp.where(x_up, pltpu.roll(a, count_x - 1, 0), 0.0) - a

    def dyp(a):
        return jnp.where(y_up, pltpu.roll(a, lanes - 1, 1), 0.0) - a

    def dxm(a):
        return a - jnp.where(x_low, pltpu.roll(a, 1, 0), 0.0)

    def dym(a):
        return a - jnp.where(y_low, pltpu.roll(a, 1, 1), 0.0)

    ca, cb = {}, {}
    for k in range(SPANS[12][0], SPANS[12][1] + 1):
        ca[k], cb[k] = coefficients(planes[12, k], planes[13, k])

    def step(ex, ey, ez, hx, hy, hz, low, high):
        nhx = {k: hx[k] - 0.5 * (dyp(ez[k]) - (ey[k + 1] - ey[k])) for k in range(low - 1, high + 1)}
        nhy = {k: hy[k] - 0.5 * ((ex[k + 1] - ex[k]) - dxp(ez[k])) for k in range(low - 1, high + 1)}
        nhz = {k: hz[k] - 0.5 * (dxp(ey[k]) - dyp(ex[k])) for k in range(low, high + 1)}
        nex = {k: ca[k] * ex[k] + cb[k] * (dym(nhz[k]) - (nhy[k] - nhy[k - 1])) for k in range(low, high + 1)}
        ney = {k: ca[k] * ey[k] + cb[k] * ((nhx[k] - nhx[k - 1]) - dxm(nhz[k])) for k in range(low, high + 1)}
        nez = {k: ca[k] * ez[k] + cb[k] * (dxm(nhy[k]) - dym(nhx[k])) for k in range(low, high + 1)}
        return nex, ney, nez, nhx, nhy, nhz

    def arrays(first):
        return [
            {k: planes[m, k] for k in range(SPANS[m][0], SPANS[m][1] + 1)} for m in range(first, first + 6)
        ]

    u1 = step(*arrays(0), -5, 1)
    u2 = step(*u1, -4, 0)
    rows = []
    for m in (0, 1, 3, 4):
        rows.append(u1[m][0] * math.cos(OMEGA) + u2[m][0] * math.cos(2 * OMEGA))
        rows.append(-u1[m][0] * math.sin(OMEGA) - u2[m][0] * math.sin(2 * OMEGA))
    dft = jnp.concatenate(rows, axis=0)

    yz = yz_ref[...]
    nd = yz.shape[1] // 2
    cos_x, sin_x = x_ref[:, :nd], x_ref[:, nd:]
    amp = 1.0 / math.sqrt(count_x * count_y * groups_z)
    prod = jnp.dot(dft, yz, precision=HIGHEST, preferred_element_type=jnp.float32)
    pattern = jnp.zeros((1, nd), jnp.float32)
    weight = (2.0 * amp) * weight_ref[...]
    mixing = []
    for c in range(4):
        re = prod[2 * c * count_x : (2 * c + 1) * count_x]
        im = prod[(2 * c + 1) * count_x : (2 * c + 2) * count_x]
        real = re[:, :nd] - im[:, nd:]
        imag = re[:, nd:] + im[:, :nd]
        far_re = amp * jnp.sum(real * cos_x - imag * sin_x, axis=0, keepdims=True)
        far_im = amp * jnp.sum(real * sin_x + imag * cos_x, axis=0, keepdims=True)
        pattern = pattern + far_re * far_re + far_im * far_im
        out_re, out_im = weight * far_re, weight * far_im
        b_re = out_re * cos_x + out_im * sin_x
        b_im = out_im * cos_x - out_re * sin_x
        mixing.append(jnp.concatenate([b_re, b_im], axis=1))
        mixing.append(jnp.concatenate([b_im, -b_re], axis=1))
    pattern_ref[...] = pattern

    src = lax.dot_general(
        jnp.concatenate(mixing, axis=0), yz, (((1,), (1,)), ((), ())),
        precision=HIGHEST, preferred_element_type=jnp.float32,
    )

    def with_sources(state, when):
        state = [dict(a) for a in state]
        for c, m in enumerate((0, 1, 3, 4)):
            gre = src[2 * c * count_x : (2 * c + 1) * count_x]
            gim = src[(2 * c + 1) * count_x : (2 * c + 2) * count_x]
            state[m][0] = state[m][0] + (gre * math.cos(OMEGA * when) - gim * math.sin(OMEGA * when))
        return state

    v1 = step(*with_sources(arrays(6), 2), -5, 0)
    v2 = step(*with_sources(v1, 1), -4, -1)
    sens = [
        sum(v1[m][k] * u2[m][k] for m in range(3)) + sum(v2[m][k] * u1[m][k] for m in range(3))
        for k in range(-4, 0)
    ]
    sens = jnp.concatenate(sens, axis=0)

    own = own_ref[0]
    senders = groups_x * groups_y * groups_z
    total = senders * slots
    lists = groups_x * slots
    if lists <= size_y:
        cell_tab = got_ref[pl.ds(ROWS - 1, senders, stride=size_x * half), :]
        elem_tab = got_ref[pl.ds(half + ROWS - 1, senders, stride=size_x * half), :]
    else:
        pieces = range(-(-lists // per_row))
        cell_tab = jnp.concatenate(
            [got_ref[pl.ds(ROWS + r, senders, stride=size_x * half), :] for r in pieces], axis=1
        )
        elem_tab = jnp.concatenate(
            [got_ref[pl.ds(half + ROWS + r, senders, stride=size_x * half), :] for r in pieces], axis=1
        )
    width = cell_tab.shape[1]
    at = lax.broadcasted_iota(jnp.int32, (width, total), 0)
    slot = lax.broadcasted_iota(jnp.int32, (width, total), 1)
    spread_cell = (at == own * slots + slot % slots).astype(jnp.float32)
    spread_elem = (at == slot % lists).astype(jnp.float32)
    sender = lax.broadcasted_iota(jnp.int32, (senders, total), 0)
    slot = lax.broadcasted_iota(jnp.int32, (senders, total), 1)
    cells = jnp.dot(cell_tab, spread_cell, precision=HIGHEST, preferred_element_type=jnp.float32)
    cells = jnp.sum(jnp.where(sender == slot // slots, cells, 0.0), axis=0, keepdims=True)
    elems = jnp.dot(elem_tab, spread_elem, precision=HIGHEST, preferred_element_type=jnp.float32)
    elems = jnp.sum(
        jnp.where(sender == (slot // lists) * groups_x + own, elems, 0.0), axis=0, keepdims=True
    )
    cells = (cells + 0.5).astype(jnp.int32)
    elems = (elems + 1.5).astype(jnp.int32) - 1
    slot = lax.broadcasted_iota(jnp.int32, (1, total), 1)
    block = slot // lists
    place_x = (slot // slots % groups_x) * size_x + cells // (size_y * size_z)
    place_y = cells // size_z % size_y
    place_z = cells % size_z - (zs - 4)
    row_want = place_z * count_x + place_x
    lane_want = (block % groups_z) * count_y + (block // groups_z) * size_y + place_y
    hot_row = (lax.broadcasted_iota(jnp.int32, (4 * count_x, total), 0) == row_want).astype(jnp.float32)
    hot_lane = lax.broadcasted_iota(jnp.int32, (lanes, total), 0) == lane_want
    picked = lax.dot_general(
        sens, hot_row, (((0,), (0,)), ((), ())), precision=HIGHEST, preferred_element_type=jnp.float32
    )
    values = jnp.sum(jnp.where(hot_lane, picked, 0.0), axis=0, keepdims=True)
    hot_elem = (lax.broadcasted_iota(jnp.int32, (per_owner, total), 0) == elems).astype(jnp.float32)
    sums = lax.dot_general(
        jnp.broadcast_to(values, (8, total)), hot_elem, (((1,), (1,)), ((), ())),
        precision=HIGHEST, preferred_element_type=jnp.float32,
    )
    scale = 1.0 / math.sqrt(groups_x * groups_x * groups_y * groups_z * slots / NE)
    elem_ref[...] = sums[:1] * scale


def local(fields, adjoint, inv_eps, loss_level, direction, pattern_weight, voxel_cell, voxel_elem):
    size_x, size_y, size_z = inv_eps.shape
    groups_x, groups_y, groups_z = (lax.axis_size(a) for a in ("gx", "gy", "gz"))
    slots = voxel_cell.shape[4]
    per_owner = NE // groups_x
    nd = direction.shape[1]
    own = lax.axis_index("gx").astype(jnp.int32).reshape(1)

    send = outgoing(fields, adjoint, inv_eps, loss_level, voxel_cell, voxel_elem)
    half = send.shape[1]
    send = send.reshape(size_x * half, 4 * size_y)
    senders = groups_x * groups_y * groups_z
    got = lax.all_to_all(
        jnp.broadcast_to(send[None], (senders,) + send.shape), GATHER, split_axis=0, concat_axis=0, tiled=True
    )
    got = got.reshape(senders * size_x * half, 4 * size_y)
    table_x, table_yz = steering(groups_x * size_x, groups_y * size_y, groups_z, size_z, direction)
    fields_out = window(fields, inv_eps, loss_level)

    dims = (groups_x, groups_y, groups_z, size_x, size_y, size_z, slots, per_owner, half)
    vmem = pl.BlockSpec(memory_space=pltpu.VMEM)
    pattern, elem = pl.pallas_call(
        functools.partial(main_kernel, dims),
        out_shape=(
            jax.ShapeDtypeStruct((1, nd), jnp.float32),
            jax.ShapeDtypeStruct((1, per_owner), jnp.float32),
        ),
        in_specs=[pl.BlockSpec(memory_space=pltpu.SMEM), vmem, vmem, vmem, vmem],
        out_specs=(vmem, vmem),
        compiler_params=pltpu.CompilerParams(vmem_limit_bytes=48 * 1024 * 1024),
        name="main",
    )(own, got, table_yz, table_x, pattern_weight.reshape(1, nd))
    return (fields_out, pattern.reshape(nd), elem.reshape(per_owner))


def solution(mesh):
    in_specs = (
        P(None, ("groups", "gx"), "gy", "gz"),
        P(None, ("groups", "gx"), "gy", "gz"),
        P(("groups", "gx"), "gy", "gz"),
        P(("groups", "gx"), "gy", "gz"),
        P(),
        P(),
        P(("groups", "gx"), "gy", "gz", None, None),
        P(("groups", "gx"), "gy", "gz", None, None),
    )
    out_specs = (P(None, ("groups", "gx"), "gy", "gz"), P("groups"), P(("groups", "gx")))
    return jax.shard_map(local, mesh=mesh, in_specs=in_specs, out_specs=out_specs, check_vma=False)
```

```python
import functools
import math

import jax
import jax.numpy as jnp
from jax import lax
from jax.experimental import pallas as pl
from jax.experimental.pallas import tpu as pltpu
from jax.sharding import PartitionSpec as P

STEPS = 2
NE = 1024
OMEGA = 0.9
KAPPA = 0.37
HIGHEST = lax.Precision.HIGHEST
HALO = 2
COMPS = (0, 1, 3, 4)

SETS = (
    ((0, 1, 2, 3), -6, 2),
    ((4, 6, 7, 12), -6, 1),
    ((5, 13, 8, 9), -6, 1),
    ((10, 11), -6, 0),
)
STARTS = (0, 9, 17, 25)
HALF = 32
FORWARD = (0, 1, 2, 3, 4, 5, 12, 13)


def coefficients(inv_eps, level):
    level = 0.15 * level
    return ((1.0 - level) / (1.0 + level), 0.5 * inv_eps / (1.0 + level))


def place_of(m):
    for t, (members, _, _) in enumerate(SETS):
        if m in members:
            return t, members.index(m)


def neighbours(axis, top, bottom):
    count = lax.axis_size(axis)
    if count == 2:
        other = lax.ppermute(top, axis, [(0, 1), (1, 0)])
        return other, other
    forward = [(i, i + 1) for i in range(count - 1)]
    return lax.ppermute(top, axis, forward), lax.ppermute(bottom, axis, [(t, s) for s, t in forward])


def first_kernel(dims, at_ref, f_ref, a_ref, ie_ref, ll_ref, tab_ref, send_ref, zt_ref, zb_ref, yt_ref, yb_ref):
    groups_x, groups_y, groups_z, size_x, size_y, size_z = dims
    zs = size_z // 2 + 2

    def array(m, x):
        if m < 6:
            return f_ref[m, x]
        if m < 12:
            return a_ref[m - 6, x]
        if m == 12:
            return ie_ref[x]
        return ll_ref[x].astype(jnp.float32)

    tops, bottoms = [], []
    for x in range(size_x):
        parts = []
        for t, (members, low, high) in enumerate(SETS):
            blocks = [array(m, x) for m in members]
            blocks += [jnp.zeros((size_y, size_z), jnp.float32)] * (4 - len(members))
            flipped = jnp.concatenate(blocks, axis=0).T
            parts.append(flipped[zs + low : zs + high + 1])
            if t < 3:
                tops.append(flipped[size_z - HALO :])
                bottoms.append(flipped[:HALO])
        parts[3] = parts[3] + tab_ref[x]
        rows = jnp.concatenate(parts, axis=0)
        for d in range(groups_x * groups_y):
            send_ref[d, x * HALF : (x + 1) * HALF] = rows
    pad = [jnp.zeros((zt_ref.shape[0] - HALO * len(tops), 4 * size_y), jnp.float32)]
    top, bottom = jnp.concatenate(tops + pad, axis=0), jnp.concatenate(bottoms + pad, axis=0)
    zt_ref[...] = jnp.where(at_ref[2] == 0, top, bottom) if groups_z == 2 else top
    zb_ref[...] = bottom
    top = jnp.concatenate([array(m, x)[size_y - HALO :] for m in FORWARD for x in range(size_x)], axis=0)
    bottom = jnp.concatenate([array(m, x)[:HALO] for m in FORWARD for x in range(size_x)], axis=0)
    yt_ref[...] = jnp.where(at_ref[1] == 0, top, bottom) if groups_y == 2 else top
    yb_ref[...] = bottom


def wide_masks(dims, at_ref):
    _, _, _, _, size_y, size_z = dims
    shape = (size_y + 8, size_z + 128)
    row = lax.broadcasted_iota(jnp.int32, shape, 0)
    lane = lax.broadcasted_iota(jnp.int32, shape, 1)
    out_y = jnp.logical_and(row >= size_y + 4, at_ref[1] == 0)
    out_z = jnp.logical_and(lane >= size_z + 64, at_ref[2] == 0)
    return jnp.where(jnp.logical_or(out_y, out_z), 0.0, 0.5)


def forward_y(a):
    return pltpu.roll(a, a.shape[0] - 1, 0) - a


def forward_z(a):
    return pltpu.roll(a, a.shape[1] - 1, 1) - a


def backward_y(a):
    return a - pltpu.roll(a, 1, 0)


def backward_z(a):
    return a - pltpu.roll(a, 1, 1)


def pack(planes, size_z):
    lane = lax.broadcasted_iota(jnp.int32, (planes[0].shape[0], 128), 1)
    border = jnp.zeros((planes[0].shape[0], 128), jnp.float32)
    for p, plane in enumerate(planes):
        moved = pltpu.roll(plane[:, size_z:], 8 * p + 2, 1)
        border = jnp.where(jnp.logical_and(lane >= 8 * p, lane < 8 * p + 4), moved, border)
    return [plane[:, :size_z] for plane in planes] + [border]


def unpack(ref, count, size_y):
    rows = size_y + 8
    border = ref[count * rows : (count + 1) * rows]
    lane = lax.broadcasted_iota(jnp.int32, border.shape, 1)
    keep = jnp.logical_or(lane < 2, lane >= 126)
    out = []
    for p in range(count):
        moved = pltpu.roll(border, 128 - (8 * p + 2), 1)
        out.append(jnp.concatenate([ref[p * rows : (p + 1) * rows], jnp.where(keep, moved, 0.0)], axis=1))
    return out


def second_kernel(dims, at_ref, f_ref, ie_ref, ll_ref, zl_ref, zh_ref, yl_ref, yh_ref, state_ref, up_ref, down_ref):
    groups_x, groups_y, groups_z, size_x, size_y, size_z = dims
    edge = 2 * size_x * len(FORWARD)
    zrows = zl_ref.shape[0]
    lane = lax.broadcasted_iota(jnp.int32, (8, 128), 1)
    high_lane = jnp.logical_and(lane < HALO, at_ref[2] < groups_z - 1)
    low_lane = jnp.logical_and(lane >= 128 - HALO, at_ref[2] > 0)
    y_high = (at_ref[1] < groups_y - 1).astype(jnp.float32)
    y_low = (at_ref[1] > 0).astype(jnp.float32)

    def flip(a):
        return jnp.concatenate([a, jnp.zeros((128 - zrows, a.shape[1]), jnp.float32)], axis=0).T

    own_low, own_high = flip(zl_ref[...]), flip(zh_ref[...])
    yl_low, yl_high = flip(yl_ref[edge : edge + zrows]), flip(yl_ref[edge + zrows :])
    yh_low, yh_high = flip(yh_ref[edge : edge + zrows]), flip(yh_ref[edge + zrows :])

    def column(low, high, rows, at):
        reps = rows // 8
        hl = jnp.concatenate([high_lane] * reps, axis=0)
        ll = jnp.concatenate([low_lane] * reps, axis=0)
        moved_high = pltpu.roll(high, (128 - at) % 128, 1)
        moved_low = pltpu.roll(low, (128 - HALO - at) % 128, 1)
        return jnp.where(hl, moved_high, jnp.where(ll, moved_low, 0.0))

    def wide(m, x):
        t, q = place_of(m)
        at = (x * 3 + t) * HALO
        if m < 6:
            body = f_ref[m, x]
        else:
            body = ie_ref[x] if m == 12 else ll_ref[x].astype(jnp.float32)
        rows = slice(q * size_y, (q + 1) * size_y)
        body_z = column(own_low[rows], own_high[rows], size_y, at)
        start = (FORWARD.index(m) * size_x + x) * HALO
        blank = jnp.zeros((8 - 2 * HALO, 128), jnp.float32)
        first, last = q * size_y, (q + 1) * size_y
        tile = jnp.concatenate(
            [yh_ref[start : start + HALO] * y_high, blank, yl_ref[start : start + HALO] * y_low], axis=0
        )
        low = jnp.concatenate(
            [yh_low[first : first + HALO] * y_high, blank, yl_low[last - HALO : last] * y_low], axis=0
        )
        high = jnp.concatenate(
            [yh_high[first : first + HALO] * y_high, blank, yl_high[last - HALO : last] * y_low], axis=0
        )
        corner = column(low, high, 8, at)
        return jnp.concatenate(
            [jnp.concatenate([body, body_z], axis=1), jnp.concatenate([tile, corner], axis=1)], axis=0
        )

    half = wide_masks(dims, at_ref)
    xs = range(size_x)
    ex, ey, ez, hx, hy, hz, ie, lv = ([wide(m, x) for x in xs] for m in FORWARD)
    pairs = [coefficients(ie[x], lv[x]) for x in xs]
    ca, cb = [p[0] for p in pairs], [p[1] for p in pairs]
    nothing = jnp.zeros_like(half)
    hx = [hx[x] - half * (forward_y(ez[x]) - forward_z(ey[x])) for x in xs]
    hy = [hy[x] - half * (forward_z(ex[x]) - ((ez[x + 1] if x + 1 < size_x else nothing) - ez[x])) for x in xs]
    hz = [hz[x] - half * (((ey[x + 1] if x + 1 < size_x else nothing) - ey[x]) - forward_y(ex[x])) for x in xs]
    first_ey, first_ez = ey[0], ez[0]
    ex = [ca[x] * ex[x] + cb[x] * (backward_y(hz[x]) - backward_z(hy[x])) for x in xs]
    ey = [ca[x] * ey[x] + cb[x] * (backward_z(hx[x]) - (hz[x] - (hz[x - 1] if x else nothing))) for x in xs]
    ez = [ca[x] * ez[x] + cb[x] * ((hy[x] - (hy[x - 1] if x else nothing)) - backward_y(hx[x])) for x in xs]
    state = [*ex, *ey, *ez, *hx, *hy, *hz, *ca, *cb, first_ey, first_ez]
    for i, a in enumerate(state):
        state_ref[i] = a
    rows = size_y + 8
    up = pack([hy[-1], hz[-1], ex[-1], ey[-1], ez[-1], cb[-1]], size_z)
    for i, a in enumerate(up):
        up_ref[i * rows : (i + 1) * rows] = a
    down = pack([first_ey, first_ez, ey[0], ez[0], cb[0]], size_z)
    for i, a in enumerate(down):
        down_ref[i * rows : (i + 1) * rows] = a


def third_kernel(dims, at_ref, state_ref, low_ref, high_ref, out_ref):
    groups_x, groups_y, groups_z, size_x, size_y, size_z = dims
    xs = range(size_x)
    half = wide_masks(dims, at_ref)
    half_low = half * (at_ref[0] > 0).astype(jnp.float32)
    state = [[state_ref[i * size_x + x] for x in xs] for i in range(8)]
    ex, ey, ez, hx, hy, hz, ca, cb = state
    first_ey, first_ez = state_ref[8 * size_x], state_ref[8 * size_x + 1]
    low_hy, low_hz, low_ex, low_ey, low_ez, low_cb = unpack(low_ref, 6, size_y)
    next_ey, next_ez, high_ey, high_ez, high_cb = unpack(high_ref, 5, size_y)
    add_y, add_z = half * next_ez, -(half * next_ey)
    hy[-1], hz[-1] = hy[-1] + add_y, hz[-1] + add_z
    ex[-1] = ex[-1] + cb[-1] * (backward_y(add_z) - backward_z(add_y))
    ey[-1] = ey[-1] - cb[-1] * add_z
    ez[-1] = ez[-1] + cb[-1] * add_y
    add_y, add_z = half_low * first_ez, -(half_low * first_ey)
    low_hy, low_hz = low_hy + add_y, low_hz + add_z
    low_ex = low_ex + low_cb * (backward_y(add_z) - backward_z(add_y))
    low_ey = low_ey - low_cb * add_z
    low_ez = low_ez + low_cb * add_y
    ey[0] = ey[0] + cb[0] * low_hz
    ez[0] = ez[0] - cb[0] * low_hy
    high_ey = high_ey + high_cb * hz[-1]
    high_ez = high_ez - high_cb * hy[-1]
    low_hy = low_hy - half_low * (forward_z(low_ex) - (ez[0] - low_ez))
    low_hz = low_hz - half_low * ((ey[0] - low_ey) - forward_y(low_ex))
    after_ey, after_ez = ey[1:] + [high_ey], ez[1:] + [high_ez]
    hx = [hx[x] - half * (forward_y(ez[x]) - forward_z(ey[x])) for x in xs]
    hy = [hy[x] - half * (forward_z(ex[x]) - (after_ez[x] - ez[x])) for x in xs]
    hz = [hz[x] - half * ((after_ey[x] - ey[x]) - forward_y(ex[x])) for x in xs]
    before_hy, before_hz = [low_hy] + hy[:-1], [low_hz] + hz[:-1]
    for x in xs:
        new = (
            ca[x] * ex[x] + cb[x] * (backward_y(hz[x]) - backward_z(hy[x])),
            ca[x] * ey[x] + cb[x] * (backward_z(hx[x]) - (hz[x] - before_hz[x])),
            ca[x] * ez[x] + cb[x] * ((hy[x] - before_hy[x]) - backward_y(hx[x])),
            hx[x], hy[x], hz[x],
        )
        for m in range(6):
            out_ref[m, x] = new[m][:size_y, :size_z]


def steering(count_x, count_y, groups_z, size_z, direction):
    zs = size_z // 2 + 2
    xs = jnp.arange(count_x, dtype=jnp.float32)[:, None]
    ys = jnp.arange(count_y, dtype=jnp.float32)[None, :, None]
    zval = (jnp.arange(groups_z, dtype=jnp.float32) * size_z + zs)[:, None, None]
    phase_x = KAPPA * xs * direction[0]
    phase_yz = (KAPPA * (ys * direction[1] + zval * direction[2])).reshape(groups_z * count_y, -1)
    return (
        jnp.concatenate([jnp.cos(phase_x), jnp.sin(phase_x)], axis=1),
        jnp.concatenate([jnp.cos(phase_yz), jnp.sin(phase_yz)], axis=1),
    )


def main_kernel(dims, slots, at_ref, *refs):
    groups_x, groups_y, groups_z, size_x, size_y, size_z = dims
    got_refs = refs[:groups_z]
    yz_ref, x_ref, weight_ref, pattern_ref, elem_ref = refs[groups_z:]
    per_owner = NE // groups_x
    count_x, count_y = groups_x * size_x, groups_y * size_y
    lanes = groups_z * count_y
    zs = size_z // 2 + 2

    def pick(c, start, size, stride):
        out = None
        for s, ref in enumerate(got_refs):
            part = ref[pl.ds(start, size, stride=stride), :]
            here = lax.rem(at_ref[2] - s + groups_z, groups_z) == c
            out = part if out is None else jnp.where(here, part, out)
        return out

    loaded = {}

    def plane(m, k):
        t, q = place_of(m)
        row = STARTS[t] + k - SETS[t][1]
        if row not in loaded:
            loaded[row] = [
                pick(c, b * groups_x * size_x * HALF + row, count_x, HALF)
                for c in range(groups_z)
                for b in range(groups_y)
            ]
        return jnp.concatenate([p[:, q * size_y : (q + 1) * size_y] for p in loaded[row]], axis=1)

    row_id = lax.broadcasted_iota(jnp.int32, (count_x, lanes), 0)
    lane_id = lax.broadcasted_iota(jnp.int32, (count_x, lanes), 1) % count_y
    x_up, x_low = row_id < count_x - 1, row_id > 0
    y_up, y_low = lane_id < count_y - 1, lane_id > 0

    def dxp(a):
        return jnp.where(x_up, pltpu.roll(a, count_x - 1, 0), 0.0) - a

    def dyp(a):
        return jnp.where(y_up, pltpu.roll(a, lanes - 1, 1), 0.0) - a

    def dxm(a):
        return a - jnp.where(x_low, pltpu.roll(a, 1, 0), 0.0)

    def dym(a):
        return a - jnp.where(y_low, pltpu.roll(a, 1, 1), 0.0)

    ca, cb = {}, {}
    for k in range(-5, 2):
        ca[k], cb[k] = coefficients(plane(12, k), plane(13, k))

    def step(ex, ey, ez, hx, hy, hz, low, high):
        nhx = {k: hx[k] - 0.5 * (dyp(ez[k]) - (ey[k + 1] - ey[k])) for k in range(low - 1, high + 1)}
        nhy = {k: hy[k] - 0.5 * ((ex[k + 1] - ex[k]) - dxp(ez[k])) for k in range(low - 1, high + 1)}
        nhz = {k: hz[k] - 0.5 * (dxp(ey[k]) - dyp(ex[k])) for k in range(low, high + 1)}
        nex = {k: ca[k] * ex[k] + cb[k] * (dym(nhz[k]) - (nhy[k] - nhy[k - 1])) for k in range(low, high + 1)}
        ney = {k: ca[k] * ey[k] + cb[k] * ((nhx[k] - nhx[k - 1]) - dxm(nhz[k])) for k in range(low, high + 1)}
        nez = {k: ca[k] * ez[k] + cb[k] * (dxm(nhy[k]) - dym(nhx[k])) for k in range(low, high + 1)}
        return nex, ney, nez, nhx, nhy, nhz

    def arrays(first):
        spans = [SETS[place_of(m)[0]] for m in range(first, first + 6)]
        return [{k: plane(first + i, k) for k in range(s[1], s[2] + 1)} for i, s in enumerate(spans)]

    u1 = step(*arrays(0), -5, 1)
    u2 = step(*u1, -4, 0)
    rows = []
    for m in (0, 1, 3, 4):
        rows.append(u1[m][0] * math.cos(OMEGA) + u2[m][0] * math.cos(2 * OMEGA))
        rows.append(-u1[m][0] * math.sin(OMEGA) - u2[m][0] * math.sin(2 * OMEGA))
    dft = jnp.concatenate(rows, axis=0)

    yz = yz_ref[...]
    nd = yz.shape[1] // 2
    cos_x, sin_x = x_ref[:, :nd], x_ref[:, nd:]
    amp = 1.0 / math.sqrt(count_x * count_y * groups_z)
    prod = jnp.dot(dft, yz, precision=HIGHEST, preferred_element_type=jnp.float32)
    pattern = jnp.zeros((1, nd), jnp.float32)
    weight = (2.0 * amp) * weight_ref[...]
    mixing = []
    for c in range(4):
        re = prod[2 * c * count_x : (2 * c + 1) * count_x]
        im = prod[(2 * c + 1) * count_x : (2 * c + 2) * count_x]
        real = re[:, :nd] - im[:, nd:]
        imag = re[:, nd:] + im[:, :nd]
        far_re = amp * jnp.sum(real * cos_x - imag * sin_x, axis=0, keepdims=True)
        far_im = amp * jnp.sum(real * sin_x + imag * cos_x, axis=0, keepdims=True)
        pattern = pattern + far_re * far_re + far_im * far_im
        out_re, out_im = weight * far_re, weight * far_im
        b_re = out_re * cos_x + out_im * sin_x
        b_im = out_im * cos_x - out_re * sin_x
        mixing.append(jnp.concatenate([b_re, b_im], axis=1))
        mixing.append(jnp.concatenate([b_im, -b_re], axis=1))
    pattern_ref[...] = pattern

    src = lax.dot_general(
        jnp.concatenate(mixing, axis=0), yz, (((1,), (1,)), ((), ())),
        precision=HIGHEST, preferred_element_type=jnp.float32,
    )

    def with_sources(state, when):
        state = [dict(a) for a in state]
        for c, m in enumerate((0, 1, 3, 4)):
            gre = src[2 * c * count_x : (2 * c + 1) * count_x]
            gim = src[(2 * c + 1) * count_x : (2 * c + 2) * count_x]
            state[m][0] = state[m][0] + (gre * math.cos(OMEGA * when) - gim * math.sin(OMEGA * when))
        return state

    v1 = step(*with_sources(arrays(6), 2), -5, 0)
    v2 = step(*with_sources(v1, 1), -4, -1)
    sens = [
        sum(v1[m][k] * u2[m][k] for m in range(3)) + sum(v2[m][k] * u1[m][k] for m in range(3))
        for k in range(-4, 0)
    ]
    sens = jnp.concatenate(sens, axis=0)

    own = at_ref[0]
    senders = groups_x * groups_y * groups_z
    total = senders * slots
    lists = groups_x * slots
    pieces = range(-(-lists // (2 * size_y)))

    def table(x):
        return jnp.concatenate(
            [
                jnp.concatenate(
                    [
                        pick(c, x * HALF + STARTS[3] + r, groups_x * groups_y, size_x * HALF)[:, 2 * size_y :]
                        for c in range(groups_z)
                    ],
                    axis=0,
                )
                for r in pieces
            ],
            axis=1,
        )

    cell_tab, elem_tab = table(0), table(1)
    width = cell_tab.shape[1]
    at = lax.broadcasted_iota(jnp.int32, (width, total), 0)
    slot = lax.broadcasted_iota(jnp.int32, (width, total), 1)
    spread_cell = (at == own * slots + slot % slots).astype(jnp.float32)
    spread_elem = (at == slot % lists).astype(jnp.float32)
    sender = lax.broadcasted_iota(jnp.int32, (senders, total), 0)
    slot = lax.broadcasted_iota(jnp.int32, (senders, total), 1)
    cells = jnp.dot(cell_tab, spread_cell, precision=HIGHEST, preferred_element_type=jnp.float32)
    cells = jnp.sum(jnp.where(sender == slot // slots, cells, 0.0), axis=0, keepdims=True)
    elems = jnp.dot(elem_tab, spread_elem, precision=HIGHEST, preferred_element_type=jnp.float32)
    elems = jnp.sum(
        jnp.where(sender == (slot // lists) * groups_x + own, elems, 0.0), axis=0, keepdims=True
    )
    cells = (cells + 0.5).astype(jnp.int32)
    elems = (elems + 1.5).astype(jnp.int32) - 1
    slot = lax.broadcasted_iota(jnp.int32, (1, total), 1)
    block = slot // lists
    place_x = (slot // slots % groups_x) * size_x + cells // (size_y * size_z)
    place_y = cells // size_z % size_y
    place_z = cells % size_z - (zs - 4)
    row_want = place_z * count_x + place_x
    lane_want = (block // groups_y) * count_y + (block % groups_y) * size_y + place_y
    hot_row = (lax.broadcasted_iota(jnp.int32, (4 * count_x, total), 0) == row_want).astype(jnp.float32)
    hot_lane = lax.broadcasted_iota(jnp.int32, (lanes, total), 0) == lane_want
    picked = lax.dot_general(
        sens, hot_row, (((0,), (0,)), ((), ())), precision=HIGHEST, preferred_element_type=jnp.float32
    )
    values = jnp.sum(jnp.where(hot_lane, picked, 0.0), axis=0, keepdims=True)
    hot_elem = (lax.broadcasted_iota(jnp.int32, (per_owner, total), 0) == elems).astype(jnp.float32)
    sums = lax.dot_general(
        jnp.broadcast_to(values, (8, total)), hot_elem, (((1,), (1,)), ((), ())),
        precision=HIGHEST, preferred_element_type=jnp.float32,
    )
    scale = 1.0 / math.sqrt(groups_x * groups_x * groups_y * groups_z * slots / NE)
    elem_ref[...] = sums[:1] * scale


def local(fields, adjoint, inv_eps, loss_level, direction, pattern_weight, voxel_cell, voxel_elem):
    size_x, size_y, size_z = inv_eps.shape
    groups_x, groups_y, groups_z = (lax.axis_size(a) for a in ("gx", "gy", "gz"))
    dims = (groups_x, groups_y, groups_z, size_x, size_y, size_z)
    slots = voxel_cell.shape[4]
    per_owner = NE // groups_x
    nd = direction.shape[1]
    at = jnp.stack([lax.axis_index(a) for a in ("gx", "gy", "gz")]).astype(jnp.int32)
    smem = pl.BlockSpec(memory_space=pltpu.SMEM)
    vmem = pl.BlockSpec(memory_space=pltpu.VMEM)

    def call(kernel, name, outs, *args):
        return pl.pallas_call(
            kernel,
            out_shape=tuple(jax.ShapeDtypeStruct(o, jnp.float32) for o in outs),
            in_specs=[smem] + [vmem] * len(args),
            out_specs=(vmem,) * len(outs),
            compiler_params=pltpu.CompilerParams(vmem_limit_bytes=48 * 1024 * 1024),
            name=name,
        )(at, *args)

    lists = groups_x * slots
    wide = 2 * size_y
    pieces = -(-lists // wide)
    deep = SETS[3][2] - SETS[3][1] + 1
    tables = jnp.stack([voxel_cell.reshape(-1), voxel_elem.reshape(-1)]).astype(jnp.float32)
    tables = jnp.pad(tables, ((0, 0), (0, pieces * wide - lists))).reshape(2, pieces, wide)
    tables = jnp.pad(tables, ((0, 0), (0, deep - pieces), (wide, 0)))
    zrows = -(-(3 * HALO * size_x) // 8) * 8
    yrows = len(FORWARD) * size_x * HALO
    send, z_top, z_bottom, y_top, y_bottom = call(
        functools.partial(first_kernel, dims), "first",
        [(groups_x * groups_y, size_x * HALF, 4 * size_y)] + [(zrows, 4 * size_y)] * 2 + [(yrows, size_z)] * 2,
        fields, adjoint, inv_eps, loss_level, tables,
    )
    got = lax.all_to_all(send, ("gy", "gx"), split_axis=0, concat_axis=0, tiled=True)
    got = got.reshape(groups_x * groups_y * size_x * HALF, 4 * size_y)
    gots = [got] + [
        lax.ppermute(got, "gz", [(i, (i + s) % groups_z) for i in range(groups_z)]) for s in range(1, groups_z)
    ]

    z_low, z_high = neighbours("gz", z_top, z_bottom)
    y_low, y_high = neighbours(
        "gy", jnp.concatenate([y_top, z_low, z_high]), jnp.concatenate([y_bottom, z_low, z_high])
    )
    rows = size_y + 8
    state, up, down = call(
        functools.partial(second_kernel, dims), "second",
        [(8 * size_x + 2, rows, size_z + 128), (7 * rows, size_z), (6 * rows, size_z)],
        fields, inv_eps, loss_level, z_low, z_high, y_low, y_high,
    )
    steps = [(i, i + 1) for i in range(groups_x - 1)]
    low = lax.ppermute(up, "gx", steps)
    high = lax.ppermute(down, "gx", [(t, s) for s, t in steps])
    (fields_out,) = call(
        functools.partial(third_kernel, dims), "third", [(6, size_x, size_y, size_z)], state, low, high
    )

    table_x, table_yz = steering(groups_x * size_x, groups_y * size_y, groups_z, size_z, direction)
    pattern, elem = call(
        functools.partial(main_kernel, dims, slots), "main", [(1, nd), (1, per_owner)],
        *gots, table_yz, table_x, pattern_weight.reshape(1, nd),
    )
    return (fields_out, pattern.reshape(nd), elem.reshape(per_owner))


def solution(mesh):
    in_specs = (
        P(None, ("groups", "gx"), "gy", "gz"),
        P(None, ("groups", "gx"), "gy", "gz"),
        P(("groups", "gx"), "gy", "gz"),
        P(("groups", "gx"), "gy", "gz"),
        P(),
        P(),
        P(("groups", "gx"), "gy", "gz", None, None),
        P(("groups", "gx"), "gy", "gz", None, None),
    )
    out_specs = (P(None, ("groups", "gx"), "gy", "gz"), P("groups"), P(("groups", "gx")))
    return jax.shard_map(local, mesh=mesh, in_specs=in_specs, out_specs=out_specs, check_vma=False)
```

```python
import functools
import math

import jax
import jax.numpy as jnp
from jax import lax
from jax.experimental import pallas as pl
from jax.experimental.pallas import tpu as pltpu
from jax.sharding import PartitionSpec as P

STEPS = 2
NE = 1024
OMEGA = 0.9
KAPPA = 0.37
HIGHEST = lax.Precision.HIGHEST
HALO = 2
COMPS = (0, 1, 3, 4)

SETS = (
    ((0, 1, 2, 3), -6, 2),
    ((4, 6, 7, 12), -6, 1),
    ((5, 13, 8, 9), -6, 1),
    ((10, 11), -6, 0),
)
STARTS = (0, 9, 17, 25)
HALF = 32
FORWARD = (0, 1, 2, 3, 4, 5, 12, 13)


def coefficients(inv_eps, level):
    level = 0.15 * level
    return ((1.0 - level) / (1.0 + level), 0.5 * inv_eps / (1.0 + level))


def place_of(m):
    for t, (members, _, _) in enumerate(SETS):
        if m in members:
            return t, members.index(m)


def neighbours(axis, top, bottom):
    count = lax.axis_size(axis)
    if count == 2:
        other = lax.ppermute(top, axis, [(0, 1), (1, 0)])
        return other, other
    forward = [(i, i + 1) for i in range(count - 1)]
    return lax.ppermute(top, axis, forward), lax.ppermute(bottom, axis, [(t, s) for s, t in forward])


def fetch(pairs, sems):
    copies = [pltpu.make_async_copy(src, dst, sems.at[i]) for i, (src, dst) in enumerate(pairs)]
    for copy in copies:
        copy.start()
    for copy in copies:
        copy.wait()


def first_kernel(dims, at, *refs):
    groups_x, groups_y, groups_z, size_x, size_y, size_z = dims
    borders = 1 if groups_z == 2 else 2, 1 if groups_y == 2 else 2
    sources, refs = refs[:6], refs[6:]
    send_ref, refs = refs[0], refs[1:]
    z_refs, y_refs, refs = refs[: borders[0]], refs[borders[0] : sum(borders)], refs[sum(borders) :]
    f_ref, a_ref, ie_ref, ll_ref, cell_ref, elem_ref, sems = refs
    fetch(list(zip(sources, refs[:6])), sems)

    def array(m, x):
        if m < 6:
            return f_ref[m, x]
        if m < 12:
            return a_ref[m - 6, x]
        return ie_ref[x] if m == 12 else ll_ref[x].astype(jnp.float32)

    def store(targets, index, top, bottom):
        if len(targets) == 1:
            targets[0][...] = jnp.where(index == 0, top, bottom)
        else:
            targets[0][...], targets[1][...] = top, bottom

    zs = size_z // 2 + 2
    lists, slots = cell_ref.shape
    per_row = 2 * size_y // slots
    deep = SETS[3][2] - SETS[3][1] + 1
    tops, bottoms = [], []
    for x in range(size_x):
        parts = []
        for t, (members, low, high) in enumerate(SETS):
            blocks = [array(m, x) for m in members]
            blocks += [jnp.zeros((size_y, size_z), jnp.float32)] * (4 - len(members))
            flipped = jnp.concatenate(blocks, axis=0).T
            parts.append(flipped[zs + low : zs + high + 1])
            if t < 3:
                tops.append(flipped[size_z - HALO :])
                bottoms.append(flipped[:HALO])
        if x < 2:
            table = (cell_ref, elem_ref)[x][...].astype(jnp.float32)
            lines = []
            for r in range(0, lists, per_row):
                line = [table[i : i + 1] for i in range(r, min(r + per_row, lists))]
                if len(line) < per_row:
                    line.append(jnp.zeros((1, (per_row - len(line)) * slots), jnp.float32))
                lines.append(jnp.concatenate(line, axis=1))
            lines.append(jnp.zeros((deep - len(lines), 2 * size_y), jnp.float32))
            parts[3] = jnp.concatenate([parts[3][:, : 2 * size_y], jnp.concatenate(lines, axis=0)], axis=1)
        rows = jnp.concatenate(parts, axis=0)
        for d in range(groups_x * groups_y):
            send_ref[d, x * HALF : (x + 1) * HALF] = rows
    pad = [jnp.zeros((z_refs[0].shape[0] - HALO * len(tops), 4 * size_y), jnp.float32)]
    store(z_refs, at[2], jnp.concatenate(tops + pad, axis=0), jnp.concatenate(bottoms + pad, axis=0))
    layers = [array(m, x) for m in FORWARD for x in range(size_x)]
    top = jnp.concatenate([a[size_y - HALO :] for a in layers], axis=0)
    store(y_refs, at[1], top, jnp.concatenate([a[:HALO] for a in layers], axis=0))


def wide_masks(dims, at):
    _, _, _, _, size_y, size_z = dims
    shape = (size_y + 8, size_z + 128)
    row = lax.broadcasted_iota(jnp.int32, shape, 0)
    lane = lax.broadcasted_iota(jnp.int32, shape, 1)
    out_y = jnp.logical_and(row >= size_y + 4, at[1] == 0)
    out_z = jnp.logical_and(lane >= size_z + 64, at[2] == 0)
    return jnp.where(jnp.logical_or(out_y, out_z), 0.0, 0.5)


def forward_y(a):
    return pltpu.roll(a, a.shape[0] - 1, 0) - a


def forward_z(a):
    return pltpu.roll(a, a.shape[1] - 1, 1) - a


def backward_y(a):
    return a - pltpu.roll(a, 1, 0)


def backward_z(a):
    return a - pltpu.roll(a, 1, 1)


def pack(planes, size_z):
    lane = lax.broadcasted_iota(jnp.int32, (planes[0].shape[0], 128), 1)
    border = jnp.zeros((planes[0].shape[0], 128), jnp.float32)
    for p, plane in enumerate(planes):
        moved = pltpu.roll(plane[:, size_z:], 8 * p + 2, 1)
        border = jnp.where(jnp.logical_and(lane >= 8 * p, lane < 8 * p + 4), moved, border)
    return [plane[:, :size_z] for plane in planes] + [border]


def unpack(blocks):
    border = blocks[-1]
    lane = lax.broadcasted_iota(jnp.int32, border.shape, 1)
    keep = jnp.logical_or(lane < 2, lane >= 126)
    out = []
    for p, block in enumerate(blocks[:-1]):
        moved = pltpu.roll(border, 128 - (8 * p + 2), 1)
        out.append(jnp.concatenate([block, jnp.where(keep, moved, 0.0)], axis=1))
    return out


def second_kernel(dims, at, f_ref, ie_ref, ll_ref, zl_ref, zh_ref, yl_ref, yh_ref, state_ref, one_ref, two_ref):
    groups_x, groups_y, groups_z, size_x, size_y, size_z = dims
    zrows = zl_ref.shape[0]
    lane = lax.broadcasted_iota(jnp.int32, (8, 128), 1)
    high_lane = jnp.logical_and(lane < HALO, at[2] < groups_z - 1)
    low_lane = jnp.logical_and(lane >= 128 - HALO, at[2] > 0)
    y_high = (at[1] < groups_y - 1).astype(jnp.float32)
    y_low = (at[1] > 0).astype(jnp.float32)

    def flip(a):
        return jnp.concatenate([a, jnp.zeros((128 - zrows, a.shape[1]), jnp.float32)], axis=0).T

    own_low, own_high = flip(zl_ref[...]), flip(zh_ref[...])
    edge = HALO * size_x * len(FORWARD)
    after = edge if groups_z == 2 else edge + zrows
    yl_low, yl_high = flip(yl_ref[edge : edge + zrows]), flip(yl_ref[after : after + zrows])
    yh_low, yh_high = flip(yh_ref[edge : edge + zrows]), flip(yh_ref[after : after + zrows])

    def column(low, high, rows, at):
        reps = rows // 8
        hl = jnp.concatenate([high_lane] * reps, axis=0)
        ll = jnp.concatenate([low_lane] * reps, axis=0)
        moved_high = pltpu.roll(high, (128 - at) % 128, 1)
        moved_low = pltpu.roll(low, (128 - HALO - at) % 128, 1)
        return jnp.where(hl, moved_high, jnp.where(ll, moved_low, 0.0))

    def wide(m, x):
        t, q = place_of(m)
        at = (x * 3 + t) * HALO
        if m < 6:
            body = f_ref[m, x]
        else:
            body = ie_ref[x] if m == 12 else ll_ref[x].astype(jnp.float32)
        rows = slice(q * size_y, (q + 1) * size_y)
        body_z = column(own_low[rows], own_high[rows], size_y, at)
        start = (FORWARD.index(m) * size_x + x) * HALO
        blank = jnp.zeros((8 - 2 * HALO, 128), jnp.float32)
        first, last = q * size_y, (q + 1) * size_y
        tile = jnp.concatenate(
            [yh_ref[start : start + HALO] * y_high, blank, yl_ref[start : start + HALO] * y_low], axis=0
        )
        low = jnp.concatenate(
            [yh_low[first : first + HALO] * y_high, blank, yl_low[last - HALO : last] * y_low], axis=0
        )
        high = jnp.concatenate(
            [yh_high[first : first + HALO] * y_high, blank, yl_high[last - HALO : last] * y_low], axis=0
        )
        corner = column(low, high, 8, at)
        return jnp.concatenate(
            [jnp.concatenate([body, body_z], axis=1), jnp.concatenate([tile, corner], axis=1)], axis=0
        )

    half = wide_masks(dims, at)
    xs = range(size_x)
    ex, ey, ez, hx, hy, hz, ie, lv = ([wide(m, x) for x in xs] for m in FORWARD)
    pairs = [coefficients(ie[x], lv[x]) for x in xs]
    ca, cb = [p[0] for p in pairs], [p[1] for p in pairs]
    nothing = jnp.zeros_like(half)
    hx = [hx[x] - half * (forward_y(ez[x]) - forward_z(ey[x])) for x in xs]
    hy = [hy[x] - half * (forward_z(ex[x]) - ((ez[x + 1] if x + 1 < size_x else nothing) - ez[x])) for x in xs]
    hz = [hz[x] - half * (((ey[x + 1] if x + 1 < size_x else nothing) - ey[x]) - forward_y(ex[x])) for x in xs]
    first_ey, first_ez = ey[0], ez[0]
    ex = [ca[x] * ex[x] + cb[x] * (backward_y(hz[x]) - backward_z(hy[x])) for x in xs]
    ey = [ca[x] * ey[x] + cb[x] * (backward_z(hx[x]) - (hz[x] - (hz[x - 1] if x else nothing))) for x in xs]
    ez = [ca[x] * ez[x] + cb[x] * ((hy[x] - (hy[x - 1] if x else nothing)) - backward_y(hx[x])) for x in xs]
    state = [*ex, *ey, *ez, *hx, *hy, *hz, *ca, *cb, first_ey, first_ez]
    for i, a in enumerate(state):
        state_ref[i] = a
    up = pack([hy[-1], hz[-1], ex[-1], ey[-1], ez[-1], cb[-1]], size_z)
    down = pack([first_ey, first_ez, ey[0], ez[0], cb[0]], size_z)
    rows = size_y + 8
    even = lax.rem(at[0], 2) == 0
    for i, a in enumerate(up):
        other = down[i] if i < len(down) else a
        one_ref[i * rows : (i + 1) * rows] = jnp.where(even, a, other)
        two_ref[i * rows : (i + 1) * rows] = jnp.where(even, other, a)


def third_kernel(dims, at, state_ref, one_ref, two_ref, out_ref):
    groups_x, groups_y, groups_z, size_x, size_y, size_z = dims
    xs = range(size_x)
    half = wide_masks(dims, at)
    half_low = half * (at[0] > 0).astype(jnp.float32)
    state = [[state_ref[i * size_x + x] for x in xs] for i in range(8)]
    ex, ey, ez, hx, hy, hz, ca, cb = state
    first_ey, first_ez = state_ref[8 * size_x], state_ref[8 * size_x + 1]
    rows = size_y + 8
    even = lax.rem(at[0], 2) == 0
    low, high = [], []
    for i in range(7):
        one, two = one_ref[i * rows : (i + 1) * rows], two_ref[i * rows : (i + 1) * rows]
        low.append(jnp.where(even, two, one))
        high.append(jnp.where(even, one, two))
    low_hy, low_hz, low_ex, low_ey, low_ez, low_cb = unpack(low)
    next_ey, next_ez, high_ey, high_ez, high_cb = unpack(high[:6])
    add_y, add_z = half * next_ez, -(half * next_ey)
    hy[-1], hz[-1] = hy[-1] + add_y, hz[-1] + add_z
    ex[-1] = ex[-1] + cb[-1] * (backward_y(add_z) - backward_z(add_y))
    ey[-1] = ey[-1] - cb[-1] * add_z
    ez[-1] = ez[-1] + cb[-1] * add_y
    add_y, add_z = half_low * first_ez, -(half_low * first_ey)
    low_hy, low_hz = low_hy + add_y, low_hz + add_z
    low_ex = low_ex + low_cb * (backward_y(add_z) - backward_z(add_y))
    low_ey = low_ey - low_cb * add_z
    low_ez = low_ez + low_cb * add_y
    ey[0] = ey[0] + cb[0] * low_hz
    ez[0] = ez[0] - cb[0] * low_hy
    high_ey = high_ey + high_cb * hz[-1]
    high_ez = high_ez - high_cb * hy[-1]
    low_hy = low_hy - half_low * (forward_z(low_ex) - (ez[0] - low_ez))
    low_hz = low_hz - half_low * ((ey[0] - low_ey) - forward_y(low_ex))
    after_ey, after_ez = ey[1:] + [high_ey], ez[1:] + [high_ez]
    hx = [hx[x] - half * (forward_y(ez[x]) - forward_z(ey[x])) for x in xs]
    hy = [hy[x] - half * (forward_z(ex[x]) - (after_ez[x] - ez[x])) for x in xs]
    hz = [hz[x] - half * ((after_ey[x] - ey[x]) - forward_y(ex[x])) for x in xs]
    before_hy, before_hz = [low_hy] + hy[:-1], [low_hz] + hz[:-1]
    for x in xs:
        new = (
            ca[x] * ex[x] + cb[x] * (backward_y(hz[x]) - backward_z(hy[x])),
            ca[x] * ey[x] + cb[x] * (backward_z(hx[x]) - (hz[x] - before_hz[x])),
            ca[x] * ez[x] + cb[x] * ((hy[x] - before_hy[x]) - backward_y(hx[x])),
            hx[x], hy[x], hz[x],
        )
        for m in range(6):
            out_ref[m, x] = new[m][:size_y, :size_z]


def steering(count_x, count_y, groups_z, size_z, direction, weight):
    zs = size_z // 2 + 2
    xs = jnp.arange(count_x, dtype=jnp.float32)[:, None]
    ys = jnp.arange(count_y, dtype=jnp.float32)[None, :, None]
    zval = (jnp.arange(groups_z, dtype=jnp.float32) * size_z + zs)[:, None, None]
    phase_x = KAPPA * xs * direction[0]
    phase_yz = (KAPPA * (ys * direction[1] + zval * direction[2])).reshape(groups_z * count_y, -1)
    return (
        jnp.concatenate([jnp.cos(phase_x), jnp.sin(phase_x), jnp.broadcast_to(weight, phase_x.shape)], axis=1),
        jnp.concatenate([jnp.cos(phase_yz), jnp.sin(phase_yz)], axis=1),
    )


def main_kernel(slots, dims, at, *refs):
    groups_x, groups_y, groups_z, size_x, size_y, size_z = dims
    got_refs = refs[:groups_z]
    yz_ref, x_ref, pattern_ref, elem_ref = refs[groups_z:]
    per_owner = NE // groups_x
    count_x, count_y = groups_x * size_x, groups_y * size_y
    lanes = groups_z * count_y
    zs = size_z // 2 + 2

    def pick(c, start, size, stride):
        out = None
        for s, ref in enumerate(got_refs):
            part = ref[pl.ds(start, size, stride=stride), :]
            here = lax.rem(at[2] - s + groups_z, groups_z) == c
            out = part if out is None else jnp.where(here, part, out)
        return out

    loaded = {}

    def plane(m, k):
        t, q = place_of(m)
        row = STARTS[t] + k - SETS[t][1]
        if row not in loaded:
            loaded[row] = [
                pick(c, b * groups_x * size_x * HALF + row, count_x, HALF)
                for c in range(groups_z)
                for b in range(groups_y)
            ]
        return jnp.concatenate([p[:, q * size_y : (q + 1) * size_y] for p in loaded[row]], axis=1)

    row_id = lax.broadcasted_iota(jnp.int32, (count_x, lanes), 0)
    lane_id = lax.broadcasted_iota(jnp.int32, (count_x, lanes), 1) % count_y
    x_up, x_low = row_id < count_x - 1, row_id > 0
    y_up, y_low = lane_id < count_y - 1, lane_id > 0

    def dxp(a):
        return jnp.where(x_up, pltpu.roll(a, count_x - 1, 0), 0.0) - a

    def dyp(a):
        return jnp.where(y_up, pltpu.roll(a, lanes - 1, 1), 0.0) - a

    def dxm(a):
        return a - jnp.where(x_low, pltpu.roll(a, 1, 0), 0.0)

    def dym(a):
        return a - jnp.where(y_low, pltpu.roll(a, 1, 1), 0.0)

    ca, cb = {}, {}
    for k in range(-5, 2):
        ca[k], cb[k] = coefficients(plane(12, k), plane(13, k))

    def step(ex, ey, ez, hx, hy, hz, low, high):
        nhx = {k: hx[k] - 0.5 * (dyp(ez[k]) - (ey[k + 1] - ey[k])) for k in range(low - 1, high + 1)}
        nhy = {k: hy[k] - 0.5 * ((ex[k + 1] - ex[k]) - dxp(ez[k])) for k in range(low - 1, high + 1)}
        nhz = {k: hz[k] - 0.5 * (dxp(ey[k]) - dyp(ex[k])) for k in range(low, high + 1)}
        nex = {k: ca[k] * ex[k] + cb[k] * (dym(nhz[k]) - (nhy[k] - nhy[k - 1])) for k in range(low, high + 1)}
        ney = {k: ca[k] * ey[k] + cb[k] * ((nhx[k] - nhx[k - 1]) - dxm(nhz[k])) for k in range(low, high + 1)}
        nez = {k: ca[k] * ez[k] + cb[k] * (dxm(nhy[k]) - dym(nhx[k])) for k in range(low, high + 1)}
        return nex, ney, nez, nhx, nhy, nhz

    def arrays(first):
        spans = [SETS[place_of(m)[0]] for m in range(first, first + 6)]
        return [{k: plane(first + i, k) for k in range(s[1], s[2] + 1)} for i, s in enumerate(spans)]

    u1 = step(*arrays(0), -5, 1)
    u2 = step(*u1, -4, 0)
    rows = []
    for m in (0, 1, 3, 4):
        rows.append(u1[m][0] * math.cos(OMEGA) + u2[m][0] * math.cos(2 * OMEGA))
        rows.append(-u1[m][0] * math.sin(OMEGA) - u2[m][0] * math.sin(2 * OMEGA))
    dft = jnp.concatenate(rows, axis=0)

    yz = yz_ref[...]
    nd = yz.shape[1] // 2
    cos_x, sin_x, weight = x_ref[:, :nd], x_ref[:, nd : 2 * nd], x_ref[:1, 2 * nd :]
    amp = 1.0 / math.sqrt(count_x * count_y * groups_z)
    prod = jnp.dot(dft, yz, precision=HIGHEST, preferred_element_type=jnp.float32)
    pattern = jnp.zeros((1, nd), jnp.float32)
    weight = (2.0 * amp) * weight
    mixing = []
    for c in range(4):
        re = prod[2 * c * count_x : (2 * c + 1) * count_x]
        im = prod[(2 * c + 1) * count_x : (2 * c + 2) * count_x]
        real = re[:, :nd] - im[:, nd:]
        imag = re[:, nd:] + im[:, :nd]
        far_re = amp * jnp.sum(real * cos_x - imag * sin_x, axis=0, keepdims=True)
        far_im = amp * jnp.sum(real * sin_x + imag * cos_x, axis=0, keepdims=True)
        pattern = pattern + far_re * far_re + far_im * far_im
        out_re, out_im = weight * far_re, weight * far_im
        b_re = out_re * cos_x + out_im * sin_x
        b_im = out_im * cos_x - out_re * sin_x
        mixing.append(jnp.concatenate([b_re, b_im], axis=1))
        mixing.append(jnp.concatenate([b_im, -b_re], axis=1))
    pattern_ref[...] = pattern

    src = lax.dot_general(
        jnp.concatenate(mixing, axis=0), yz, (((1,), (1,)), ((), ())),
        precision=HIGHEST, preferred_element_type=jnp.float32,
    )

    def with_sources(state, when):
        state = [dict(a) for a in state]
        for c, m in enumerate((0, 1, 3, 4)):
            gre = src[2 * c * count_x : (2 * c + 1) * count_x]
            gim = src[(2 * c + 1) * count_x : (2 * c + 2) * count_x]
            state[m][0] = state[m][0] + (gre * math.cos(OMEGA * when) - gim * math.sin(OMEGA * when))
        return state

    v1 = step(*with_sources(arrays(6), 2), -5, 0)
    v2 = step(*with_sources(v1, 1), -4, -1)
    sens = [
        sum(v1[m][k] * u2[m][k] for m in range(3)) + sum(v2[m][k] * u1[m][k] for m in range(3))
        for k in range(-4, 0)
    ]
    sens = jnp.concatenate(sens, axis=0)

    own = at[0]
    senders = groups_x * groups_y * groups_z
    total = senders * slots
    lists = groups_x * slots
    pieces = range(-(-lists // (2 * size_y)))

    def table(x):
        return jnp.concatenate(
            [
                jnp.concatenate(
                    [
                        pick(c, x * HALF + STARTS[3] + r, groups_x * groups_y, size_x * HALF)[:, 2 * size_y :]
                        for c in range(groups_z)
                    ],
                    axis=0,
                )
                for r in pieces
            ],
            axis=1,
        )

    cell_tab, elem_tab = table(0), table(1)
    width = cell_tab.shape[1]
    at = lax.broadcasted_iota(jnp.int32, (width, total), 0)
    slot = lax.broadcasted_iota(jnp.int32, (width, total), 1)
    spread_cell = (at == own * slots + slot % slots).astype(jnp.float32)
    spread_elem = (at == slot % lists).astype(jnp.float32)
    sender = lax.broadcasted_iota(jnp.int32, (senders, total), 0)
    slot = lax.broadcasted_iota(jnp.int32, (senders, total), 1)
    cells = jnp.dot(cell_tab, spread_cell, precision=HIGHEST, preferred_element_type=jnp.float32)
    cells = jnp.sum(jnp.where(sender == slot // slots, cells, 0.0), axis=0, keepdims=True)
    elems = jnp.dot(elem_tab, spread_elem, precision=HIGHEST, preferred_element_type=jnp.float32)
    elems = jnp.sum(
        jnp.where(sender == (slot // lists) * groups_x + own, elems, 0.0), axis=0, keepdims=True
    )
    cells = (cells + 0.5).astype(jnp.int32)
    elems = (elems + 1.5).astype(jnp.int32) - 1
    slot = lax.broadcasted_iota(jnp.int32, (1, total), 1)
    block = slot // lists
    place_x = (slot // slots % groups_x) * size_x + cells // (size_y * size_z)
    place_y = cells // size_z % size_y
    place_z = cells % size_z - (zs - 4)
    row_want = place_z * count_x + place_x
    lane_want = (block // groups_y) * count_y + (block % groups_y) * size_y + place_y
    hot_row = (lax.broadcasted_iota(jnp.int32, (4 * count_x, total), 0) == row_want).astype(jnp.float32)
    hot_lane = lax.broadcasted_iota(jnp.int32, (lanes, total), 0) == lane_want
    picked = lax.dot_general(
        sens, hot_row, (((0,), (0,)), ((), ())), precision=HIGHEST, preferred_element_type=jnp.float32
    )
    values = jnp.sum(jnp.where(hot_lane, picked, 0.0), axis=0, keepdims=True)
    hot_elem = (lax.broadcasted_iota(jnp.int32, (per_owner, total), 0) == elems).astype(jnp.float32)
    sums = lax.dot_general(
        jnp.broadcast_to(values, (8, total)), hot_elem, (((1,), (1,)), ((), ())),
        precision=HIGHEST, preferred_element_type=jnp.float32,
    )
    scale = 1.0 / math.sqrt(groups_x * groups_x * groups_y * groups_z * slots / NE)
    elem_ref[...] = sums[:1] * scale


def local(fields, adjoint, inv_eps, loss_level, direction, pattern_weight, voxel_cell, voxel_elem):
    size_x, size_y, size_z = inv_eps.shape
    groups_x, groups_y, groups_z = (lax.axis_size(a) for a in ("gx", "gy", "gz"))
    dims = (groups_x, groups_y, groups_z, size_x, size_y, size_z)
    slots = voxel_cell.shape[4]
    per_owner = NE // groups_x
    nd = direction.shape[1]
    vmem = pl.BlockSpec(memory_space=pltpu.VMEM)
    hbm = pl.BlockSpec(memory_space=pltpu.HBM)

    def call(kernel, name, outs, *args, fetched=0, limit=48):
        scratch = [pltpu.VMEM(a.shape, a.dtype) for a in args[:fetched]]
        if fetched:
            scratch.append(pltpu.SemaphoreType.DMA((fetched,)))

        def located(*refs):
            kernel(dims, tuple(lax.axis_index(a) for a in ("gx", "gy", "gz")), *refs)

        return pl.pallas_call(
            located,
            out_shape=tuple(jax.ShapeDtypeStruct(o, jnp.float32) for o in outs),
            in_specs=[hbm] * fetched + [vmem] * (len(args) - fetched),
            out_specs=(vmem,) * len(outs),
            scratch_shapes=scratch,
            compiler_params=pltpu.CompilerParams(vmem_limit_bytes=limit * 1024 * 1024),
            name=name,
        )(*args)

    zrows = -(-(3 * HALO * size_x) // 8) * 8
    yrows = len(FORWARD) * size_x * HALO
    z_count, y_count = 1 if groups_z == 2 else 2, 1 if groups_y == 2 else 2
    send, *edges = call(
        first_kernel, "first",
        [(groups_x * groups_y, size_x * HALF, 4 * size_y)]
        + [(zrows, 4 * size_y)] * z_count + [(yrows, size_z)] * y_count,
        fields, adjoint, inv_eps, loss_level, voxel_cell.reshape(groups_x, slots),
        voxel_elem.reshape(groups_x, slots), fetched=6, limit=60,
    )
    z_top, z_bottom = edges[0], edges[z_count - 1]
    y_top, y_bottom = edges[z_count], edges[-1]
    z_low, z_high = neighbours("gz", z_top, z_bottom)
    z_sides = [z_low] if groups_z == 2 else [z_low, z_high]
    y_low, y_high = neighbours("gy", jnp.concatenate([y_top] + z_sides), jnp.concatenate([y_bottom] + z_sides))
    got = lax.all_to_all(send, ("gy", "gx"), split_axis=0, concat_axis=0, tiled=True)
    got = got.reshape(groups_x * groups_y * size_x * HALF, 4 * size_y)
    table_x, table_yz = steering(
        groups_x * size_x, groups_y * size_y, groups_z, size_z, direction, pattern_weight
    )
    y_low, y_high, table_x, table_yz = lax.optimization_barrier((y_low, y_high, table_x, table_yz))

    rows = size_y + 8
    state, one, two = call(
        second_kernel, "second",
        [(8 * size_x + 2, rows, size_z + 128)] + [(7 * rows, size_z)] * 2,
        fields, inv_eps, loss_level, z_low, z_high, y_low, y_high,
    )
    one_side, other_side = (
        lax.ppermute(sent, "gx", [p for i in range(first, groups_x - 1, 2) for p in ((i, i + 1), (i + 1, i))])
        for first, sent in ((0, one), (1, two))
    )

    got, _ = lax.optimization_barrier((got, one))
    gots = [got] + [
        lax.ppermute(got, "gz", [(i, (i + s) % groups_z) for i in range(groups_z)]) for s in range(1, groups_z)
    ]

    pattern, elem = call(
        functools.partial(main_kernel, slots), "main", [(1, nd), (1, per_owner)],
        *gots, table_yz, table_x,
    )
    state, pattern = lax.optimization_barrier((state, pattern))
    (fields_out,) = call(
        third_kernel, "third", [(6, size_x, size_y, size_z)], state, one_side, other_side
    )
    return (fields_out, pattern.reshape(nd), elem.reshape(per_owner))


def solution(mesh):
    in_specs = (
        P(None, ("groups", "gx"), "gy", "gz"),
        P(None, ("groups", "gx"), "gy", "gz"),
        P(("groups", "gx"), "gy", "gz"),
        P(("groups", "gx"), "gy", "gz"),
        P(),
        P(),
        P(("groups", "gx"), "gy", "gz", None, None),
        P(("groups", "gx"), "gy", "gz", None, None),
    )
    out_specs = (P(None, ("groups", "gx"), "gy", "gz"), P("groups"), P(("groups", "gx")))
    return jax.shard_map(local, mesh=mesh, in_specs=in_specs, out_specs=out_specs, check_vma=False)
```

```python
import functools
import math

import jax
import jax.numpy as jnp
from jax import lax
from jax.experimental import pallas as pl
from jax.experimental.pallas import tpu as pltpu
from jax.sharding import PartitionSpec as P

STEPS = 2
NE = 1024
OMEGA = 0.9
KAPPA = 0.37
HIGHEST = lax.Precision.HIGHEST
HALO = 2
COMPS = (0, 1, 3, 4)

SETS = ((0, 1, 2, 3), (4, 6, 7, 12), (5, 13, 8, 9), (10, 11))
STARTS = (0, 9, 17, 24)
BODY = 28
LOWEST = (-6, -6, -6, -6, -6, -5, -6, -6, -6, -6, -6, -6, -6, -5)
TOPMOST = (2, 2, 1, 1, 1, 1, 1, 1, 0, 0, 0, 0, 1, 1)
FORWARD = (0, 1, 2, 3, 4, 5, 12, 13)


def coefficients(inv_eps, level):
    level = 0.15 * level
    return ((1.0 - level) / (1.0 + level), 0.5 * inv_eps / (1.0 + level))


def place_of(m):
    for t, members in enumerate(SETS):
        if m in members:
            return t, members.index(m)


def slab_place(m, k):
    t, q = place_of(m)
    if t == 3:
        return STARTS[t] + (k - LOWEST[m]) % 4, q + 2 * ((k - LOWEST[m]) // 4)
    return STARTS[t] + k - LOWEST[m], q


def half_rows(lists, size_y):
    return BODY if lists <= 2 * size_y else BODY + 4


def neighbours(axis, top, bottom):
    count = lax.axis_size(axis)
    if count == 2:
        other = lax.ppermute(top, axis, [(0, 1), (1, 0)])
        return other, other
    forward = [(i, i + 1) for i in range(count - 1)]
    return lax.ppermute(top, axis, forward), lax.ppermute(bottom, axis, [(t, s) for s, t in forward])


def fetch(pairs, sems):
    copies = [pltpu.make_async_copy(src, dst, sems.at[i]) for i, (src, dst) in enumerate(pairs)]
    for copy in copies:
        copy.start()
    for copy in copies:
        copy.wait()


def first_kernel(dims, at, *refs):
    groups_x, groups_y, groups_z, size_x, size_y, size_z = dims
    borders = 1 if groups_z == 2 else 2, 1 if groups_y == 2 else 2
    sources, refs = refs[:6], refs[6:]
    send_ref, refs = refs[0], refs[1:]
    z_refs, y_refs, refs = refs[: borders[0]], refs[borders[0] : sum(borders)], refs[sum(borders) :]
    f_ref, a_ref, ie_ref, ll_ref, cell_ref, elem_ref, sems = refs
    fetch(list(zip(sources, refs[:6])), sems)

    def array(m, x):
        if m < 6:
            return f_ref[m, x]
        if m < 12:
            return a_ref[m - 6, x]
        return ie_ref[x] if m == 12 else ll_ref[x].astype(jnp.float32)

    def store(targets, index, top, bottom):
        if len(targets) == 1:
            targets[0][...] = jnp.where(index == 0, top, bottom)
        else:
            targets[0][...], targets[1][...] = top, bottom

    zs = size_z // 2 + 2
    lists, slots = cell_ref.shape
    half = half_rows(lists * slots, size_y)
    per_row = (2 if half == BODY else 4) * size_y // slots
    tops, bottoms = [], []
    for x in range(size_x):
        parts = []
        for t, members in enumerate(SETS):
            blocks = [array(m, x) for m in members]
            blocks += [jnp.zeros((size_y, size_z), jnp.float32)] * (4 - len(members))
            flipped = jnp.concatenate(blocks, axis=0).T
            if t < 2:
                parts.append(flipped[zs + LOWEST[members[0]] : zs + TOPMOST[members[0]] + 1])
            else:
                first, last = (-5, -6) if t == 2 else (-6, -2)
                count, last_lanes = (7, slice(2 * size_y, None)) if t == 2 else (4, slice(0, 2 * size_y))
                left = flipped[zs + first : zs + first + count, : 2 * size_y]
                parts.append(jnp.concatenate([left, flipped[zs + last : zs + last + count, last_lanes]], axis=1))
            if t < 3:
                tops.append(flipped[size_z - HALO :])
                bottoms.append(flipped[:HALO])
        if x < 2:
            table = (cell_ref, elem_ref)[x][...].astype(jnp.float32)
            lines = []
            for r in range(0, lists, per_row):
                line = [table[i : i + 1] for i in range(r, min(r + per_row, lists))]
                if len(line) < per_row:
                    line.append(jnp.zeros((1, (per_row - len(line)) * slots), jnp.float32))
                lines.append(jnp.concatenate(line, axis=1))
            if half == BODY:
                last = jnp.concatenate([parts[0][8:, : 2 * size_y], lines[0]], axis=1)
                parts[0] = jnp.concatenate([parts[0][:8], last], axis=0)
            else:
                lines.append(jnp.zeros((half - BODY - len(lines), 4 * size_y), jnp.float32))
                parts += lines
        rows = jnp.concatenate(parts, axis=0)
        for d in range(groups_x * groups_y):
            send_ref[d, x * half : (x + 1) * half] = rows
    pad = [jnp.zeros((z_refs[0].shape[0] - HALO * len(tops), 4 * size_y), jnp.float32)]
    store(z_refs, at[2], jnp.concatenate(tops + pad, axis=0), jnp.concatenate(bottoms + pad, axis=0))
    layers = [array(m, x) for m in FORWARD for x in range(size_x)]
    top = jnp.concatenate([a[size_y - HALO :] for a in layers], axis=0)
    store(y_refs, at[1], top, jnp.concatenate([a[:HALO] for a in layers], axis=0))


def wide_masks(dims, at):
    _, _, _, _, size_y, size_z = dims
    shape = (size_y + 8, size_z + 128)
    row = lax.broadcasted_iota(jnp.int32, shape, 0)
    lane = lax.broadcasted_iota(jnp.int32, shape, 1)
    out_y = jnp.logical_and(row >= size_y + 4, at[1] == 0)
    out_z = jnp.logical_and(lane >= size_z + 64, at[2] == 0)
    return jnp.where(jnp.logical_or(out_y, out_z), 0.0, 0.5)


def forward_y(a):
    return pltpu.roll(a, a.shape[0] - 1, 0) - a


def forward_z(a):
    return pltpu.roll(a, a.shape[1] - 1, 1) - a


def backward_y(a):
    return a - pltpu.roll(a, 1, 0)


def backward_z(a):
    return a - pltpu.roll(a, 1, 1)


def pack(planes, size_y, size_z):
    row = lax.broadcasted_iota(jnp.int32, (8, size_z), 0)
    own = jnp.logical_or(row < 2, row >= 6)
    lane = lax.broadcasted_iota(jnp.int32, (planes[0].shape[0], 128), 1)
    out = [plane[:size_y, :size_z] for plane in planes]
    for p in range(0, len(planes), 2):
        tile = planes[p][size_y:, :size_z]
        if p + 1 < len(planes):
            tile = jnp.where(own, tile, pltpu.roll(planes[p + 1][size_y:, :size_z], 4, 0))
        out.append(tile)
    border = jnp.zeros((planes[0].shape[0], 128), jnp.float32)
    for p, plane in enumerate(planes):
        moved = pltpu.roll(plane[:, size_z:], 8 * p + 2, 1)
        border = jnp.where(jnp.logical_and(lane >= 8 * p, lane < 8 * p + 4), moved, border)
    return jnp.concatenate(out + [border], axis=0)


def unpack(rows, count, size_y):
    tiles = count * size_y
    border = rows[tiles + 8 * ((count + 1) // 2) :]
    out = []
    for p in range(count):
        tile = rows[tiles + 8 * (p // 2) : tiles + 8 * (p // 2) + 8]
        body = jnp.concatenate(
            [rows[p * size_y : (p + 1) * size_y], pltpu.roll(tile, 4, 0) if p % 2 else tile], axis=0
        )
        out.append(jnp.concatenate([body, pltpu.roll(border, 128 - (8 * p + 2), 1)], axis=1))
    return out


def second_kernel(dims, at, f_ref, ie_ref, ll_ref, zl_ref, zh_ref, yl_ref, yh_ref, state_ref, one_ref, two_ref):
    groups_x, groups_y, groups_z, size_x, size_y, size_z = dims
    zrows = zl_ref.shape[0]
    lane = lax.broadcasted_iota(jnp.int32, (8, 128), 1)
    high_lane = jnp.logical_and(lane < HALO, at[2] < groups_z - 1)
    low_lane = jnp.logical_and(lane >= 128 - HALO, at[2] > 0)
    y_high = (at[1] < groups_y - 1).astype(jnp.float32)
    y_low = (at[1] > 0).astype(jnp.float32)

    def flip(a):
        return jnp.concatenate([a, jnp.zeros((128 - zrows, a.shape[1]), jnp.float32)], axis=0).T

    own_low, own_high = flip(zl_ref[...]), flip(zh_ref[...])
    edge = HALO * size_x * len(FORWARD)
    after = edge if groups_z == 2 else edge + zrows
    yl_low, yl_high = flip(yl_ref[edge : edge + zrows]), flip(yl_ref[after : after + zrows])
    yh_low, yh_high = flip(yh_ref[edge : edge + zrows]), flip(yh_ref[after : after + zrows])

    def column(low, high, rows, at):
        reps = rows // 8
        hl = jnp.concatenate([high_lane] * reps, axis=0)
        ll = jnp.concatenate([low_lane] * reps, axis=0)
        moved_high = pltpu.roll(high, (128 - at) % 128, 1)
        moved_low = pltpu.roll(low, (128 - HALO - at) % 128, 1)
        return jnp.where(hl, moved_high, jnp.where(ll, moved_low, 0.0))

    def wide(m, x):
        t, q = place_of(m)
        at = (x * 3 + t) * HALO
        if m < 6:
            body = f_ref[m, x]
        else:
            body = ie_ref[x] if m == 12 else ll_ref[x].astype(jnp.float32)
        rows = slice(q * size_y, (q + 1) * size_y)
        body_z = column(own_low[rows], own_high[rows], size_y, at)
        start = (FORWARD.index(m) * size_x + x) * HALO
        blank = jnp.zeros((8 - 2 * HALO, 128), jnp.float32)
        first, last = q * size_y, (q + 1) * size_y
        tile = jnp.concatenate(
            [yh_ref[start : start + HALO] * y_high, blank, yl_ref[start : start + HALO] * y_low], axis=0
        )
        low = jnp.concatenate(
            [yh_low[first : first + HALO] * y_high, blank, yl_low[last - HALO : last] * y_low], axis=0
        )
        high = jnp.concatenate(
            [yh_high[first : first + HALO] * y_high, blank, yl_high[last - HALO : last] * y_low], axis=0
        )
        corner = column(low, high, 8, at)
        return jnp.concatenate(
            [jnp.concatenate([body, body_z], axis=1), jnp.concatenate([tile, corner], axis=1)], axis=0
        )

    half = wide_masks(dims, at)
    xs = range(size_x)
    ex, ey, ez, hx, hy, hz, ie, lv = ([wide(m, x) for x in xs] for m in FORWARD)
    pairs = [coefficients(ie[x], lv[x]) for x in xs]
    ca, cb = [p[0] for p in pairs], [p[1] for p in pairs]
    nothing = jnp.zeros_like(half)
    hx = [hx[x] - half * (forward_y(ez[x]) - forward_z(ey[x])) for x in xs]
    hy = [hy[x] - half * (forward_z(ex[x]) - ((ez[x + 1] if x + 1 < size_x else nothing) - ez[x])) for x in xs]
    hz = [hz[x] - half * (((ey[x + 1] if x + 1 < size_x else nothing) - ey[x]) - forward_y(ex[x])) for x in xs]
    first_ey, first_ez = ey[0], ez[0]
    ex = [ca[x] * ex[x] + cb[x] * (backward_y(hz[x]) - backward_z(hy[x])) for x in xs]
    ey = [ca[x] * ey[x] + cb[x] * (backward_z(hx[x]) - (hz[x] - (hz[x - 1] if x else nothing))) for x in xs]
    ez = [ca[x] * ez[x] + cb[x] * ((hy[x] - (hy[x - 1] if x else nothing)) - backward_y(hx[x])) for x in xs]
    state = [*ex, *ey, *ez, *hx, *hy, *hz, *ca, *cb, first_ey, first_ez]
    for i, a in enumerate(state):
        state_ref[i] = a
    next_hy = hy[-1] - half * (forward_z(ex[-1]) + ez[-1])
    next_hz = hz[-1] + half * (ey[-1] + forward_y(ex[-1]))
    up = pack([hy[-1], hz[-1], next_hy, next_hz, cb[-1]], size_y, size_z)
    down = pack([first_ey, first_ez, ey[0], ez[0], cb[0]], size_y, size_z)
    even = lax.rem(at[0], 2) == 0
    one_ref[...] = jnp.where(even, up, down)
    two_ref[...] = jnp.where(even, down, up)


def third_kernel(dims, at, state_ref, one_ref, two_ref, out_ref):
    groups_x, groups_y, groups_z, size_x, size_y, size_z = dims
    xs = range(size_x)
    half = wide_masks(dims, at)
    half_low = half * (at[0] > 0).astype(jnp.float32)
    state = [[state_ref[i * size_x + x] for x in xs] for i in range(8)]
    ex, ey, ez, hx, hy, hz, ca, cb = state
    first_ey, first_ez = state_ref[8 * size_x], state_ref[8 * size_x + 1]
    even = lax.rem(at[0], 2) == 0
    one, two = one_ref[...], two_ref[...]
    low_hy, low_hz, below_hy, below_hz, low_cb = unpack(jnp.where(even, two, one), 5, size_y)
    next_ey, next_ez, high_ey, high_ez, high_cb = unpack(jnp.where(even, one, two), 5, size_y)
    add_y, add_z = half * next_ez, -(half * next_ey)
    hy[-1], hz[-1] = hy[-1] + add_y, hz[-1] + add_z
    ex[-1] = ex[-1] + cb[-1] * (backward_y(add_z) - backward_z(add_y))
    ey[-1] = ey[-1] - cb[-1] * add_z
    ez[-1] = ez[-1] + cb[-1] * add_y
    add_y, add_z = half_low * first_ez, -(half_low * first_ey)
    low_hy, low_hz = low_hy + add_y, low_hz + add_z
    more_ex = low_cb * (backward_y(add_z) - backward_z(add_y))
    more_ey, more_ez = -(low_cb * add_z), low_cb * add_y
    ey[0] = ey[0] + cb[0] * low_hz
    ez[0] = ez[0] - cb[0] * low_hy
    high_ey = high_ey + high_cb * hz[-1]
    high_ez = high_ez - high_cb * hy[-1]
    low_hy = below_hy + add_y - half_low * (forward_z(more_ex) + more_ez - ez[0])
    low_hz = below_hz + add_z + half_low * (more_ey + forward_y(more_ex) - ey[0])
    after_ey, after_ez = ey[1:] + [high_ey], ez[1:] + [high_ez]
    hx = [hx[x] - half * (forward_y(ez[x]) - forward_z(ey[x])) for x in xs]
    hy = [hy[x] - half * (forward_z(ex[x]) - (after_ez[x] - ez[x])) for x in xs]
    hz = [hz[x] - half * ((after_ey[x] - ey[x]) - forward_y(ex[x])) for x in xs]
    before_hy, before_hz = [low_hy] + hy[:-1], [low_hz] + hz[:-1]
    for x in xs:
        new = (
            ca[x] * ex[x] + cb[x] * (backward_y(hz[x]) - backward_z(hy[x])),
            ca[x] * ey[x] + cb[x] * (backward_z(hx[x]) - (hz[x] - before_hz[x])),
            ca[x] * ez[x] + cb[x] * ((hy[x] - before_hy[x]) - backward_y(hx[x])),
            hx[x], hy[x], hz[x],
        )
        for m in range(6):
            out_ref[m, x] = new[m][:size_y, :size_z]


def halves_of_table(a):
    high = lax.reduce_precision(a, 8, 7)
    return high.astype(jnp.bfloat16), (a - high).astype(jnp.bfloat16)


def halves(a):
    high = a.astype(jnp.bfloat16)
    return high, (a - high.astype(jnp.float32)).astype(jnp.bfloat16)


def product(a, high_ref, low_ref, contract):
    high, low = halves(a)
    dims = (((1,), (contract,)), ((), ()))
    both = lax.dot_general(
        jnp.concatenate([high, low], axis=0), high_ref[...], dims, preferred_element_type=jnp.float32
    )
    rest = lax.dot_general(high, low_ref[...], dims, preferred_element_type=jnp.float32)
    return both[: a.shape[0]] + (both[a.shape[0] :] + rest)


def steering(count_x, count_y, groups_z, size_z, direction, weight):
    zs = size_z // 2 + 2
    xs = jnp.arange(count_x, dtype=jnp.float32)[:, None]
    ys = jnp.arange(count_y, dtype=jnp.float32)[None, :, None]
    zval = (jnp.arange(groups_z, dtype=jnp.float32) * size_z + zs)[:, None, None]
    phase_x = KAPPA * xs * direction[0]
    phase_yz = (KAPPA * (ys * direction[1] + zval * direction[2])).reshape(groups_z * count_y, -1)
    return (
        jnp.concatenate([jnp.cos(phase_x), jnp.sin(phase_x), jnp.broadcast_to(weight, phase_x.shape)], axis=1),
        *halves_of_table(jnp.concatenate([jnp.cos(phase_yz), jnp.sin(phase_yz)], axis=1)),
    )


def main_kernel(slots, dims, at, *refs):
    groups_x, groups_y, groups_z, size_x, size_y, size_z = dims
    got_refs = refs[:groups_z]
    high_ref, low_ref, x_ref, pattern_ref, elem_ref = refs[groups_z:]
    per_owner = NE // groups_x
    half = half_rows(groups_x * slots, size_y)
    count_x, count_y = groups_x * size_x, groups_y * size_y
    lanes = groups_z * count_y
    zs = size_z // 2 + 2

    def pick(c, start, size, stride):
        out = None
        for s, ref in enumerate(got_refs):
            part = ref[pl.ds(start, size, stride=stride), :]
            here = lax.rem(at[2] - s + groups_z, groups_z) == c
            out = part if out is None else jnp.where(here, part, out)
        return out

    loaded = {}

    def plane(m, k):
        row, q = slab_place(m, k)
        if row not in loaded:
            loaded[row] = [
                pick(c, b * groups_x * size_x * half + row, count_x, half)
                for c in range(groups_z)
                for b in range(groups_y)
            ]
        return jnp.concatenate([p[:, q * size_y : (q + 1) * size_y] for p in loaded[row]], axis=1)

    row_id = lax.broadcasted_iota(jnp.int32, (count_x, lanes), 0)
    lane_id = lax.broadcasted_iota(jnp.int32, (count_x, lanes), 1) % count_y
    x_up, x_low = row_id < count_x - 1, row_id > 0
    y_up, y_low = lane_id < count_y - 1, lane_id > 0

    def dxp(a):
        return jnp.where(x_up, pltpu.roll(a, count_x - 1, 0), 0.0) - a

    def dyp(a):
        return jnp.where(y_up, pltpu.roll(a, lanes - 1, 1), 0.0) - a

    def dxm(a):
        return a - jnp.where(x_low, pltpu.roll(a, 1, 0), 0.0)

    def dym(a):
        return a - jnp.where(y_low, pltpu.roll(a, 1, 1), 0.0)

    ca, cb = {}, {}
    for k in range(-5, 2):
        ca[k], cb[k] = coefficients(plane(12, k), plane(13, k))

    def step(ex, ey, ez, hx, hy, hz, low, high):
        nhx = {k: hx[k] - 0.5 * (dyp(ez[k]) - (ey[k + 1] - ey[k])) for k in range(low - 1, high + 1)}
        nhy = {k: hy[k] - 0.5 * ((ex[k + 1] - ex[k]) - dxp(ez[k])) for k in range(low - 1, high + 1)}
        nhz = {k: hz[k] - 0.5 * (dxp(ey[k]) - dyp(ex[k])) for k in range(low, high + 1)}
        nex = {k: ca[k] * ex[k] + cb[k] * (dym(nhz[k]) - (nhy[k] - nhy[k - 1])) for k in range(low, high + 1)}
        ney = {k: ca[k] * ey[k] + cb[k] * ((nhx[k] - nhx[k - 1]) - dxm(nhz[k])) for k in range(low, high + 1)}
        nez = {k: ca[k] * ez[k] + cb[k] * (dxm(nhy[k]) - dym(nhx[k])) for k in range(low, high + 1)}
        return nex, ney, nez, nhx, nhy, nhz

    def arrays(first):
        return [
            {k: plane(m, k) for k in range(LOWEST[m], TOPMOST[m] + 1)} for m in range(first, first + 6)
        ]

    u1 = step(*arrays(0), -5, 1)
    u2 = step(*u1, -4, 0)
    rows = []
    for m in (0, 1, 3, 4):
        rows.append(u1[m][0] * math.cos(OMEGA) + u2[m][0] * math.cos(2 * OMEGA))
        rows.append(-u1[m][0] * math.sin(OMEGA) - u2[m][0] * math.sin(2 * OMEGA))
    dft = jnp.concatenate(rows, axis=0)

    nd = high_ref.shape[1] // 2
    cos_x, sin_x, weight = x_ref[:, :nd], x_ref[:, nd : 2 * nd], x_ref[:1, 2 * nd :]
    amp = 1.0 / math.sqrt(count_x * count_y * groups_z)
    prod = product(dft, high_ref, low_ref, 0)
    pattern = jnp.zeros((1, nd), jnp.float32)
    weight = (2.0 * amp) * weight
    mixing = []
    for c in range(4):
        re = prod[2 * c * count_x : (2 * c + 1) * count_x]
        im = prod[(2 * c + 1) * count_x : (2 * c + 2) * count_x]
        real = re[:, :nd] - im[:, nd:]
        imag = re[:, nd:] + im[:, :nd]
        far_re = amp * jnp.sum(real * cos_x - imag * sin_x, axis=0, keepdims=True)
        far_im = amp * jnp.sum(real * sin_x + imag * cos_x, axis=0, keepdims=True)
        pattern = pattern + far_re * far_re + far_im * far_im
        out_re, out_im = weight * far_re, weight * far_im
        b_re = out_re * cos_x + out_im * sin_x
        b_im = out_im * cos_x - out_re * sin_x
        mixing.append(jnp.concatenate([b_re, b_im], axis=1))
        mixing.append(jnp.concatenate([b_im, -b_re], axis=1))
    pattern_ref[...] = pattern

    src = product(jnp.concatenate(mixing, axis=0), high_ref, low_ref, 1)

    def with_sources(state, when):
        state = [dict(a) for a in state]
        for c, m in enumerate((0, 1, 3, 4)):
            gre = src[2 * c * count_x : (2 * c + 1) * count_x]
            gim = src[(2 * c + 1) * count_x : (2 * c + 2) * count_x]
            state[m][0] = state[m][0] + (gre * math.cos(OMEGA * when) - gim * math.sin(OMEGA * when))
        return state

    v1 = step(*with_sources(arrays(6), 2), -5, 0)
    v2 = step(*with_sources(v1, 1), -4, -1)
    sens = [
        sum(v1[m][k] * u2[m][k] for m in range(3)) + sum(v2[m][k] * u1[m][k] for m in range(3))
        for k in range(-4, 0)
    ]
    sens = jnp.concatenate(sens, axis=0)

    own = at[0]
    senders = groups_x * groups_y * groups_z
    total = senders * slots
    lists = groups_x * slots
    row, lane = (8, 2 * size_y) if half == BODY else (BODY, 0)
    pieces = range(-(-lists // (4 * size_y - lane)))

    def table(x):
        def piece(r):
            return jnp.concatenate(
                [pick(c, x * half + row + r, groups_x * groups_y, size_x * half)[:, lane:] for c in range(groups_z)], axis=0
            )

        return jnp.concatenate([piece(r) for r in pieces], axis=1)

    cell_tab, elem_tab = table(0), table(1)
    width = cell_tab.shape[1]
    at_lane = lax.broadcasted_iota(jnp.int32, (width, total), 0)
    slot = lax.broadcasted_iota(jnp.int32, (width, total), 1)
    spread_cell = (at_lane == own * slots + slot % slots).astype(jnp.float32).astype(jnp.bfloat16)
    spread_elem = (at_lane == slot % lists).astype(jnp.float32).astype(jnp.bfloat16)
    sender = lax.broadcasted_iota(jnp.int32, (senders, total), 0)
    slot = lax.broadcasted_iota(jnp.int32, (senders, total), 1)
    mine, owned = sender == slot // slots, sender == (slot // lists) * groups_x + own

    def spread(table, places, rows):
        moved = jnp.dot(table.astype(jnp.bfloat16), places, preferred_element_type=jnp.float32)
        return jnp.sum(jnp.where(rows, moved, 0.0), axis=0, keepdims=True)

    cell_tab = (cell_tab + 0.5).astype(jnp.int32)
    column = spread((cell_tab // size_z).astype(jnp.float32), spread_cell, mine)
    place_z = spread((cell_tab % size_z).astype(jnp.float32), spread_cell, mine)
    elems = spread(elem_tab, spread_elem, owned)
    column = (column + 0.5).astype(jnp.int32)
    place_z = (place_z + 0.5).astype(jnp.int32) - (zs - 4)
    elems = (elems + 1.5).astype(jnp.int32) - 1
    slot = lax.broadcasted_iota(jnp.int32, (1, total), 1)
    block = slot // lists
    place_x = (slot // slots % groups_x) * size_x + column // size_y
    place_y = column % size_y
    row_want = place_z * count_x + place_x
    lane_want = (block // groups_y) * count_y + (block % groups_y) * size_y + place_y
    hot_row = (lax.broadcasted_iota(jnp.int32, (4 * count_x, total), 0) == row_want).astype(jnp.float32)
    hot_row = hot_row.astype(jnp.bfloat16)
    hot_lane = lax.broadcasted_iota(jnp.int32, (lanes, total), 0) == lane_want
    picked = lax.dot_general(
        jnp.concatenate(halves(sens), axis=0), jnp.concatenate([hot_row, hot_row], axis=0),
        (((0,), (0,)), ((), ())), preferred_element_type=jnp.float32,
    )
    values = jnp.sum(jnp.where(hot_lane, picked, 0.0), axis=0, keepdims=True)
    hot_elem = (lax.broadcasted_iota(jnp.int32, (per_owner, total), 0) == elems).astype(jnp.float32)
    high = values.astype(jnp.bfloat16).astype(jnp.float32)
    both = jnp.where(lax.broadcasted_iota(jnp.int32, (8, total), 0) == 0, high, values - high)
    sums = lax.dot_general(
        both.astype(jnp.bfloat16), hot_elem.astype(jnp.bfloat16), (((1,), (1,)), ((), ())),
        preferred_element_type=jnp.float32,
    )
    sums = sums[:1] + sums[1:2]
    scale = 1.0 / math.sqrt(groups_x * groups_x * groups_y * groups_z * slots / NE)
    elem_ref[...] = sums * scale


def local(fields, adjoint, inv_eps, loss_level, direction, pattern_weight, voxel_cell, voxel_elem):
    size_x, size_y, size_z = inv_eps.shape
    groups_x, groups_y, groups_z = (lax.axis_size(a) for a in ("gx", "gy", "gz"))
    dims = (groups_x, groups_y, groups_z, size_x, size_y, size_z)
    slots = voxel_cell.shape[4]
    per_owner = NE // groups_x
    half = half_rows(groups_x * slots, size_y)
    nd = direction.shape[1]
    vmem = pl.BlockSpec(memory_space=pltpu.VMEM)
    hbm = pl.BlockSpec(memory_space=pltpu.HBM)

    def call(kernel, name, outs, *args, fetched=0, limit=48):
        scratch = [pltpu.VMEM(a.shape, a.dtype) for a in args[:fetched]]
        if fetched:
            scratch.append(pltpu.SemaphoreType.DMA((fetched,)))

        def located(*refs):
            kernel(dims, tuple(lax.axis_index(a) for a in ("gx", "gy", "gz")), *refs)

        return pl.pallas_call(
            located,
            out_shape=tuple(jax.ShapeDtypeStruct(o, jnp.float32) for o in outs),
            in_specs=[hbm] * fetched + [vmem] * (len(args) - fetched),
            out_specs=(vmem,) * len(outs),
            scratch_shapes=scratch,
            compiler_params=pltpu.CompilerParams(vmem_limit_bytes=limit * 1024 * 1024),
            name=name,
        )(*args)

    zrows = -(-(3 * HALO * size_x) // 8) * 8
    yrows = len(FORWARD) * size_x * HALO
    z_count, y_count = 1 if groups_z == 2 else 2, 1 if groups_y == 2 else 2
    send, *edges = call(
        first_kernel, "first",
        [(groups_x * groups_y, size_x * half, 4 * size_y)]
        + [(zrows, 4 * size_y)] * z_count + [(yrows, size_z)] * y_count,
        fields, adjoint, inv_eps, loss_level, voxel_cell.reshape(groups_x, slots),
        voxel_elem.reshape(groups_x, slots), fetched=6, limit=60,
    )
    z_top, z_bottom = edges[0], edges[z_count - 1]
    y_top, y_bottom = edges[z_count], edges[-1]
    z_low, z_high = neighbours("gz", z_top, z_bottom)
    z_sides = [z_low] if groups_z == 2 else [z_low, z_high]
    y_low, y_high = neighbours("gy", jnp.concatenate([y_top] + z_sides), jnp.concatenate([y_bottom] + z_sides))
    got = lax.all_to_all(send, ("gy", "gx"), split_axis=0, concat_axis=0, tiled=True)
    got = got.reshape(groups_x * groups_y * size_x * half, 4 * size_y)
    seen, _ = lax.optimization_barrier((direction, z_low))
    table_x, table_high, table_low = steering(
        groups_x * size_x, groups_y * size_y, groups_z, size_z, seen, pattern_weight
    )
    y_low, y_high, table_x, table_high, table_low = lax.optimization_barrier(
        (y_low, y_high, table_x, table_high, table_low)
    )

    rows = size_y + 8
    state, one, two = call(
        second_kernel, "second",
        [(8 * size_x + 2, rows, size_z + 128)] + [(5 * size_y + 24 + rows, size_z)] * 2,
        fields, inv_eps, loss_level, z_low, z_high, y_low, y_high,
    )
    one_side, other_side = (
        lax.ppermute(sent, "gx", [p for i in range(first, groups_x - 1, 2) for p in ((i, i + 1), (i + 1, i))])
        for first, sent in ((0, one), (1, two))
    )

    got, _ = lax.optimization_barrier((got, one))
    gots = [got] + [
        lax.ppermute(got, "gz", [(i, (i + s) % groups_z) for i in range(groups_z)]) for s in range(1, groups_z)
    ]

    pattern, elem = call(
        functools.partial(main_kernel, slots), "main", [(1, nd), (1, per_owner)],
        *gots, table_high, table_low, table_x,
    )
    state, pattern = lax.optimization_barrier((state, pattern))
    (fields_out,) = call(
        third_kernel, "third", [(6, size_x, size_y, size_z)], state, one_side, other_side
    )
    return (fields_out, pattern.reshape(nd), elem.reshape(per_owner))


def solution(mesh):
    in_specs = (
        P(None, ("groups", "gx"), "gy", "gz"),
        P(None, ("groups", "gx"), "gy", "gz"),
        P(("groups", "gx"), "gy", "gz"),
        P(("groups", "gx"), "gy", "gz"),
        P(),
        P(),
        P(("groups", "gx"), "gy", "gz", None, None),
        P(("groups", "gx"), "gy", "gz", None, None),
    )
    out_specs = (P(None, ("groups", "gx"), "gy", "gz"), P("groups"), P(("groups", "gx")))
    return jax.shard_map(local, mesh=mesh, in_specs=in_specs, out_specs=out_specs, check_vma=False)
```

```python
import functools
import math

import jax
import jax.numpy as jnp
from jax import lax
from jax.experimental import pallas as pl
from jax.experimental.pallas import tpu as pltpu
from jax.sharding import PartitionSpec as P

STEPS = 2
NE = 1024
OMEGA = 0.9
KAPPA = 0.37
HIGHEST = lax.Precision.HIGHEST
HALO = 2
COMPS = (0, 1, 3, 4)

SETS = ((0, 1, 2, 3), (4, 6, 7, 12), (5, 13, 8, 9), (10, 11))
STARTS = (0, 9, 17, 24)
BODY = 28
LOWEST = (-6, -6, -6, -6, -6, -5, -6, -6, -6, -6, -6, -6, -6, -5)
TOPMOST = (2, 2, 1, 1, 1, 1, 1, 1, 0, 0, 0, 0, 1, 1)
FORWARD = (0, 1, 2, 3, 4, 5, 12, 13)


def coefficients(inv_eps, level):
    level = 0.15 * level
    return ((1.0 - level) / (1.0 + level), 0.5 * inv_eps / (1.0 + level))


def place_of(m):
    for t, members in enumerate(SETS):
        if m in members:
            return t, members.index(m)


def slab_place(m, k):
    t, q = place_of(m)
    if t == 3:
        return STARTS[t] + (k - LOWEST[m]) % 4, q + 2 * ((k - LOWEST[m]) // 4)
    return STARTS[t] + k - LOWEST[m], q


def half_rows(lists, size_y):
    return BODY if lists <= 2 * size_y else BODY + 4


def neighbours(axis, top, bottom):
    count = lax.axis_size(axis)
    if count == 2:
        other = lax.ppermute(top, axis, [(0, 1), (1, 0)])
        return other, other
    forward = [(i, i + 1) for i in range(count - 1)]
    return lax.ppermute(top, axis, forward), lax.ppermute(bottom, axis, [(t, s) for s, t in forward])


def fetch(pairs, sems):
    copies = [pltpu.make_async_copy(src, dst, sems.at[i]) for i, (src, dst) in enumerate(pairs)]
    for copy in copies:
        copy.start()
    for copy in copies:
        copy.wait()


def first_kernel(dims, at, *refs):
    groups_x, groups_y, groups_z, size_x, size_y, size_z = dims
    borders = 1 if groups_z == 2 else 2, 1 if groups_y == 2 else 2
    sources, refs = refs[:6], refs[6:]
    send_ref, refs = refs[0], refs[1:]
    z_refs, y_refs, refs = refs[: borders[0]], refs[borders[0] : sum(borders)], refs[sum(borders) :]
    f_ref, a_ref, ie_ref, ll_ref, cell_ref, elem_ref, sems = refs
    fetch(list(zip(sources, refs[:6])), sems)

    def array(m, x):
        if m < 6:
            return f_ref[m, x]
        if m < 12:
            return a_ref[m - 6, x]
        return ie_ref[x] if m == 12 else ll_ref[x].astype(jnp.float32)

    def store(targets, index, top, bottom):
        if len(targets) == 1:
            targets[0][...] = jnp.where(index == 0, top, bottom)
        else:
            targets[0][...], targets[1][...] = top, bottom

    zs = size_z // 2 + 2
    lists, slots = cell_ref.shape
    half = half_rows(lists * slots, size_y)
    per_row = (2 if half == BODY else 4) * size_y // slots
    tops, bottoms = [], []
    for x in range(size_x):
        parts = []
        for t, members in enumerate(SETS):
            blocks = [array(m, x) for m in members]
            blocks += [jnp.zeros((size_y, size_z), jnp.float32)] * (4 - len(members))
            flipped = jnp.concatenate(blocks, axis=0).T
            if t < 2:
                parts.append(flipped[zs + LOWEST[members[0]] : zs + TOPMOST[members[0]] + 1])
            else:
                first, last = (-5, -6) if t == 2 else (-6, -2)
                count, last_lanes = (7, slice(2 * size_y, None)) if t == 2 else (4, slice(0, 2 * size_y))
                left = flipped[zs + first : zs + first + count, : 2 * size_y]
                parts.append(jnp.concatenate([left, flipped[zs + last : zs + last + count, last_lanes]], axis=1))
            if t < 3:
                tops.append(flipped[size_z - HALO :])
                bottoms.append(flipped[:HALO])
        if x < 2:
            table = (cell_ref, elem_ref)[x][...].astype(jnp.float32)
            lines = []
            for r in range(0, lists, per_row):
                line = [table[i : i + 1] for i in range(r, min(r + per_row, lists))]
                if len(line) < per_row:
                    line.append(jnp.zeros((1, (per_row - len(line)) * slots), jnp.float32))
                lines.append(jnp.concatenate(line, axis=1))
            if half == BODY:
                last = jnp.concatenate([parts[0][8:, : 2 * size_y], lines[0]], axis=1)
                parts[0] = jnp.concatenate([parts[0][:8], last], axis=0)
            else:
                lines.append(jnp.zeros((half - BODY - len(lines), 4 * size_y), jnp.float32))
                parts += lines
        rows = jnp.concatenate(parts, axis=0)
        for d in range(groups_x * groups_y):
            send_ref[d, x * half : (x + 1) * half] = rows
    pad = [jnp.zeros((z_refs[0].shape[0] - HALO * len(tops), 4 * size_y), jnp.float32)]
    store(z_refs, at[2], jnp.concatenate(tops + pad, axis=0), jnp.concatenate(bottoms + pad, axis=0))
    layers = [array(m, x) for m in FORWARD for x in range(size_x)]
    top = jnp.concatenate([a[size_y - HALO :] for a in layers], axis=0)
    store(y_refs, at[1], top, jnp.concatenate([a[:HALO] for a in layers], axis=0))


def wide_masks(dims, at):
    _, _, _, _, size_y, size_z = dims
    shape = (size_y + 8, size_z + 128)
    row = lax.broadcasted_iota(jnp.int32, shape, 0)
    lane = lax.broadcasted_iota(jnp.int32, shape, 1)
    out_y = jnp.logical_and(row >= size_y + 4, at[1] == 0)
    out_z = jnp.logical_and(lane >= size_z + 64, at[2] == 0)
    return jnp.where(jnp.logical_or(out_y, out_z), 0.0, 0.5)


def forward_y(a):
    return pltpu.roll(a, a.shape[0] - 1, 0) - a


def forward_z(a):
    return pltpu.roll(a, a.shape[1] - 1, 1) - a


def backward_y(a):
    return a - pltpu.roll(a, 1, 0)


def backward_z(a):
    return a - pltpu.roll(a, 1, 1)


def pack(planes, size_y, size_z):
    row = lax.broadcasted_iota(jnp.int32, (8, size_z), 0)
    own = jnp.logical_or(row < 2, row >= 6)
    lane = lax.broadcasted_iota(jnp.int32, (planes[0].shape[0], 128), 1)
    out = [plane[:size_y, :size_z] for plane in planes]
    for p in range(0, len(planes), 2):
        tile = planes[p][size_y:, :size_z]
        if p + 1 < len(planes):
            tile = jnp.where(own, tile, pltpu.roll(planes[p + 1][size_y:, :size_z], 4, 0))
        out.append(tile)
    border = jnp.zeros((planes[0].shape[0], 128), jnp.float32)
    for p, plane in enumerate(planes):
        moved = pltpu.roll(plane[:, size_z:], 8 * p + 2, 1)
        border = jnp.where(jnp.logical_and(lane >= 8 * p, lane < 8 * p + 4), moved, border)
    return jnp.concatenate(out + [border], axis=0)


def unpack(rows, count, size_y):
    tiles = count * size_y
    border = rows[tiles + 8 * ((count + 1) // 2) :]
    out = []
    for p in range(count):
        tile = rows[tiles + 8 * (p // 2) : tiles + 8 * (p // 2) + 8]
        body = jnp.concatenate(
            [rows[p * size_y : (p + 1) * size_y], pltpu.roll(tile, 4, 0) if p % 2 else tile], axis=0
        )
        out.append(jnp.concatenate([body, pltpu.roll(border, 128 - (8 * p + 2), 1)], axis=1))
    return out


def second_kernel(dims, at, f_ref, ie_ref, ll_ref, zl_ref, zh_ref, yl_ref, yh_ref, state_ref, one_ref, two_ref):
    groups_x, groups_y, groups_z, size_x, size_y, size_z = dims
    zrows = zl_ref.shape[0]
    lane = lax.broadcasted_iota(jnp.int32, (8, 128), 1)
    high_lane = jnp.logical_and(lane < HALO, at[2] < groups_z - 1)
    low_lane = jnp.logical_and(lane >= 128 - HALO, at[2] > 0)
    y_high = (at[1] < groups_y - 1).astype(jnp.float32)
    y_low = (at[1] > 0).astype(jnp.float32)

    def flip(a):
        return jnp.concatenate([a, jnp.zeros((128 - zrows, a.shape[1]), jnp.float32)], axis=0).T

    own_low, own_high = flip(zl_ref[...]), flip(zh_ref[...])
    edge = HALO * size_x * len(FORWARD)
    after = edge if groups_z == 2 else edge + zrows
    yl_low, yl_high = flip(yl_ref[edge : edge + zrows]), flip(yl_ref[after : after + zrows])
    yh_low, yh_high = flip(yh_ref[edge : edge + zrows]), flip(yh_ref[after : after + zrows])

    def column(low, high, rows, at):
        reps = rows // 8
        hl = jnp.concatenate([high_lane] * reps, axis=0)
        ll = jnp.concatenate([low_lane] * reps, axis=0)
        moved_high = pltpu.roll(high, (128 - at) % 128, 1)
        moved_low = pltpu.roll(low, (128 - HALO - at) % 128, 1)
        return jnp.where(hl, moved_high, jnp.where(ll, moved_low, 0.0))

    def wide(m, x):
        t, q = place_of(m)
        at = (x * 3 + t) * HALO
        if m < 6:
            body = f_ref[m, x]
        else:
            body = ie_ref[x] if m == 12 else ll_ref[x].astype(jnp.float32)
        rows = slice(q * size_y, (q + 1) * size_y)
        body_z = column(own_low[rows], own_high[rows], size_y, at)
        start = (FORWARD.index(m) * size_x + x) * HALO
        blank = jnp.zeros((8 - 2 * HALO, 128), jnp.float32)
        first, last = q * size_y, (q + 1) * size_y
        tile = jnp.concatenate(
            [yh_ref[start : start + HALO] * y_high, blank, yl_ref[start : start + HALO] * y_low], axis=0
        )
        low = jnp.concatenate(
            [yh_low[first : first + HALO] * y_high, blank, yl_low[last - HALO : last] * y_low], axis=0
        )
        high = jnp.concatenate(
            [yh_high[first : first + HALO] * y_high, blank, yl_high[last - HALO : last] * y_low], axis=0
        )
        corner = column(low, high, 8, at)
        return jnp.concatenate(
            [jnp.concatenate([body, body_z], axis=1), jnp.concatenate([tile, corner], axis=1)], axis=0
        )

    half = wide_masks(dims, at)
    xs = range(size_x)
    ex, ey, ez, hx, hy, hz, ie, lv = ([wide(m, x) for x in xs] for m in FORWARD)
    pairs = [coefficients(ie[x], lv[x]) for x in xs]
    ca, cb = [p[0] for p in pairs], [p[1] for p in pairs]
    nothing = jnp.zeros_like(half)
    hx = [hx[x] - half * (forward_y(ez[x]) - forward_z(ey[x])) for x in xs]
    hy = [hy[x] - half * (forward_z(ex[x]) - ((ez[x + 1] if x + 1 < size_x else nothing) - ez[x])) for x in xs]
    hz = [hz[x] - half * (((ey[x + 1] if x + 1 < size_x else nothing) - ey[x]) - forward_y(ex[x])) for x in xs]
    first_ey, first_ez = ey[0], ez[0]
    ex = [ca[x] * ex[x] + cb[x] * (backward_y(hz[x]) - backward_z(hy[x])) for x in xs]
    ey = [ca[x] * ey[x] + cb[x] * (backward_z(hx[x]) - (hz[x] - (hz[x - 1] if x else nothing))) for x in xs]
    ez = [ca[x] * ez[x] + cb[x] * ((hy[x] - (hy[x - 1] if x else nothing)) - backward_y(hx[x])) for x in xs]
    state = [*ex, *ey, *ez, *hx, *hy, *hz, *ca, *cb, first_ey, first_ez]
    for i, a in enumerate(state):
        state_ref[i] = a
    next_hy = hy[-1] - half * (forward_z(ex[-1]) + ez[-1])
    next_hz = hz[-1] + half * (ey[-1] + forward_y(ex[-1]))
    up = pack([hy[-1], hz[-1], next_hy, next_hz, cb[-1]], size_y, size_z)
    down = pack([first_ey, first_ez, ey[0], ez[0], cb[0]], size_y, size_z)
    even = lax.rem(at[0], 2) == 0
    one_ref[...] = jnp.where(even, up, down)
    two_ref[...] = jnp.where(even, down, up)


def third_kernel(dims, at, state_ref, one_ref, two_ref, out_ref):
    groups_x, groups_y, groups_z, size_x, size_y, size_z = dims
    xs = range(size_x)
    half = wide_masks(dims, at)
    half_low = half * (at[0] > 0).astype(jnp.float32)
    state = [[state_ref[i * size_x + x] for x in xs] for i in range(8)]
    ex, ey, ez, hx, hy, hz, ca, cb = state
    first_ey, first_ez = state_ref[8 * size_x], state_ref[8 * size_x + 1]
    even = lax.rem(at[0], 2) == 0
    one, two = one_ref[...], two_ref[...]
    low_hy, low_hz, below_hy, below_hz, low_cb = unpack(jnp.where(even, two, one), 5, size_y)
    next_ey, next_ez, high_ey, high_ez, high_cb = unpack(jnp.where(even, one, two), 5, size_y)
    add_y, add_z = half * next_ez, -(half * next_ey)
    hy[-1], hz[-1] = hy[-1] + add_y, hz[-1] + add_z
    ex[-1] = ex[-1] + cb[-1] * (backward_y(add_z) - backward_z(add_y))
    ey[-1] = ey[-1] - cb[-1] * add_z
    ez[-1] = ez[-1] + cb[-1] * add_y
    add_y, add_z = half_low * first_ez, -(half_low * first_ey)
    low_hy, low_hz = low_hy + add_y, low_hz + add_z
    more_ex = low_cb * (backward_y(add_z) - backward_z(add_y))
    more_ey, more_ez = -(low_cb * add_z), low_cb * add_y
    ey[0] = ey[0] + cb[0] * low_hz
    ez[0] = ez[0] - cb[0] * low_hy
    high_ey = high_ey + high_cb * hz[-1]
    high_ez = high_ez - high_cb * hy[-1]
    low_hy = below_hy + add_y - half_low * (forward_z(more_ex) + more_ez - ez[0])
    low_hz = below_hz + add_z + half_low * (more_ey + forward_y(more_ex) - ey[0])
    after_ey, after_ez = ey[1:] + [high_ey], ez[1:] + [high_ez]
    hx = [hx[x] - half * (forward_y(ez[x]) - forward_z(ey[x])) for x in xs]
    hy = [hy[x] - half * (forward_z(ex[x]) - (after_ez[x] - ez[x])) for x in xs]
    hz = [hz[x] - half * ((after_ey[x] - ey[x]) - forward_y(ex[x])) for x in xs]
    before_hy, before_hz = [low_hy] + hy[:-1], [low_hz] + hz[:-1]
    for x in xs:
        new = (
            ca[x] * ex[x] + cb[x] * (backward_y(hz[x]) - backward_z(hy[x])),
            ca[x] * ey[x] + cb[x] * (backward_z(hx[x]) - (hz[x] - before_hz[x])),
            ca[x] * ez[x] + cb[x] * ((hy[x] - before_hy[x]) - backward_y(hx[x])),
            hx[x], hy[x], hz[x],
        )
        for m in range(6):
            out_ref[m, x] = new[m][:size_y, :size_z]


def halves_of_table(a):
    high = lax.reduce_precision(a, 8, 7)
    return high.astype(jnp.bfloat16), (a - high).astype(jnp.bfloat16)


def halves(a):
    high = a.astype(jnp.bfloat16)
    return high, (a - high.astype(jnp.float32)).astype(jnp.bfloat16)


def product(a, high_ref, low_ref, contract):
    high, low = halves(a)
    dims = (((1,), (contract,)), ((), ()))
    both = lax.dot_general(
        jnp.concatenate([high, low], axis=0), high_ref[...], dims, preferred_element_type=jnp.float32
    )
    rest = lax.dot_general(high, low_ref[...], dims, preferred_element_type=jnp.float32)
    return both[: a.shape[0]] + (both[a.shape[0] :] + rest)


def steering(count_x, count_y, groups_z, size_z, direction, weight):
    zs = size_z // 2 + 2
    xs = jnp.arange(count_x, dtype=jnp.float32)[:, None]
    ys = jnp.arange(count_y, dtype=jnp.float32)[None, :, None]
    zval = (jnp.arange(groups_z, dtype=jnp.float32) * size_z + zs)[:, None, None]
    phase_x = KAPPA * xs * direction[0]
    phase_yz = (KAPPA * (ys * direction[1] + zval * direction[2])).reshape(groups_z * count_y, -1)
    return (
        jnp.concatenate([jnp.cos(phase_x), jnp.sin(phase_x), jnp.broadcast_to(weight, phase_x.shape)], axis=1),
        *halves_of_table(jnp.concatenate([jnp.cos(phase_yz), jnp.sin(phase_yz)], axis=1)),
    )


def main_kernel(slots, dims, at, *refs):
    groups_x, groups_y, groups_z, size_x, size_y, size_z = dims
    got_refs = refs[:groups_z]
    high_ref, low_ref, x_ref, pattern_ref, elem_ref = refs[groups_z:]
    per_owner = NE // groups_x
    half = half_rows(groups_x * slots, size_y)
    count_x, count_y = groups_x * size_x, groups_y * size_y
    lanes = groups_z * count_y
    zs = size_z // 2 + 2

    def pick(c, start, size, stride):
        out = None
        for s, ref in enumerate(got_refs):
            part = ref[pl.ds(start, size, stride=stride), :]
            here = lax.rem(at[2] - s + groups_z, groups_z) == c
            out = part if out is None else jnp.where(here, part, out)
        return out

    loaded = {}

    def plane(m, k):
        row, q = slab_place(m, k)
        if row not in loaded:
            loaded[row] = [
                pick(c, b * groups_x * size_x * half + row, count_x, half)
                for c in range(groups_z)
                for b in range(groups_y)
            ]
        return jnp.concatenate([p[:, q * size_y : (q + 1) * size_y] for p in loaded[row]], axis=1)

    row_id = lax.broadcasted_iota(jnp.int32, (count_x, lanes), 0)
    lane_id = lax.broadcasted_iota(jnp.int32, (count_x, lanes), 1) % count_y
    x_up, x_low = row_id < count_x - 1, row_id > 0
    y_up, y_low = lane_id < count_y - 1, lane_id > 0

    def dxp(a):
        return jnp.where(x_up, pltpu.roll(a, count_x - 1, 0), 0.0) - a

    def dyp(a):
        return jnp.where(y_up, pltpu.roll(a, lanes - 1, 1), 0.0) - a

    def dxm(a):
        return a - jnp.where(x_low, pltpu.roll(a, 1, 0), 0.0)

    def dym(a):
        return a - jnp.where(y_low, pltpu.roll(a, 1, 1), 0.0)

    ca, cb = {}, {}
    for k in range(-5, 2):
        ca[k], cb[k] = coefficients(plane(12, k), plane(13, k))

    def step(ex, ey, ez, hx, hy, hz, low, high):
        nhx = {k: hx[k] - 0.5 * (dyp(ez[k]) - (ey[k + 1] - ey[k])) for k in range(low - 1, high + 1)}
        nhy = {k: hy[k] - 0.5 * ((ex[k + 1] - ex[k]) - dxp(ez[k])) for k in range(low - 1, high + 1)}
        nhz = {k: hz[k] - 0.5 * (dxp(ey[k]) - dyp(ex[k])) for k in range(low, high + 1)}
        nex = {k: ca[k] * ex[k] + cb[k] * (dym(nhz[k]) - (nhy[k] - nhy[k - 1])) for k in range(low, high + 1)}
        ney = {k: ca[k] * ey[k] + cb[k] * ((nhx[k] - nhx[k - 1]) - dxm(nhz[k])) for k in range(low, high + 1)}
        nez = {k: ca[k] * ez[k] + cb[k] * (dxm(nhy[k]) - dym(nhx[k])) for k in range(low, high + 1)}
        return nex, ney, nez, nhx, nhy, nhz

    def arrays(first):
        return [
            {k: plane(m, k) for k in range(LOWEST[m], TOPMOST[m] + 1)} for m in range(first, first + 6)
        ]

    u1 = step(*arrays(0), -5, 1)
    u2 = step(*u1, -4, 0)
    rows = []
    for m in (0, 1, 3, 4):
        rows.append(u1[m][0] * math.cos(OMEGA) + u2[m][0] * math.cos(2 * OMEGA))
        rows.append(-u1[m][0] * math.sin(OMEGA) - u2[m][0] * math.sin(2 * OMEGA))
    dft = jnp.concatenate(rows, axis=0)

    nd = high_ref.shape[1] // 2
    cos_x, sin_x, weight = x_ref[:, :nd], x_ref[:, nd : 2 * nd], x_ref[:1, 2 * nd :]
    amp = 1.0 / math.sqrt(count_x * count_y * groups_z)
    prod = product(dft, high_ref, low_ref, 0)
    pattern = jnp.zeros((1, nd), jnp.float32)
    weight = (2.0 * amp) * weight
    mixing = []
    for c in range(4):
        re = prod[2 * c * count_x : (2 * c + 1) * count_x]
        im = prod[(2 * c + 1) * count_x : (2 * c + 2) * count_x]
        real = re[:, :nd] - im[:, nd:]
        imag = re[:, nd:] + im[:, :nd]
        far_re = amp * jnp.sum(real * cos_x - imag * sin_x, axis=0, keepdims=True)
        far_im = amp * jnp.sum(real * sin_x + imag * cos_x, axis=0, keepdims=True)
        pattern = pattern + far_re * far_re + far_im * far_im
        out_re, out_im = weight * far_re, weight * far_im
        b_re = out_re * cos_x + out_im * sin_x
        b_im = out_im * cos_x - out_re * sin_x
        mixing.append(jnp.concatenate([b_re, b_im], axis=1))
        mixing.append(jnp.concatenate([b_im, -b_re], axis=1))
    pattern_ref[...] = pattern

    src = product(jnp.concatenate(mixing, axis=0), high_ref, low_ref, 1)

    def with_sources(state, when):
        state = [dict(a) for a in state]
        for c, m in enumerate((0, 1, 3, 4)):
            gre = src[2 * c * count_x : (2 * c + 1) * count_x]
            gim = src[(2 * c + 1) * count_x : (2 * c + 2) * count_x]
            state[m][0] = state[m][0] + (gre * math.cos(OMEGA * when) - gim * math.sin(OMEGA * when))
        return state

    v1 = step(*with_sources(arrays(6), 2), -5, 0)
    v2 = step(*with_sources(v1, 1), -4, -1)
    sens = [
        sum(v1[m][k] * u2[m][k] for m in range(3)) + sum(v2[m][k] * u1[m][k] for m in range(3))
        for k in range(-4, 0)
    ]
    sens = jnp.concatenate(sens, axis=0)

    own = at[0]
    senders = groups_x * groups_y * groups_z
    total = senders * slots
    lists = groups_x * slots
    row, lane = (8, 2 * size_y) if half == BODY else (BODY, 0)
    pieces = range(-(-lists // (4 * size_y - lane)))

    def table(x):
        def piece(r):
            return jnp.concatenate(
                [pick(c, x * half + row + r, groups_x * groups_y, size_x * half)[:, lane:] for c in range(groups_z)], axis=0
            )

        return jnp.concatenate([piece(r) for r in pieces], axis=1)

    cell_tab, elem_tab = table(0), table(1)
    width = cell_tab.shape[1]
    at_lane = lax.broadcasted_iota(jnp.int32, (width, total), 0)
    slot = lax.broadcasted_iota(jnp.int32, (width, total), 1)
    spread_cell = (at_lane == own * slots + slot % slots).astype(jnp.float32).astype(jnp.bfloat16)
    spread_elem = (at_lane == slot % lists).astype(jnp.float32).astype(jnp.bfloat16)
    sender = lax.broadcasted_iota(jnp.int32, (senders, total), 0)
    slot = lax.broadcasted_iota(jnp.int32, (senders, total), 1)
    mine, owned = sender == slot // slots, sender == (slot // lists) * groups_x + own

    def spread(table, places, rows):
        moved = jnp.dot(table.astype(jnp.bfloat16), places, preferred_element_type=jnp.float32)
        return jnp.sum(jnp.where(rows, moved, 0.0), axis=0, keepdims=True)

    cell_tab = (cell_tab + 0.5).astype(jnp.int32)
    column = spread((cell_tab // size_z).astype(jnp.float32), spread_cell, mine)
    place_z = spread((cell_tab % size_z).astype(jnp.float32), spread_cell, mine)
    elems = spread(elem_tab, spread_elem, owned)
    column = (column + 0.5).astype(jnp.int32)
    place_z = (place_z + 0.5).astype(jnp.int32) - (zs - 4)
    elems = (elems + 1.5).astype(jnp.int32) - 1
    slot = lax.broadcasted_iota(jnp.int32, (1, total), 1)
    block = slot // lists
    place_x = (slot // slots % groups_x) * size_x + column // size_y
    place_y = column % size_y
    row_want = place_z * count_x + place_x
    lane_want = (block // groups_y) * count_y + (block % groups_y) * size_y + place_y
    hot_row = (lax.broadcasted_iota(jnp.int32, (4 * count_x, total), 0) == row_want).astype(jnp.float32)
    hot_row = hot_row.astype(jnp.bfloat16)
    hot_lane = lax.broadcasted_iota(jnp.int32, (lanes, total), 0) == lane_want
    picked = lax.dot_general(
        jnp.concatenate(halves(sens), axis=0), jnp.concatenate([hot_row, hot_row], axis=0),
        (((0,), (0,)), ((), ())), preferred_element_type=jnp.float32,
    )
    values = jnp.sum(jnp.where(hot_lane, picked, 0.0), axis=0, keepdims=True)
    hot_elem = (lax.broadcasted_iota(jnp.int32, (per_owner, total), 0) == elems).astype(jnp.float32)
    high = values.astype(jnp.bfloat16).astype(jnp.float32)
    both = jnp.where(lax.broadcasted_iota(jnp.int32, (8, total), 0) == 0, high, values - high)
    sums = lax.dot_general(
        both.astype(jnp.bfloat16), hot_elem.astype(jnp.bfloat16), (((1,), (1,)), ((), ())),
        preferred_element_type=jnp.float32,
    )
    sums = sums[:1] + sums[1:2]
    scale = 1.0 / math.sqrt(groups_x * groups_x * groups_y * groups_z * slots / NE)
    elem_ref[...] = sums * scale


def local(fields, adjoint, inv_eps, loss_level, direction, pattern_weight, voxel_cell, voxel_elem):
    size_x, size_y, size_z = inv_eps.shape
    groups_x, groups_y, groups_z = (lax.axis_size(a) for a in ("gx", "gy", "gz"))
    dims = (groups_x, groups_y, groups_z, size_x, size_y, size_z)
    slots = voxel_cell.shape[4]
    per_owner = NE // groups_x
    half = half_rows(groups_x * slots, size_y)
    nd = direction.shape[1]
    vmem = pl.BlockSpec(memory_space=pltpu.VMEM)
    hbm = pl.BlockSpec(memory_space=pltpu.HBM)

    def call(kernel, name, outs, *args, fetched=0, limit=48):
        scratch = [pltpu.VMEM(a.shape, a.dtype) for a in args[:fetched]]
        args = [
            pltpu.with_memory_space_constraint(a, pltpu.HBM) if i < fetched else a for i, a in enumerate(args)
        ]
        if fetched:
            scratch.append(pltpu.SemaphoreType.DMA((fetched,)))

        def located(*refs):
            kernel(dims, tuple(lax.axis_index(a) for a in ("gx", "gy", "gz")), *refs)

        return pl.pallas_call(
            located,
            out_shape=tuple(jax.ShapeDtypeStruct(o, jnp.float32) for o in outs),
            in_specs=[hbm] * fetched + [vmem] * (len(args) - fetched),
            out_specs=(vmem,) * len(outs),
            scratch_shapes=scratch,
            compiler_params=pltpu.CompilerParams(vmem_limit_bytes=limit * 1024 * 1024),
            name=name,
        )(*args)

    zrows = -(-(3 * HALO * size_x) // 8) * 8
    yrows = len(FORWARD) * size_x * HALO
    z_count, y_count = 1 if groups_z == 2 else 2, 1 if groups_y == 2 else 2
    send, *edges = call(
        first_kernel, "first",
        [(groups_x * groups_y, size_x * half, 4 * size_y)]
        + [(zrows, 4 * size_y)] * z_count + [(yrows, size_z)] * y_count,
        fields, adjoint, inv_eps, loss_level, voxel_cell.reshape(groups_x, slots),
        voxel_elem.reshape(groups_x, slots), fetched=6, limit=16,
    )
    z_top, z_bottom = edges[0], edges[z_count - 1]
    y_top, y_bottom = edges[z_count], edges[-1]
    z_low, z_high = neighbours("gz", z_top, z_bottom)
    z_sides = [z_low] if groups_z == 2 else [z_low, z_high]
    y_low, y_high = neighbours("gy", jnp.concatenate([y_top] + z_sides), jnp.concatenate([y_bottom] + z_sides))
    got = lax.all_to_all(send, ("gy", "gx"), split_axis=0, concat_axis=0, tiled=True)
    got = got.reshape(groups_x * groups_y * size_x * half, 4 * size_y)
    rows = size_y + 8
    state, one, two = call(
        second_kernel, "second",
        [(8 * size_x + 2, rows, size_z + 128)] + [(5 * size_y + 24 + rows, size_z)] * 2,
        fields, inv_eps, loss_level, z_low, z_high, y_low, y_high,
    )
    seen, seen_weight, _ = lax.optimization_barrier((direction, pattern_weight, one))
    table_x, table_high, table_low = steering(
        groups_x * size_x, groups_y * size_y, groups_z, size_z, seen, seen_weight
    )

    one_side, other_side = (
        lax.ppermute(sent, "gx", [p for i in range(first, groups_x - 1, 2) for p in ((i, i + 1), (i + 1, i))])
        for first, sent in ((0, one), (1, two))
    )

    got, _ = lax.optimization_barrier((got, one))
    gots = [got] + [
        lax.ppermute(got, "gz", [(i, (i + s) % groups_z) for i in range(groups_z)]) for s in range(1, groups_z)
    ]

    pattern, elem = call(
        functools.partial(main_kernel, slots), "main", [(1, nd), (1, per_owner)],
        *gots, table_high, table_low, table_x,
    )
    state, pattern = lax.optimization_barrier((state, pattern))
    (fields_out,) = call(
        third_kernel, "third", [(6, size_x, size_y, size_z)], state, one_side, other_side
    )
    return (fields_out, pattern.reshape(nd), elem.reshape(per_owner))


def solution(mesh):
    in_specs = (
        P(None, ("groups", "gx"), "gy", "gz"),
        P(None, ("groups", "gx"), "gy", "gz"),
        P(("groups", "gx"), "gy", "gz"),
        P(("groups", "gx"), "gy", "gz"),
        P(),
        P(),
        P(("groups", "gx"), "gy", "gz", None, None),
        P(("groups", "gx"), "gy", "gz", None, None),
    )
    out_specs = (P(None, ("groups", "gx"), "gy", "gz"), P("groups"), P(("groups", "gx")))
    return jax.shard_map(local, mesh=mesh, in_specs=in_specs, out_specs=out_specs, check_vma=False)
```

```python
import functools
import math

import jax
import jax.numpy as jnp
from jax import lax
from jax.experimental import pallas as pl
from jax.experimental.pallas import tpu as pltpu
from jax.sharding import PartitionSpec as P

STEPS = 2
NE = 1024
OMEGA = 0.9
KAPPA = 0.37
HIGHEST = lax.Precision.HIGHEST
HALO = 2
COMPS = (0, 1, 3, 4)

SETS = ((0, 1, 2, 3), (4, 6, 7, 12), (5, 13, 8, 9), (10, 11))
STARTS = (0, 9, 17, 24)
BODY = 28
LOWEST = (-6, -6, -6, -6, -6, -5, -6, -6, -6, -6, -6, -6, -6, -5)
TOPMOST = (2, 2, 1, 1, 1, 1, 1, 1, 0, 0, 0, 0, 1, 1)
FORWARD = (0, 1, 2, 3, 4, 5, 12, 13)


def coefficients(inv_eps, level):
    level = 0.15 * level
    return ((1.0 - level) / (1.0 + level), 0.5 * inv_eps / (1.0 + level))


def place_of(m):
    for t, members in enumerate(SETS):
        if m in members:
            return t, members.index(m)


def slab_place(m, k):
    t, q = place_of(m)
    if t == 3:
        return STARTS[t] + (k - LOWEST[m]) % 4, q + 2 * ((k - LOWEST[m]) // 4)
    return STARTS[t] + k - LOWEST[m], q


def half_rows(lists, size_y):
    return BODY if lists <= 2 * size_y else BODY + 4


def neighbours(axis, top, bottom):
    count = lax.axis_size(axis)
    if count == 2:
        other = lax.ppermute(top, axis, [(0, 1), (1, 0)])
        return other, other
    forward = [(i, i + 1) for i in range(count - 1)]
    return lax.ppermute(top, axis, forward), lax.ppermute(bottom, axis, [(t, s) for s, t in forward])


def fetch(pairs, sems):
    copies = [pltpu.make_async_copy(src, dst, sems.at[i]) for i, (src, dst) in enumerate(pairs)]
    for copy in copies:
        copy.start()
    for copy in copies:
        copy.wait()


def first_kernel(dims, at, *refs):
    groups_x, groups_y, groups_z, size_x, size_y, size_z = dims
    borders = 1 if groups_z == 2 else 2, 1 if groups_y == 2 else 2
    sources, refs = refs[:6], refs[6:]
    send_ref, refs = refs[0], refs[1:]
    z_refs, y_refs, refs = refs[: borders[0]], refs[borders[0] : sum(borders)], refs[sum(borders) :]
    f_ref, a_ref, ie_ref, ll_ref, cell_ref, elem_ref, sems = refs
    fetch(list(zip(sources, refs[:6])), sems)

    def array(m, x):
        if m < 6:
            return f_ref[m, x]
        if m < 12:
            return a_ref[m - 6, x]
        return ie_ref[x] if m == 12 else ll_ref[x].astype(jnp.float32)

    def store(targets, index, top, bottom):
        if len(targets) == 1:
            targets[0][...] = jnp.where(index == 0, top, bottom)
        else:
            targets[0][...], targets[1][...] = top, bottom

    zs = size_z // 2 + 2
    lists, slots = cell_ref.shape
    half = half_rows(lists * slots, size_y)
    per_row = (2 if half == BODY else 4) * size_y // slots
    tops, bottoms = [], []
    for x in range(size_x):
        parts = []
        for t, members in enumerate(SETS):
            blocks = [array(m, x) for m in members]
            blocks += [jnp.zeros((size_y, size_z), jnp.float32)] * (4 - len(members))
            flipped = jnp.concatenate(blocks, axis=0).T
            if t < 2:
                parts.append(flipped[zs + LOWEST[members[0]] : zs + TOPMOST[members[0]] + 1])
            else:
                first, last = (-5, -6) if t == 2 else (-6, -2)
                count, last_lanes = (7, slice(2 * size_y, None)) if t == 2 else (4, slice(0, 2 * size_y))
                left = flipped[zs + first : zs + first + count, : 2 * size_y]
                parts.append(jnp.concatenate([left, flipped[zs + last : zs + last + count, last_lanes]], axis=1))
            if t < 3:
                tops.append(flipped[size_z - HALO :])
                bottoms.append(flipped[:HALO])
        if x < 2:
            table = (cell_ref, elem_ref)[x][...].astype(jnp.float32)
            lines = []
            for r in range(0, lists, per_row):
                line = [table[i : i + 1] for i in range(r, min(r + per_row, lists))]
                if len(line) < per_row:
                    line.append(jnp.zeros((1, (per_row - len(line)) * slots), jnp.float32))
                lines.append(jnp.concatenate(line, axis=1))
            if half == BODY:
                last = jnp.concatenate([parts[0][8:, : 2 * size_y], lines[0]], axis=1)
                parts[0] = jnp.concatenate([parts[0][:8], last], axis=0)
            else:
                lines.append(jnp.zeros((half - BODY - len(lines), 4 * size_y), jnp.float32))
                parts += lines
        rows = jnp.concatenate(parts, axis=0)
        for d in range(groups_x * groups_y):
            send_ref[d, x * half : (x + 1) * half] = rows
    pad = [jnp.zeros((z_refs[0].shape[0] - HALO * len(tops), 4 * size_y), jnp.float32)]
    store(z_refs, at[2], jnp.concatenate(tops + pad, axis=0), jnp.concatenate(bottoms + pad, axis=0))
    layers = [array(m, x) for m in FORWARD for x in range(size_x)]
    top = jnp.concatenate([a[size_y - HALO :] for a in layers], axis=0)
    store(y_refs, at[1], top, jnp.concatenate([a[:HALO] for a in layers], axis=0))


def wide_masks(dims, at):
    _, _, _, _, size_y, size_z = dims
    shape = (size_y + 8, size_z + 128)
    row = lax.broadcasted_iota(jnp.int32, shape, 0)
    lane = lax.broadcasted_iota(jnp.int32, shape, 1)
    out_y = jnp.logical_and(row >= size_y + 4, at[1] == 0)
    out_z = jnp.logical_and(lane >= size_z + 64, at[2] == 0)
    return jnp.where(jnp.logical_or(out_y, out_z), 0.0, 0.5)


def forward_y(a):
    return pltpu.roll(a, a.shape[0] - 1, 0) - a


def forward_z(a):
    return pltpu.roll(a, a.shape[1] - 1, 1) - a


def backward_y(a):
    return a - pltpu.roll(a, 1, 0)


def backward_z(a):
    return a - pltpu.roll(a, 1, 1)


def pack(planes, size_y, size_z):
    row = lax.broadcasted_iota(jnp.int32, (8, size_z), 0)
    own = jnp.logical_or(row < 2, row >= 6)
    lane = lax.broadcasted_iota(jnp.int32, (planes[0].shape[0], 128), 1)
    out = [plane[:size_y, :size_z] for plane in planes]
    for p in range(0, len(planes), 2):
        tile = planes[p][size_y:, :size_z]
        if p + 1 < len(planes):
            tile = jnp.where(own, tile, pltpu.roll(planes[p + 1][size_y:, :size_z], 4, 0))
        out.append(tile)
    border = jnp.zeros((planes[0].shape[0], 128), jnp.float32)
    for p, plane in enumerate(planes):
        moved = pltpu.roll(plane[:, size_z:], 8 * p + 2, 1)
        border = jnp.where(jnp.logical_and(lane >= 8 * p, lane < 8 * p + 4), moved, border)
    return jnp.concatenate(out + [border], axis=0)


def unpack(rows, count, size_y):
    tiles = count * size_y
    border = rows[tiles + 8 * ((count + 1) // 2) :]
    out = []
    for p in range(count):
        tile = rows[tiles + 8 * (p // 2) : tiles + 8 * (p // 2) + 8]
        body = jnp.concatenate(
            [rows[p * size_y : (p + 1) * size_y], pltpu.roll(tile, 4, 0) if p % 2 else tile], axis=0
        )
        out.append(jnp.concatenate([body, pltpu.roll(border, 128 - (8 * p + 2), 1)], axis=1))
    return out


def second_kernel(dims, at, f_ref, ie_ref, ll_ref, zl_ref, zh_ref, yl_ref, yh_ref, state_ref, one_ref, two_ref):
    groups_x, groups_y, groups_z, size_x, size_y, size_z = dims
    zrows = zl_ref.shape[0]
    lane = lax.broadcasted_iota(jnp.int32, (8, 128), 1)
    high_lane = jnp.logical_and(lane < HALO, at[2] < groups_z - 1)
    low_lane = jnp.logical_and(lane >= 128 - HALO, at[2] > 0)
    y_high = (at[1] < groups_y - 1).astype(jnp.float32)
    y_low = (at[1] > 0).astype(jnp.float32)

    def flip(a):
        return jnp.concatenate([a, jnp.zeros((128 - zrows, a.shape[1]), jnp.float32)], axis=0).T

    own_low, own_high = flip(zl_ref[...]), flip(zh_ref[...])
    edge = HALO * size_x * len(FORWARD)
    after = edge if groups_z == 2 else edge + zrows
    yl_low, yl_high = flip(yl_ref[edge : edge + zrows]), flip(yl_ref[after : after + zrows])
    yh_low, yh_high = flip(yh_ref[edge : edge + zrows]), flip(yh_ref[after : after + zrows])

    def column(low, high, rows, at):
        reps = rows // 8
        hl = jnp.concatenate([high_lane] * reps, axis=0)
        ll = jnp.concatenate([low_lane] * reps, axis=0)
        moved_high = pltpu.roll(high, (128 - at) % 128, 1)
        moved_low = pltpu.roll(low, (128 - HALO - at) % 128, 1)
        return jnp.where(hl, moved_high, jnp.where(ll, moved_low, 0.0))

    def wide(m, x):
        t, q = place_of(m)
        at = (x * 3 + t) * HALO
        if m < 6:
            body = f_ref[m, x]
        else:
            body = ie_ref[x] if m == 12 else ll_ref[x].astype(jnp.float32)
        rows = slice(q * size_y, (q + 1) * size_y)
        body_z = column(own_low[rows], own_high[rows], size_y, at)
        start = (FORWARD.index(m) * size_x + x) * HALO
        blank = jnp.zeros((8 - 2 * HALO, 128), jnp.float32)
        first, last = q * size_y, (q + 1) * size_y
        tile = jnp.concatenate(
            [yh_ref[start : start + HALO] * y_high, blank, yl_ref[start : start + HALO] * y_low], axis=0
        )
        low = jnp.concatenate(
            [yh_low[first : first + HALO] * y_high, blank, yl_low[last - HALO : last] * y_low], axis=0
        )
        high = jnp.concatenate(
            [yh_high[first : first + HALO] * y_high, blank, yl_high[last - HALO : last] * y_low], axis=0
        )
        corner = column(low, high, 8, at)
        return jnp.concatenate(
            [jnp.concatenate([body, body_z], axis=1), jnp.concatenate([tile, corner], axis=1)], axis=0
        )

    half = wide_masks(dims, at)
    xs = range(size_x)
    ex, ey, ez, hx, hy, hz, ie, lv = ([wide(m, x) for x in xs] for m in FORWARD)
    pairs = [coefficients(ie[x], lv[x]) for x in xs]
    ca, cb = [p[0] for p in pairs], [p[1] for p in pairs]
    nothing = jnp.zeros_like(half)
    hx = [hx[x] - half * (forward_y(ez[x]) - forward_z(ey[x])) for x in xs]
    hy = [hy[x] - half * (forward_z(ex[x]) - ((ez[x + 1] if x + 1 < size_x else nothing) - ez[x])) for x in xs]
    hz = [hz[x] - half * (((ey[x + 1] if x + 1 < size_x else nothing) - ey[x]) - forward_y(ex[x])) for x in xs]
    first_ey, first_ez = ey[0], ez[0]
    ex = [ca[x] * ex[x] + cb[x] * (backward_y(hz[x]) - backward_z(hy[x])) for x in xs]
    ey = [ca[x] * ey[x] + cb[x] * (backward_z(hx[x]) - (hz[x] - (hz[x - 1] if x else nothing))) for x in xs]
    ez = [ca[x] * ez[x] + cb[x] * ((hy[x] - (hy[x - 1] if x else nothing)) - backward_y(hx[x])) for x in xs]
    state = [*ex, *ey, *ez, *hx, *hy, *hz, *ca, *cb, first_ey, first_ez]
    for i, a in enumerate(state):
        state_ref[i] = a
    next_hy = hy[-1] - half * (forward_z(ex[-1]) + ez[-1])
    next_hz = hz[-1] + half * (ey[-1] + forward_y(ex[-1]))
    up = pack([hy[-1], hz[-1], next_hy, next_hz, cb[-1]], size_y, size_z)
    down = pack([first_ey, first_ez, ey[0], ez[0], cb[0]], size_y, size_z)
    even = lax.rem(at[0], 2) == 0
    one_ref[...] = jnp.where(even, up, down)
    two_ref[...] = jnp.where(even, down, up)


def third_kernel(dims, at, state_ref, one_ref, two_ref, out_ref):
    groups_x, groups_y, groups_z, size_x, size_y, size_z = dims
    xs = range(size_x)
    half = wide_masks(dims, at)
    half_low = half * (at[0] > 0).astype(jnp.float32)
    state = [[state_ref[i * size_x + x] for x in xs] for i in range(8)]
    ex, ey, ez, hx, hy, hz, ca, cb = state
    first_ey, first_ez = state_ref[8 * size_x], state_ref[8 * size_x + 1]
    even = lax.rem(at[0], 2) == 0
    one, two = one_ref[...], two_ref[...]
    low_hy, low_hz, below_hy, below_hz, low_cb = unpack(jnp.where(even, two, one), 5, size_y)
    next_ey, next_ez, high_ey, high_ez, high_cb = unpack(jnp.where(even, one, two), 5, size_y)
    add_y, add_z = half * next_ez, -(half * next_ey)
    hy[-1], hz[-1] = hy[-1] + add_y, hz[-1] + add_z
    ex[-1] = ex[-1] + cb[-1] * (backward_y(add_z) - backward_z(add_y))
    ey[-1] = ey[-1] - cb[-1] * add_z
    ez[-1] = ez[-1] + cb[-1] * add_y
    add_y, add_z = half_low * first_ez, -(half_low * first_ey)
    low_hy, low_hz = low_hy + add_y, low_hz + add_z
    more_ex = low_cb * (backward_y(add_z) - backward_z(add_y))
    more_ey, more_ez = -(low_cb * add_z), low_cb * add_y
    ey[0] = ey[0] + cb[0] * low_hz
    ez[0] = ez[0] - cb[0] * low_hy
    high_ey = high_ey + high_cb * hz[-1]
    high_ez = high_ez - high_cb * hy[-1]
    low_hy = below_hy + add_y - half_low * (forward_z(more_ex) + more_ez - ez[0])
    low_hz = below_hz + add_z + half_low * (more_ey + forward_y(more_ex) - ey[0])
    after_ey, after_ez = ey[1:] + [high_ey], ez[1:] + [high_ez]
    hx = [hx[x] - half * (forward_y(ez[x]) - forward_z(ey[x])) for x in xs]
    hy = [hy[x] - half * (forward_z(ex[x]) - (after_ez[x] - ez[x])) for x in xs]
    hz = [hz[x] - half * ((after_ey[x] - ey[x]) - forward_y(ex[x])) for x in xs]
    before_hy, before_hz = [low_hy] + hy[:-1], [low_hz] + hz[:-1]
    for x in xs:
        new = (
            ca[x] * ex[x] + cb[x] * (backward_y(hz[x]) - backward_z(hy[x])),
            ca[x] * ey[x] + cb[x] * (backward_z(hx[x]) - (hz[x] - before_hz[x])),
            ca[x] * ez[x] + cb[x] * ((hy[x] - before_hy[x]) - backward_y(hx[x])),
            hx[x], hy[x], hz[x],
        )
        for m in range(6):
            out_ref[m, x] = new[m][:size_y, :size_z]


def halves_of_table(a):
    high = lax.reduce_precision(a, 8, 7)
    return high.astype(jnp.bfloat16), (a - high).astype(jnp.bfloat16)


def halves(a):
    high = a.astype(jnp.bfloat16)
    return high, (a - high.astype(jnp.float32)).astype(jnp.bfloat16)


def product(a, high_ref, low_ref, contract):
    high, low = halves(a)
    dims = (((1,), (contract,)), ((), ()))
    both = lax.dot_general(
        jnp.concatenate([high, low], axis=0), high_ref[...], dims, preferred_element_type=jnp.float32
    )
    rest = lax.dot_general(high, low_ref[...], dims, preferred_element_type=jnp.float32)
    return both[: a.shape[0]] + (both[a.shape[0] :] + rest)


def steering_x(count_x, direction, weight):
    phase = KAPPA * jnp.arange(count_x, dtype=jnp.float32)[:, None] * direction[0]
    return jnp.concatenate([jnp.cos(phase), jnp.sin(phase), jnp.broadcast_to(weight, phase.shape)], axis=1)


def steering_yz(count_y, groups_z, size_z, direction):
    ys = jnp.arange(count_y, dtype=jnp.float32)[None, :, None]
    zval = (jnp.arange(groups_z, dtype=jnp.float32) * size_z + size_z // 2 + 2)[:, None, None]
    phase = (KAPPA * (ys * direction[1] + zval * direction[2])).reshape(groups_z * count_y, -1)
    return jnp.concatenate([jnp.cos(phase), jnp.sin(phase)], axis=1)


def main_kernel(slots, dims, at, *refs):
    groups_x, groups_y, groups_z, size_x, size_y, size_z = dims
    got_refs = refs[:groups_z]
    high_ref, low_ref, x_ref, pattern_ref, elem_ref = refs[groups_z:]
    per_owner = NE // groups_x
    half = half_rows(groups_x * slots, size_y)
    count_x, count_y = groups_x * size_x, groups_y * size_y
    lanes = groups_z * count_y
    zs = size_z // 2 + 2

    def pick(c, start, size, stride):
        out = None
        for s, ref in enumerate(got_refs):
            part = ref[pl.ds(start, size, stride=stride), :]
            here = lax.rem(at[2] - s + groups_z, groups_z) == c
            out = part if out is None else jnp.where(here, part, out)
        return out

    loaded = {}

    def plane(m, k):
        row, q = slab_place(m, k)
        if row not in loaded:
            loaded[row] = [
                pick(c, b * groups_x * size_x * half + row, count_x, half)
                for c in range(groups_z)
                for b in range(groups_y)
            ]
        return jnp.concatenate([p[:, q * size_y : (q + 1) * size_y] for p in loaded[row]], axis=1)

    row_id = lax.broadcasted_iota(jnp.int32, (count_x, lanes), 0)
    lane_id = lax.broadcasted_iota(jnp.int32, (count_x, lanes), 1) % count_y
    x_up, x_low = row_id < count_x - 1, row_id > 0
    y_up, y_low = lane_id < count_y - 1, lane_id > 0

    def dxp(a):
        return jnp.where(x_up, pltpu.roll(a, count_x - 1, 0), 0.0) - a

    def dyp(a):
        return jnp.where(y_up, pltpu.roll(a, lanes - 1, 1), 0.0) - a

    def dxm(a):
        return a - jnp.where(x_low, pltpu.roll(a, 1, 0), 0.0)

    def dym(a):
        return a - jnp.where(y_low, pltpu.roll(a, 1, 1), 0.0)

    ca, cb = {}, {}
    for k in range(-5, 2):
        ca[k], cb[k] = coefficients(plane(12, k), plane(13, k))

    def step(ex, ey, ez, hx, hy, hz, low, high):
        nhx = {k: hx[k] - 0.5 * (dyp(ez[k]) - (ey[k + 1] - ey[k])) for k in range(low - 1, high + 1)}
        nhy = {k: hy[k] - 0.5 * ((ex[k + 1] - ex[k]) - dxp(ez[k])) for k in range(low - 1, high + 1)}
        nhz = {k: hz[k] - 0.5 * (dxp(ey[k]) - dyp(ex[k])) for k in range(low, high + 1)}
        nex = {k: ca[k] * ex[k] + cb[k] * (dym(nhz[k]) - (nhy[k] - nhy[k - 1])) for k in range(low, high + 1)}
        ney = {k: ca[k] * ey[k] + cb[k] * ((nhx[k] - nhx[k - 1]) - dxm(nhz[k])) for k in range(low, high + 1)}
        nez = {k: ca[k] * ez[k] + cb[k] * (dxm(nhy[k]) - dym(nhx[k])) for k in range(low, high + 1)}
        return nex, ney, nez, nhx, nhy, nhz

    def arrays(first):
        return [
            {k: plane(m, k) for k in range(LOWEST[m], TOPMOST[m] + 1)} for m in range(first, first + 6)
        ]

    u1 = step(*arrays(0), -5, 1)
    u2 = step(*u1, -4, 0)
    rows = []
    for m in (0, 1, 3, 4):
        rows.append(u1[m][0] * math.cos(OMEGA) + u2[m][0] * math.cos(2 * OMEGA))
        rows.append(-u1[m][0] * math.sin(OMEGA) - u2[m][0] * math.sin(2 * OMEGA))
    dft = jnp.concatenate(rows, axis=0)

    nd = high_ref.shape[1] // 2
    cos_x, sin_x, weight = x_ref[:, :nd], x_ref[:, nd : 2 * nd], x_ref[:1, 2 * nd :]
    amp = 1.0 / math.sqrt(count_x * count_y * groups_z)
    prod = product(dft, high_ref, low_ref, 0)
    pattern = jnp.zeros((1, nd), jnp.float32)
    weight = (2.0 * amp) * weight
    mixing = []
    for c in range(4):
        re = prod[2 * c * count_x : (2 * c + 1) * count_x]
        im = prod[(2 * c + 1) * count_x : (2 * c + 2) * count_x]
        real = re[:, :nd] - im[:, nd:]
        imag = re[:, nd:] + im[:, :nd]
        far_re = amp * jnp.sum(real * cos_x - imag * sin_x, axis=0, keepdims=True)
        far_im = amp * jnp.sum(real * sin_x + imag * cos_x, axis=0, keepdims=True)
        pattern = pattern + far_re * far_re + far_im * far_im
        out_re, out_im = weight * far_re, weight * far_im
        b_re = out_re * cos_x + out_im * sin_x
        b_im = out_im * cos_x - out_re * sin_x
        mixing.append(jnp.concatenate([b_re, b_im], axis=1))
        mixing.append(jnp.concatenate([b_im, -b_re], axis=1))
    pattern_ref[...] = pattern

    src = product(jnp.concatenate(mixing, axis=0), high_ref, low_ref, 1)

    def with_sources(state, when):
        state = [dict(a) for a in state]
        for c, m in enumerate((0, 1, 3, 4)):
            gre = src[2 * c * count_x : (2 * c + 1) * count_x]
            gim = src[(2 * c + 1) * count_x : (2 * c + 2) * count_x]
            state[m][0] = state[m][0] + (gre * math.cos(OMEGA * when) - gim * math.sin(OMEGA * when))
        return state

    v1 = step(*with_sources(arrays(6), 2), -5, 0)
    v2 = step(*with_sources(v1, 1), -4, -1)
    sens = [
        sum(v1[m][k] * u2[m][k] for m in range(3)) + sum(v2[m][k] * u1[m][k] for m in range(3))
        for k in range(-4, 0)
    ]
    sens = jnp.concatenate(sens, axis=0)

    own = at[0]
    senders = groups_x * groups_y * groups_z
    total = senders * slots
    lists = groups_x * slots
    row, lane = (8, 2 * size_y) if half == BODY else (BODY, 0)
    pieces = range(-(-lists // (4 * size_y - lane)))

    def table(x):
        def piece(r):
            return jnp.concatenate(
                [pick(c, x * half + row + r, groups_x * groups_y, size_x * half)[:, lane:] for c in range(groups_z)], axis=0
            )

        return jnp.concatenate([piece(r) for r in pieces], axis=1)

    cell_tab, elem_tab = table(0), table(1)
    width = cell_tab.shape[1]
    at_lane = lax.broadcasted_iota(jnp.int32, (width, total), 0)
    slot = lax.broadcasted_iota(jnp.int32, (width, total), 1)
    spread_cell = (at_lane == own * slots + slot % slots).astype(jnp.float32).astype(jnp.bfloat16)
    spread_elem = (at_lane == slot % lists).astype(jnp.float32).astype(jnp.bfloat16)
    sender = lax.broadcasted_iota(jnp.int32, (senders, total), 0)
    slot = lax.broadcasted_iota(jnp.int32, (senders, total), 1)
    mine, owned = sender == slot // slots, sender == (slot // lists) * groups_x + own

    def spread(table, places, rows):
        moved = jnp.dot(table.astype(jnp.bfloat16), places, preferred_element_type=jnp.float32)
        return jnp.sum(jnp.where(rows, moved, 0.0), axis=0, keepdims=True)

    cell_tab = (cell_tab + 0.5).astype(jnp.int32)
    column = spread((cell_tab // size_z).astype(jnp.float32), spread_cell, mine)
    place_z = spread((cell_tab % size_z).astype(jnp.float32), spread_cell, mine)
    elems = spread(elem_tab, spread_elem, owned)
    column = (column + 0.5).astype(jnp.int32)
    place_z = (place_z + 0.5).astype(jnp.int32) - (zs - 4)
    elems = (elems + 1.5).astype(jnp.int32) - 1
    slot = lax.broadcasted_iota(jnp.int32, (1, total), 1)
    block = slot // lists
    place_x = (slot // slots % groups_x) * size_x + column // size_y
    place_y = column % size_y
    row_want = place_z * count_x + place_x
    lane_want = (block // groups_y) * count_y + (block % groups_y) * size_y + place_y
    hot_row = (lax.broadcasted_iota(jnp.int32, (4 * count_x, total), 0) == row_want).astype(jnp.float32)
    hot_row = hot_row.astype(jnp.bfloat16)
    hot_lane = lax.broadcasted_iota(jnp.int32, (lanes, total), 0) == lane_want
    picked = lax.dot_general(
        jnp.concatenate(halves(sens), axis=0), jnp.concatenate([hot_row, hot_row], axis=0),
        (((0,), (0,)), ((), ())), preferred_element_type=jnp.float32,
    )
    values = jnp.sum(jnp.where(hot_lane, picked, 0.0), axis=0, keepdims=True)
    hot_elem = (lax.broadcasted_iota(jnp.int32, (per_owner, total), 0) == elems).astype(jnp.float32)
    high = values.astype(jnp.bfloat16).astype(jnp.float32)
    both = jnp.where(lax.broadcasted_iota(jnp.int32, (8, total), 0) == 0, high, values - high)
    sums = lax.dot_general(
        both.astype(jnp.bfloat16), hot_elem.astype(jnp.bfloat16), (((1,), (1,)), ((), ())),
        preferred_element_type=jnp.float32,
    )
    sums = sums[:1] + sums[1:2]
    scale = 1.0 / math.sqrt(groups_x * groups_x * groups_y * groups_z * slots / NE)
    elem_ref[...] = sums * scale


def local(fields, adjoint, inv_eps, loss_level, direction, pattern_weight, voxel_cell, voxel_elem):
    size_x, size_y, size_z = inv_eps.shape
    groups_x, groups_y, groups_z = (lax.axis_size(a) for a in ("gx", "gy", "gz"))
    dims = (groups_x, groups_y, groups_z, size_x, size_y, size_z)
    slots = voxel_cell.shape[4]
    per_owner = NE // groups_x
    half = half_rows(groups_x * slots, size_y)
    nd = direction.shape[1]
    vmem = pl.BlockSpec(memory_space=pltpu.VMEM)
    hbm = pl.BlockSpec(memory_space=pltpu.HBM)

    def call(kernel, name, outs, *args, fetched=0, limit=48):
        scratch = [pltpu.VMEM(a.shape, a.dtype) for a in args[:fetched]]
        args = [
            pltpu.with_memory_space_constraint(a, pltpu.HBM) if i < fetched else a for i, a in enumerate(args)
        ]
        if fetched:
            scratch.append(pltpu.SemaphoreType.DMA((fetched,)))

        def located(*refs):
            kernel(dims, tuple(lax.axis_index(a) for a in ("gx", "gy", "gz")), *refs)

        return pl.pallas_call(
            located,
            out_shape=tuple(jax.ShapeDtypeStruct(o, jnp.float32) for o in outs),
            in_specs=[hbm] * fetched + [vmem] * (len(args) - fetched),
            out_specs=(vmem,) * len(outs),
            scratch_shapes=scratch,
            compiler_params=pltpu.CompilerParams(vmem_limit_bytes=limit * 1024 * 1024),
            name=name,
        )(*args)

    zrows = -(-(3 * HALO * size_x) // 8) * 8
    yrows = len(FORWARD) * size_x * HALO
    z_count, y_count = 1 if groups_z == 2 else 2, 1 if groups_y == 2 else 2
    send, *edges = call(
        first_kernel, "first",
        [(groups_x * groups_y, size_x * half, 4 * size_y)]
        + [(zrows, 4 * size_y)] * z_count + [(yrows, size_z)] * y_count,
        fields, adjoint, inv_eps, loss_level, voxel_cell.reshape(groups_x, slots),
        voxel_elem.reshape(groups_x, slots), fetched=6, limit=16,
    )
    z_top, z_bottom = edges[0], edges[z_count - 1]
    y_top, y_bottom = edges[z_count], edges[-1]
    z_low, z_high = neighbours("gz", z_top, z_bottom)
    z_sides = [z_low] if groups_z == 2 else [z_low, z_high]
    y_low, y_high = neighbours("gy", jnp.concatenate([y_top] + z_sides), jnp.concatenate([y_bottom] + z_sides))
    got = lax.all_to_all(send, ("gy", "gx"), split_axis=0, concat_axis=0, tiled=True)
    got = got.reshape(groups_x * groups_y * size_x * half, 4 * size_y)
    seen, _ = lax.optimization_barrier((direction, z_low))
    table_high, table_low = halves_of_table(steering_yz(groups_y * size_y, groups_z, size_z, seen))
    rows = size_y + 8
    state, one, two = call(
        second_kernel, "second",
        [(8 * size_x + 2, rows, size_z + 128)] + [(5 * size_y + 24 + rows, size_z)] * 2,
        fields, inv_eps, loss_level, z_low, z_high, y_low, y_high,
    )
    seen, seen_weight, _ = lax.optimization_barrier((direction, pattern_weight, one))
    table_x = steering_x(groups_x * size_x, seen, seen_weight)

    one_side, other_side = (
        lax.ppermute(sent, "gx", [p for i in range(first, groups_x - 1, 2) for p in ((i, i + 1), (i + 1, i))])
        for first, sent in ((0, one), (1, two))
    )

    got, _ = lax.optimization_barrier((got, one))
    gots = [got] + [
        lax.ppermute(got, "gz", [(i, (i + s) % groups_z) for i in range(groups_z)]) for s in range(1, groups_z)
    ]

    pattern, elem = call(
        functools.partial(main_kernel, slots), "main", [(1, nd), (1, per_owner)],
        *gots, table_high, table_low, table_x,
    )
    state, pattern = lax.optimization_barrier((state, pattern))
    (fields_out,) = call(
        third_kernel, "third", [(6, size_x, size_y, size_z)], state, one_side, other_side
    )
    return (fields_out, pattern.reshape(nd), elem.reshape(per_owner))


def solution(mesh):
    in_specs = (
        P(None, ("groups", "gx"), "gy", "gz"),
        P(None, ("groups", "gx"), "gy", "gz"),
        P(("groups", "gx"), "gy", "gz"),
        P(("groups", "gx"), "gy", "gz"),
        P(),
        P(),
        P(("groups", "gx"), "gy", "gz", None, None),
        P(("groups", "gx"), "gy", "gz", None, None),
    )
    out_specs = (P(None, ("groups", "gx"), "gy", "gz"), P("groups"), P(("groups", "gx")))
    return jax.shard_map(local, mesh=mesh, in_specs=in_specs, out_specs=out_specs, check_vma=False)
```

```python
import functools
import math

import jax
import jax.numpy as jnp
from jax import lax
from jax.experimental import pallas as pl
from jax.experimental.pallas import tpu as pltpu
from jax.sharding import PartitionSpec as P

STEPS = 2
NE = 1024
OMEGA = 0.9
KAPPA = 0.37
HIGHEST = lax.Precision.HIGHEST
HALO = 2
COMPS = (0, 1, 3, 4)

SETS = ((0, 1, 2, 3), (4, 6, 7, 12), (5, 13, 8, 9), (10, 11))
STARTS = (0, 9, 17, 24)
BODY = 28
LOWEST = (-6, -6, -6, -6, -6, -5, -6, -6, -6, -6, -6, -6, -6, -5)
TOPMOST = (2, 2, 1, 1, 1, 1, 1, 1, 0, 0, 0, 0, 1, 1)
FORWARD = (0, 1, 2, 3, 4, 5, 12, 13)


def coefficients(inv_eps, level):
    level = 0.15 * level
    return ((1.0 - level) / (1.0 + level), 0.5 * inv_eps / (1.0 + level))


def place_of(m):
    for t, members in enumerate(SETS):
        if m in members:
            return t, members.index(m)


def slab_place(m, k):
    t, q = place_of(m)
    if t == 3:
        return STARTS[t] + (k - LOWEST[m]) % 4, q + 2 * ((k - LOWEST[m]) // 4)
    return STARTS[t] + k - LOWEST[m], q


def half_rows(lists, size_y):
    return BODY if lists <= 2 * size_y else BODY + 4


def neighbours(axis, top, bottom):
    count = lax.axis_size(axis)
    if count == 2:
        other = lax.ppermute(top, axis, [(0, 1), (1, 0)])
        return other, other
    forward = [(i, i + 1) for i in range(count - 1)]
    return lax.ppermute(top, axis, forward), lax.ppermute(bottom, axis, [(t, s) for s, t in forward])


def fetch(pairs, sems):
    copies = [pltpu.make_async_copy(src, dst, sems.at[i]) for i, (src, dst) in enumerate(pairs)]
    for copy in copies:
        copy.start()
    for copy in copies:
        copy.wait()


def first_kernel(dims, at, *refs):
    groups_x, groups_y, groups_z, size_x, size_y, size_z = dims
    borders = 1 if groups_z == 2 else 2, 1 if groups_y == 2 else 2
    sources, refs = refs[:6], refs[6:]
    send_ref, refs = refs[0], refs[1:]
    z_refs, y_refs, refs = refs[: borders[0]], refs[borders[0] : sum(borders)], refs[sum(borders) :]
    f_ref, a_ref, ie_ref, ll_ref, cell_ref, elem_ref, sems = refs
    fetch(list(zip(sources, refs[:6])), sems)

    def array(m, x):
        if m < 6:
            return f_ref[m, x]
        if m < 12:
            return a_ref[m - 6, x]
        return ie_ref[x] if m == 12 else ll_ref[x].astype(jnp.float32)

    def store(targets, index, top, bottom):
        if len(targets) == 1:
            targets[0][...] = jnp.where(index == 0, top, bottom)
        else:
            targets[0][...], targets[1][...] = top, bottom

    zs = size_z // 2 + 2
    lists, slots = cell_ref.shape
    half = half_rows(lists * slots, size_y)
    per_row = (2 if half == BODY else 4) * size_y // slots
    tops, bottoms = [], []
    for x in range(size_x):
        parts = []
        for t, members in enumerate(SETS):
            blocks = [array(m, x) for m in members]
            blocks += [jnp.zeros((size_y, size_z), jnp.float32)] * (4 - len(members))
            flipped = jnp.concatenate(blocks, axis=0).T
            if t < 2:
                parts.append(flipped[zs + LOWEST[members[0]] : zs + TOPMOST[members[0]] + 1])
            else:
                first, last = (-5, -6) if t == 2 else (-6, -2)
                count, last_lanes = (7, slice(2 * size_y, None)) if t == 2 else (4, slice(0, 2 * size_y))
                left = flipped[zs + first : zs + first + count, : 2 * size_y]
                parts.append(jnp.concatenate([left, flipped[zs + last : zs + last + count, last_lanes]], axis=1))
            if t < 3:
                tops.append(flipped[size_z - HALO :])
                bottoms.append(flipped[:HALO])
        if x < 2:
            table = (cell_ref, elem_ref)[x][...].astype(jnp.float32)
            lines = []
            for r in range(0, lists, per_row):
                line = [table[i : i + 1] for i in range(r, min(r + per_row, lists))]
                if len(line) < per_row:
                    line.append(jnp.zeros((1, (per_row - len(line)) * slots), jnp.float32))
                lines.append(jnp.concatenate(line, axis=1))
            if half == BODY:
                last = jnp.concatenate([parts[0][8:, : 2 * size_y], lines[0]], axis=1)
                parts[0] = jnp.concatenate([parts[0][:8], last], axis=0)
            else:
                lines.append(jnp.zeros((half - BODY - len(lines), 4 * size_y), jnp.float32))
                parts += lines
        rows = jnp.concatenate(parts, axis=0)
        for d in range(groups_x * groups_y):
            send_ref[d, x * half : (x + 1) * half] = rows
    pad = [jnp.zeros((z_refs[0].shape[0] - HALO * len(tops), 4 * size_y), jnp.float32)]
    store(z_refs, at[2], jnp.concatenate(tops + pad, axis=0), jnp.concatenate(bottoms + pad, axis=0))
    layers = [array(m, x) for m in FORWARD for x in range(size_x)]
    top = jnp.concatenate([a[size_y - HALO :] for a in layers], axis=0)
    store(y_refs, at[1], top, jnp.concatenate([a[:HALO] for a in layers], axis=0))


def wide_masks(dims, at):
    _, _, _, _, size_y, size_z = dims
    shape = (size_y + 8, size_z + 128)
    row = lax.broadcasted_iota(jnp.int32, shape, 0)
    lane = lax.broadcasted_iota(jnp.int32, shape, 1)
    out_y = jnp.logical_and(row >= size_y + 4, at[1] == 0)
    out_z = jnp.logical_and(lane >= size_z + 64, at[2] == 0)
    return jnp.where(jnp.logical_or(out_y, out_z), 0.0, 0.5)


def forward_y(a):
    return pltpu.roll(a, a.shape[0] - 1, 0) - a


def forward_z(a):
    return pltpu.roll(a, a.shape[1] - 1, 1) - a


def backward_y(a):
    return a - pltpu.roll(a, 1, 0)


def backward_z(a):
    return a - pltpu.roll(a, 1, 1)


def pack(planes, size_y, size_z):
    row = lax.broadcasted_iota(jnp.int32, (8, size_z), 0)
    own = jnp.logical_or(row < 2, row >= 6)
    lane = lax.broadcasted_iota(jnp.int32, (planes[0].shape[0], 128), 1)
    out = [plane[:size_y, :size_z] for plane in planes]
    for p in range(0, len(planes), 2):
        tile = planes[p][size_y:, :size_z]
        if p + 1 < len(planes):
            tile = jnp.where(own, tile, pltpu.roll(planes[p + 1][size_y:, :size_z], 4, 0))
        out.append(tile)
    border = jnp.zeros((planes[0].shape[0], 128), jnp.float32)
    for p, plane in enumerate(planes):
        moved = pltpu.roll(plane[:, size_z:], 8 * p + 2, 1)
        border = jnp.where(jnp.logical_and(lane >= 8 * p, lane < 8 * p + 4), moved, border)
    return jnp.concatenate(out + [border], axis=0)


def unpack(rows, count, size_y):
    tiles = count * size_y
    border = rows[tiles + 8 * ((count + 1) // 2) :]
    out = []
    for p in range(count):
        tile = rows[tiles + 8 * (p // 2) : tiles + 8 * (p // 2) + 8]
        body = jnp.concatenate(
            [rows[p * size_y : (p + 1) * size_y], pltpu.roll(tile, 4, 0) if p % 2 else tile], axis=0
        )
        out.append(jnp.concatenate([body, pltpu.roll(border, 128 - (8 * p + 2), 1)], axis=1))
    return out


def second_kernel(dims, at, f_ref, ie_ref, ll_ref, zl_ref, zh_ref, yl_ref, yh_ref, state_ref, one_ref, two_ref):
    groups_x, groups_y, groups_z, size_x, size_y, size_z = dims
    zrows = zl_ref.shape[0]
    lane = lax.broadcasted_iota(jnp.int32, (8, 128), 1)
    high_lane = jnp.logical_and(lane < HALO, at[2] < groups_z - 1)
    low_lane = jnp.logical_and(lane >= 128 - HALO, at[2] > 0)
    y_high = (at[1] < groups_y - 1).astype(jnp.float32)
    y_low = (at[1] > 0).astype(jnp.float32)

    def flip(a):
        return jnp.concatenate([a, jnp.zeros((128 - zrows, a.shape[1]), jnp.float32)], axis=0).T

    own_low, own_high = flip(zl_ref[...]), flip(zh_ref[...])
    edge = HALO * size_x * len(FORWARD)
    after = edge if groups_z == 2 else edge + zrows
    yl_low, yl_high = flip(yl_ref[edge : edge + zrows]), flip(yl_ref[after : after + zrows])
    yh_low, yh_high = flip(yh_ref[edge : edge + zrows]), flip(yh_ref[after : after + zrows])

    def column(low, high, rows, at):
        reps = rows // 8
        hl = jnp.concatenate([high_lane] * reps, axis=0)
        ll = jnp.concatenate([low_lane] * reps, axis=0)
        moved_high = pltpu.roll(high, (128 - at) % 128, 1)
        moved_low = pltpu.roll(low, (128 - HALO - at) % 128, 1)
        return jnp.where(hl, moved_high, jnp.where(ll, moved_low, 0.0))

    def wide(m, x):
        t, q = place_of(m)
        at = (x * 3 + t) * HALO
        if m < 6:
            body = f_ref[m, x]
        else:
            body = ie_ref[x] if m == 12 else ll_ref[x].astype(jnp.float32)
        rows = slice(q * size_y, (q + 1) * size_y)
        body_z = column(own_low[rows], own_high[rows], size_y, at)
        start = (FORWARD.index(m) * size_x + x) * HALO
        blank = jnp.zeros((8 - 2 * HALO, 128), jnp.float32)
        first, last = q * size_y, (q + 1) * size_y
        tile = jnp.concatenate(
            [yh_ref[start : start + HALO] * y_high, blank, yl_ref[start : start + HALO] * y_low], axis=0
        )
        low = jnp.concatenate(
            [yh_low[first : first + HALO] * y_high, blank, yl_low[last - HALO : last] * y_low], axis=0
        )
        high = jnp.concatenate(
            [yh_high[first : first + HALO] * y_high, blank, yl_high[last - HALO : last] * y_low], axis=0
        )
        corner = column(low, high, 8, at)
        return jnp.concatenate(
            [jnp.concatenate([body, body_z], axis=1), jnp.concatenate([tile, corner], axis=1)], axis=0
        )

    half = wide_masks(dims, at)
    xs = range(size_x)
    ex, ey, ez, hx, hy, hz, ie, lv = ([wide(m, x) for x in xs] for m in FORWARD)
    pairs = [coefficients(ie[x], lv[x]) for x in xs]
    ca, cb = [p[0] for p in pairs], [p[1] for p in pairs]
    nothing = jnp.zeros_like(half)
    hx = [hx[x] - half * (forward_y(ez[x]) - forward_z(ey[x])) for x in xs]
    hy = [hy[x] - half * (forward_z(ex[x]) - ((ez[x + 1] if x + 1 < size_x else nothing) - ez[x])) for x in xs]
    hz = [hz[x] - half * (((ey[x + 1] if x + 1 < size_x else nothing) - ey[x]) - forward_y(ex[x])) for x in xs]
    first_ey, first_ez = ey[0], ez[0]
    ex = [ca[x] * ex[x] + cb[x] * (backward_y(hz[x]) - backward_z(hy[x])) for x in xs]
    ey = [ca[x] * ey[x] + cb[x] * (backward_z(hx[x]) - (hz[x] - (hz[x - 1] if x else nothing))) for x in xs]
    ez = [ca[x] * ez[x] + cb[x] * ((hy[x] - (hy[x - 1] if x else nothing)) - backward_y(hx[x])) for x in xs]
    state = [*ex, *ey, *ez, *hx, *hy, *hz, *ca, *cb, first_ey, first_ez]
    for i, a in enumerate(state):
        state_ref[i] = a
    next_hy = hy[-1] - half * (forward_z(ex[-1]) + ez[-1])
    next_hz = hz[-1] + half * (ey[-1] + forward_y(ex[-1]))
    up = pack([hy[-1], hz[-1], next_hy, next_hz, cb[-1]], size_y, size_z)
    down = pack([first_ey, first_ez, ey[0], ez[0], cb[0]], size_y, size_z)
    even = lax.rem(at[0], 2) == 0
    one_ref[...] = jnp.where(even, up, down)
    two_ref[...] = jnp.where(even, down, up)


def third_kernel(dims, at, state_ref, one_ref, two_ref, out_ref):
    groups_x, groups_y, groups_z, size_x, size_y, size_z = dims
    xs = range(size_x)
    half = wide_masks(dims, at)
    half_low = half * (at[0] > 0).astype(jnp.float32)
    state = [[state_ref[i * size_x + x] for x in xs] for i in range(8)]
    ex, ey, ez, hx, hy, hz, ca, cb = state
    first_ey, first_ez = state_ref[8 * size_x], state_ref[8 * size_x + 1]
    even = lax.rem(at[0], 2) == 0
    one, two = one_ref[...], two_ref[...]
    low_hy, low_hz, below_hy, below_hz, low_cb = unpack(jnp.where(even, two, one), 5, size_y)
    next_ey, next_ez, high_ey, high_ez, high_cb = unpack(jnp.where(even, one, two), 5, size_y)
    add_y, add_z = half * next_ez, -(half * next_ey)
    hy[-1], hz[-1] = hy[-1] + add_y, hz[-1] + add_z
    ex[-1] = ex[-1] + cb[-1] * (backward_y(add_z) - backward_z(add_y))
    ey[-1] = ey[-1] - cb[-1] * add_z
    ez[-1] = ez[-1] + cb[-1] * add_y
    add_y, add_z = half_low * first_ez, -(half_low * first_ey)
    low_hy, low_hz = low_hy + add_y, low_hz + add_z
    more_ex = low_cb * (backward_y(add_z) - backward_z(add_y))
    more_ey, more_ez = -(low_cb * add_z), low_cb * add_y
    ey[0] = ey[0] + cb[0] * low_hz
    ez[0] = ez[0] - cb[0] * low_hy
    high_ey = high_ey + high_cb * hz[-1]
    high_ez = high_ez - high_cb * hy[-1]
    low_hy = below_hy + add_y - half_low * (forward_z(more_ex) + more_ez - ez[0])
    low_hz = below_hz + add_z + half_low * (more_ey + forward_y(more_ex) - ey[0])
    after_ey, after_ez = ey[1:] + [high_ey], ez[1:] + [high_ez]
    hx = [hx[x] - half * (forward_y(ez[x]) - forward_z(ey[x])) for x in xs]
    hy = [hy[x] - half * (forward_z(ex[x]) - (after_ez[x] - ez[x])) for x in xs]
    hz = [hz[x] - half * ((after_ey[x] - ey[x]) - forward_y(ex[x])) for x in xs]
    before_hy, before_hz = [low_hy] + hy[:-1], [low_hz] + hz[:-1]
    for x in xs:
        new = (
            ca[x] * ex[x] + cb[x] * (backward_y(hz[x]) - backward_z(hy[x])),
            ca[x] * ey[x] + cb[x] * (backward_z(hx[x]) - (hz[x] - before_hz[x])),
            ca[x] * ez[x] + cb[x] * ((hy[x] - before_hy[x]) - backward_y(hx[x])),
            hx[x], hy[x], hz[x],
        )
        for m in range(6):
            out_ref[m, x] = new[m][:size_y, :size_z]


def halves_of_table(a):
    high = lax.reduce_precision(a, 8, 7)
    return jnp.concatenate([high, a - high], axis=0).astype(jnp.bfloat16)


def halves(a):
    high = a.astype(jnp.bfloat16)
    return high, (a - high.astype(jnp.float32)).astype(jnp.bfloat16)


def product(a, table_ref, contract):
    rows, size = a.shape[0], table_ref.shape[0] // 2
    high, low = halves(a)
    if contract == 0:
        nothing = jnp.zeros_like(low)
        left = jnp.concatenate(
            [jnp.concatenate([high, high], axis=1), jnp.concatenate([low, nothing], axis=1)], axis=0
        )
    else:
        left = jnp.concatenate([high, low], axis=0)
    dims = (((1,), (contract,)), ((), ()))
    both = lax.dot_general(left, table_ref[...], dims, preferred_element_type=jnp.float32)
    if contract == 0:
        return both[:rows] + both[rows:]
    return both[:rows, :size] + (both[rows:, :size] + both[:rows, size:])


def steering_x(count_x, direction, weight):
    phase = KAPPA * jnp.arange(count_x, dtype=jnp.float32)[:, None] * direction[0]
    return jnp.concatenate([jnp.cos(phase), jnp.sin(phase), jnp.broadcast_to(weight, phase.shape)], axis=1)


def steering_yz(count_y, groups_z, size_z, direction):
    ys = jnp.arange(count_y, dtype=jnp.float32)[None, :, None]
    zval = (jnp.arange(groups_z, dtype=jnp.float32) * size_z + size_z // 2 + 2)[:, None, None]
    phase = (KAPPA * (ys * direction[1] + zval * direction[2])).reshape(groups_z * count_y, -1)
    return jnp.concatenate([jnp.cos(phase), jnp.sin(phase)], axis=1)


def main_kernel(slots, dims, at, *refs):
    groups_x, groups_y, groups_z, size_x, size_y, size_z = dims
    got_refs = refs[:groups_z]
    table_ref, x_ref, pattern_ref, elem_ref = refs[groups_z:]
    per_owner = NE // groups_x
    half = half_rows(groups_x * slots, size_y)
    count_x, count_y = groups_x * size_x, groups_y * size_y
    lanes = groups_z * count_y
    zs = size_z // 2 + 2

    def pick(c, start, size, stride):
        out = None
        for s, ref in enumerate(got_refs):
            part = ref[pl.ds(start, size, stride=stride), :]
            here = lax.rem(at[2] - s + groups_z, groups_z) == c
            out = part if out is None else jnp.where(here, part, out)
        return out

    loaded = {}

    def plane(m, k):
        row, q = slab_place(m, k)
        if row not in loaded:
            loaded[row] = [
                pick(c, b * groups_x * size_x * half + row, count_x, half)
                for c in range(groups_z)
                for b in range(groups_y)
            ]
        return jnp.concatenate([p[:, q * size_y : (q + 1) * size_y] for p in loaded[row]], axis=1)

    row_id = lax.broadcasted_iota(jnp.int32, (count_x, lanes), 0)
    lane_id = lax.broadcasted_iota(jnp.int32, (count_x, lanes), 1) % count_y
    x_up, x_low = row_id < count_x - 1, row_id > 0
    y_up, y_low = lane_id < count_y - 1, lane_id > 0

    def dxp(a):
        return jnp.where(x_up, pltpu.roll(a, count_x - 1, 0), 0.0) - a

    def dyp(a):
        return jnp.where(y_up, pltpu.roll(a, lanes - 1, 1), 0.0) - a

    def dxm(a):
        return a - jnp.where(x_low, pltpu.roll(a, 1, 0), 0.0)

    def dym(a):
        return a - jnp.where(y_low, pltpu.roll(a, 1, 1), 0.0)

    ca, cb = {}, {}
    for k in range(-5, 2):
        ca[k], cb[k] = coefficients(plane(12, k), plane(13, k))

    def step(ex, ey, ez, hx, hy, hz, low, high):
        nhx = {k: hx[k] - 0.5 * (dyp(ez[k]) - (ey[k + 1] - ey[k])) for k in range(low - 1, high + 1)}
        nhy = {k: hy[k] - 0.5 * ((ex[k + 1] - ex[k]) - dxp(ez[k])) for k in range(low - 1, high + 1)}
        nhz = {k: hz[k] - 0.5 * (dxp(ey[k]) - dyp(ex[k])) for k in range(low, high + 1)}
        nex = {k: ca[k] * ex[k] + cb[k] * (dym(nhz[k]) - (nhy[k] - nhy[k - 1])) for k in range(low, high + 1)}
        ney = {k: ca[k] * ey[k] + cb[k] * ((nhx[k] - nhx[k - 1]) - dxm(nhz[k])) for k in range(low, high + 1)}
        nez = {k: ca[k] * ez[k] + cb[k] * (dxm(nhy[k]) - dym(nhx[k])) for k in range(low, high + 1)}
        return nex, ney, nez, nhx, nhy, nhz

    def arrays(first):
        return [
            {k: plane(m, k) for k in range(LOWEST[m], TOPMOST[m] + 1)} for m in range(first, first + 6)
        ]

    u1 = step(*arrays(0), -5, 1)
    u2 = step(*u1, -4, 0)
    rows = []
    for m in (0, 1, 3, 4):
        rows.append(u1[m][0] * math.cos(OMEGA) + u2[m][0] * math.cos(2 * OMEGA))
        rows.append(-u1[m][0] * math.sin(OMEGA) - u2[m][0] * math.sin(2 * OMEGA))
    dft = jnp.concatenate(rows, axis=0)

    nd = table_ref.shape[1] // 2
    cos_x, sin_x, weight = x_ref[:, :nd], x_ref[:, nd : 2 * nd], x_ref[:1, 2 * nd :]
    amp = 1.0 / math.sqrt(count_x * count_y * groups_z)
    prod = product(dft, table_ref, 0)
    pattern = jnp.zeros((1, nd), jnp.float32)
    weight = (2.0 * amp) * weight
    mixing = []
    for c in range(4):
        re = prod[2 * c * count_x : (2 * c + 1) * count_x]
        im = prod[(2 * c + 1) * count_x : (2 * c + 2) * count_x]
        real = re[:, :nd] - im[:, nd:]
        imag = re[:, nd:] + im[:, :nd]
        far_re = amp * jnp.sum(real * cos_x - imag * sin_x, axis=0, keepdims=True)
        far_im = amp * jnp.sum(real * sin_x + imag * cos_x, axis=0, keepdims=True)
        pattern = pattern + far_re * far_re + far_im * far_im
        out_re, out_im = weight * far_re, weight * far_im
        b_re = out_re * cos_x + out_im * sin_x
        b_im = out_im * cos_x - out_re * sin_x
        mixing.append(jnp.concatenate([b_re, b_im], axis=1))
        mixing.append(jnp.concatenate([b_im, -b_re], axis=1))
    pattern_ref[...] = pattern

    src = product(jnp.concatenate(mixing, axis=0), table_ref, 1)

    def with_sources(state, when):
        state = [dict(a) for a in state]
        for c, m in enumerate((0, 1, 3, 4)):
            gre = src[2 * c * count_x : (2 * c + 1) * count_x]
            gim = src[(2 * c + 1) * count_x : (2 * c + 2) * count_x]
            state[m][0] = state[m][0] + (gre * math.cos(OMEGA * when) - gim * math.sin(OMEGA * when))
        return state

    v1 = step(*with_sources(arrays(6), 2), -5, 0)
    v2 = step(*with_sources(v1, 1), -4, -1)
    sens = [
        sum(v1[m][k] * u2[m][k] for m in range(3)) + sum(v2[m][k] * u1[m][k] for m in range(3))
        for k in range(-4, 0)
    ]
    sens = jnp.concatenate(sens, axis=0)

    own = at[0]
    senders = groups_x * groups_y * groups_z
    total = senders * slots
    lists = groups_x * slots
    row, lane = (8, 2 * size_y) if half == BODY else (BODY, 0)
    pieces = range(-(-lists // (4 * size_y - lane)))

    def table(x):
        def piece(r):
            return jnp.concatenate(
                [pick(c, x * half + row + r, groups_x * groups_y, size_x * half)[:, lane:] for c in range(groups_z)], axis=0
            )

        return jnp.concatenate([piece(r) for r in pieces], axis=1)

    cell_tab, elem_tab = table(0), table(1)
    width = cell_tab.shape[1]
    at_lane = lax.broadcasted_iota(jnp.int32, (width, total), 0)
    slot = lax.broadcasted_iota(jnp.int32, (width, total), 1)
    spread_cell = (at_lane == own * slots + slot % slots).astype(jnp.float32).astype(jnp.bfloat16)
    spread_elem = (at_lane == slot % lists).astype(jnp.float32).astype(jnp.bfloat16)
    sender = lax.broadcasted_iota(jnp.int32, (senders, total), 0)
    slot = lax.broadcasted_iota(jnp.int32, (senders, total), 1)
    mine, owned = sender == slot // slots, sender == (slot // lists) * groups_x + own

    def spread(table, places, rows):
        moved = jnp.dot(table.astype(jnp.bfloat16), places, preferred_element_type=jnp.float32)
        return jnp.sum(jnp.where(rows, moved, 0.0), axis=0, keepdims=True)

    cell_tab = (cell_tab + 0.5).astype(jnp.int32)
    column = spread((cell_tab // size_z).astype(jnp.float32), spread_cell, mine)
    place_z = spread((cell_tab % size_z).astype(jnp.float32), spread_cell, mine)
    elems = spread(elem_tab, spread_elem, owned)
    column = (column + 0.5).astype(jnp.int32)
    place_z = (place_z + 0.5).astype(jnp.int32) - (zs - 4)
    elems = (elems + 1.5).astype(jnp.int32) - 1
    slot = lax.broadcasted_iota(jnp.int32, (1, total), 1)
    block = slot // lists
    place_x = (slot // slots % groups_x) * size_x + column // size_y
    place_y = column % size_y
    row_want = place_z * count_x + place_x
    lane_want = (block // groups_y) * count_y + (block % groups_y) * size_y + place_y
    hot_row = (lax.broadcasted_iota(jnp.int32, (4 * count_x, total), 0) == row_want).astype(jnp.float32)
    hot_row = hot_row.astype(jnp.bfloat16)
    hot_lane = lax.broadcasted_iota(jnp.int32, (lanes, total), 0) == lane_want
    picked = lax.dot_general(
        jnp.concatenate(halves(sens), axis=0), jnp.concatenate([hot_row, hot_row], axis=0),
        (((0,), (0,)), ((), ())), preferred_element_type=jnp.float32,
    )
    values = jnp.sum(jnp.where(hot_lane, picked, 0.0), axis=0, keepdims=True)
    hot_elem = (lax.broadcasted_iota(jnp.int32, (per_owner, total), 0) == elems).astype(jnp.float32)
    high = values.astype(jnp.bfloat16).astype(jnp.float32)
    both = jnp.where(lax.broadcasted_iota(jnp.int32, (8, total), 0) == 0, high, values - high)
    sums = lax.dot_general(
        both.astype(jnp.bfloat16), hot_elem.astype(jnp.bfloat16), (((1,), (1,)), ((), ())),
        preferred_element_type=jnp.float32,
    )
    sums = sums[:1] + sums[1:2]
    scale = 1.0 / math.sqrt(groups_x * groups_x * groups_y * groups_z * slots / NE)
    elem_ref[...] = sums * scale


def local(fields, adjoint, inv_eps, loss_level, direction, pattern_weight, voxel_cell, voxel_elem):
    size_x, size_y, size_z = inv_eps.shape
    groups_x, groups_y, groups_z = (lax.axis_size(a) for a in ("gx", "gy", "gz"))
    dims = (groups_x, groups_y, groups_z, size_x, size_y, size_z)
    slots = voxel_cell.shape[4]
    per_owner = NE // groups_x
    half = half_rows(groups_x * slots, size_y)
    nd = direction.shape[1]
    vmem = pl.BlockSpec(memory_space=pltpu.VMEM)
    hbm = pl.BlockSpec(memory_space=pltpu.HBM)

    def call(kernel, name, outs, *args, fetched=0, limit=48):
        scratch = [pltpu.VMEM(a.shape, a.dtype) for a in args[:fetched]]
        args = [
            pltpu.with_memory_space_constraint(a, pltpu.HBM) if i < fetched else a for i, a in enumerate(args)
        ]
        if fetched:
            scratch.append(pltpu.SemaphoreType.DMA((fetched,)))

        def located(*refs):
            kernel(dims, tuple(lax.axis_index(a) for a in ("gx", "gy", "gz")), *refs)

        return pl.pallas_call(
            located,
            out_shape=tuple(jax.ShapeDtypeStruct(o, jnp.float32) for o in outs),
            in_specs=[hbm] * fetched + [vmem] * (len(args) - fetched),
            out_specs=(vmem,) * len(outs),
            scratch_shapes=scratch,
            compiler_params=pltpu.CompilerParams(vmem_limit_bytes=limit * 1024 * 1024),
            name=name,
        )(*args)

    zrows = -(-(3 * HALO * size_x) // 8) * 8
    yrows = len(FORWARD) * size_x * HALO
    z_count, y_count = 1 if groups_z == 2 else 2, 1 if groups_y == 2 else 2
    send, *edges = call(
        first_kernel, "first",
        [(groups_x * groups_y, size_x * half, 4 * size_y)]
        + [(zrows, 4 * size_y)] * z_count + [(yrows, size_z)] * y_count,
        fields, adjoint, inv_eps, loss_level, voxel_cell.reshape(groups_x, slots),
        voxel_elem.reshape(groups_x, slots), fetched=6, limit=16,
    )
    z_top, z_bottom = edges[0], edges[z_count - 1]
    y_top, y_bottom = edges[z_count], edges[-1]
    z_low, z_high = neighbours("gz", z_top, z_bottom)
    z_sides = [z_low] if groups_z == 2 else [z_low, z_high]
    y_low, y_high = neighbours("gy", jnp.concatenate([y_top] + z_sides), jnp.concatenate([y_bottom] + z_sides))
    got = lax.all_to_all(send, ("gy", "gx"), split_axis=0, concat_axis=0, tiled=True)
    got = got.reshape(groups_x * groups_y * size_x * half, 4 * size_y)
    seen, _ = lax.optimization_barrier((direction, z_low))
    table_yz = halves_of_table(steering_yz(groups_y * size_y, groups_z, size_z, seen))
    rows = size_y + 8
    state, one, two = call(
        second_kernel, "second",
        [(8 * size_x + 2, rows, size_z + 128)] + [(5 * size_y + 24 + rows, size_z)] * 2,
        fields, inv_eps, loss_level, z_low, z_high, y_low, y_high,
    )
    seen, seen_weight, _ = lax.optimization_barrier((direction, pattern_weight, one))
    table_x = steering_x(groups_x * size_x, seen, seen_weight)

    one_side, other_side = (
        lax.ppermute(sent, "gx", [p for i in range(first, groups_x - 1, 2) for p in ((i, i + 1), (i + 1, i))])
        for first, sent in ((0, one), (1, two))
    )

    got, _ = lax.optimization_barrier((got, one))
    gots = [got] + [
        lax.ppermute(got, "gz", [(i, (i + s) % groups_z) for i in range(groups_z)]) for s in range(1, groups_z)
    ]

    pattern, elem = call(
        functools.partial(main_kernel, slots), "main", [(1, nd), (1, per_owner)],
        *gots, table_yz, table_x,
    )
    state, pattern = lax.optimization_barrier((state, pattern))
    (fields_out,) = call(
        third_kernel, "third", [(6, size_x, size_y, size_z)], state, one_side, other_side
    )
    return (fields_out, pattern.reshape(nd), elem.reshape(per_owner))


def solution(mesh):
    in_specs = (
        P(None, ("groups", "gx"), "gy", "gz"),
        P(None, ("groups", "gx"), "gy", "gz"),
        P(("groups", "gx"), "gy", "gz"),
        P(("groups", "gx"), "gy", "gz"),
        P(),
        P(),
        P(("groups", "gx"), "gy", "gz", None, None),
        P(("groups", "gx"), "gy", "gz", None, None),
    )
    out_specs = (P(None, ("groups", "gx"), "gy", "gz"), P("groups"), P(("groups", "gx")))
    return jax.shard_map(local, mesh=mesh, in_specs=in_specs, out_specs=out_specs, check_vma=False)
```

```python
import functools
import math

import jax
import jax.numpy as jnp
from jax import lax
from jax.experimental import pallas as pl
from jax.experimental.pallas import tpu as pltpu
from jax.sharding import PartitionSpec as P

STEPS = 2
NE = 1024
OMEGA = 0.9
KAPPA = 0.37
HIGHEST = lax.Precision.HIGHEST
HALO = 2
COMPS = (0, 1, 3, 4)

SETS = ((0, 1, 2, 3), (4, 6, 7, 12), (5, 13, 8, 9), (10, 11))
STARTS = (0, 9, 17, 24)
BODY = 28
LOWEST = (-6, -6, -6, -6, -6, -5, -6, -6, -6, -6, -6, -6, -6, -5)
TOPMOST = (2, 2, 1, 1, 1, 1, 1, 1, 0, 0, 0, 0, 1, 1)
FORWARD = (0, 1, 2, 3, 4, 5, 12, 13)


def coefficients(inv_eps, level):
    level = 0.15 * level
    return ((1.0 - level) / (1.0 + level), 0.5 * inv_eps / (1.0 + level))


def place_of(m):
    for t, members in enumerate(SETS):
        if m in members:
            return t, members.index(m)


def slab_place(m, k):
    t, q = place_of(m)
    if t == 3:
        return STARTS[t] + (k - LOWEST[m]) % 4, q + 2 * ((k - LOWEST[m]) // 4)
    return STARTS[t] + k - LOWEST[m], q


def half_rows(lists, size_y):
    return BODY if lists <= 2 * size_y else BODY + 4


def neighbours(axis, top, bottom):
    count = lax.axis_size(axis)
    if count == 2:
        other = lax.ppermute(top, axis, [(0, 1), (1, 0)])
        return other, other
    forward = [(i, i + 1) for i in range(count - 1)]
    return lax.ppermute(top, axis, forward), lax.ppermute(bottom, axis, [(t, s) for s, t in forward])


def fetch(pairs, sems):
    copies = [pltpu.make_async_copy(src, dst, sems.at[i]) for i, (src, dst) in enumerate(pairs)]
    for copy in copies:
        copy.start()
    for copy in copies:
        copy.wait()


def first_kernel(dims, at, *refs):
    groups_x, groups_y, groups_z, size_x, size_y, size_z = dims
    borders = 1 if groups_z == 2 else 2, 1 if groups_y == 2 else 2
    sources, refs = refs[:6], refs[6:]
    send_ref, refs = refs[0], refs[1:]
    z_refs, y_refs, refs = refs[: borders[0]], refs[borders[0] : sum(borders)], refs[sum(borders) :]
    f_ref, a_ref, ie_ref, ll_ref, cell_ref, elem_ref, sems = refs
    fetch(list(zip(sources, refs[:6])), sems)

    def array(m, x):
        if m < 6:
            return f_ref[m, x]
        if m < 12:
            return a_ref[m - 6, x]
        return ie_ref[x] if m == 12 else ll_ref[x].astype(jnp.float32)

    def store(targets, index, top, bottom):
        if len(targets) == 1:
            targets[0][...] = jnp.where(index == 0, top, bottom)
        else:
            targets[0][...], targets[1][...] = top, bottom

    zs = size_z // 2 + 2
    lists, slots = cell_ref.shape
    half = half_rows(lists * slots, size_y)
    per_row = (2 if half == BODY else 4) * size_y // slots
    tops, bottoms = [], []
    for x in range(size_x):
        parts = []
        for t, members in enumerate(SETS):
            blocks = [array(m, x) for m in members]
            blocks += [jnp.zeros((size_y, size_z), jnp.float32)] * (4 - len(members))
            flipped = jnp.concatenate(blocks, axis=0).T
            if t < 2:
                parts.append(flipped[zs + LOWEST[members[0]] : zs + TOPMOST[members[0]] + 1])
            else:
                first, last = (-5, -6) if t == 2 else (-6, -2)
                count, last_lanes = (7, slice(2 * size_y, None)) if t == 2 else (4, slice(0, 2 * size_y))
                left = flipped[zs + first : zs + first + count, : 2 * size_y]
                parts.append(jnp.concatenate([left, flipped[zs + last : zs + last + count, last_lanes]], axis=1))
            if t < 3:
                tops.append(flipped[size_z - HALO :])
                bottoms.append(flipped[:HALO])
        if x < 2:
            table = (cell_ref, elem_ref)[x][...].astype(jnp.float32)
            lines = []
            for r in range(0, lists, per_row):
                line = [table[i : i + 1] for i in range(r, min(r + per_row, lists))]
                if len(line) < per_row:
                    line.append(jnp.zeros((1, (per_row - len(line)) * slots), jnp.float32))
                lines.append(jnp.concatenate(line, axis=1))
            if half == BODY:
                last = jnp.concatenate([parts[0][8:, : 2 * size_y], lines[0]], axis=1)
                parts[0] = jnp.concatenate([parts[0][:8], last], axis=0)
            else:
                lines.append(jnp.zeros((half - BODY - len(lines), 4 * size_y), jnp.float32))
                parts += lines
        rows = jnp.concatenate(parts, axis=0)
        for d in range(groups_x * groups_y):
            send_ref[d, x * half : (x + 1) * half] = rows
    pad = [jnp.zeros((z_refs[0].shape[0] - HALO * len(tops), 4 * size_y), jnp.float32)]
    store(z_refs, at[2], jnp.concatenate(tops + pad, axis=0), jnp.concatenate(bottoms + pad, axis=0))
    layers = [array(m, x) for m in FORWARD for x in range(size_x)]
    top = jnp.concatenate([a[size_y - HALO :] for a in layers], axis=0)
    store(y_refs, at[1], top, jnp.concatenate([a[:HALO] for a in layers], axis=0))


def wide_masks(dims, at):
    _, _, _, _, size_y, size_z = dims
    shape = (size_y + 8, size_z + 128)
    row = lax.broadcasted_iota(jnp.int32, shape, 0)
    lane = lax.broadcasted_iota(jnp.int32, shape, 1)
    out_y = jnp.logical_and(row >= size_y + 4, at[1] == 0)
    out_z = jnp.logical_and(lane >= size_z + 64, at[2] == 0)
    return jnp.where(jnp.logical_or(out_y, out_z), 0.0, 0.5)


def forward_y(a):
    return pltpu.roll(a, a.shape[0] - 1, 0) - a


def forward_z(a):
    return pltpu.roll(a, a.shape[1] - 1, 1) - a


def backward_y(a):
    return a - pltpu.roll(a, 1, 0)


def backward_z(a):
    return a - pltpu.roll(a, 1, 1)


def pack(planes, size_y, size_z):
    row = lax.broadcasted_iota(jnp.int32, (8, size_z), 0)
    own = jnp.logical_or(row < 2, row >= 6)
    lane = lax.broadcasted_iota(jnp.int32, (planes[0].shape[0], 128), 1)
    out = [plane[:size_y, :size_z] for plane in planes]
    for p in range(0, len(planes), 2):
        tile = planes[p][size_y:, :size_z]
        if p + 1 < len(planes):
            tile = jnp.where(own, tile, pltpu.roll(planes[p + 1][size_y:, :size_z], 4, 0))
        out.append(tile)
    border = jnp.zeros((planes[0].shape[0], 128), jnp.float32)
    for p, plane in enumerate(planes):
        moved = pltpu.roll(plane[:, size_z:], 8 * p + 2, 1)
        border = jnp.where(jnp.logical_and(lane >= 8 * p, lane < 8 * p + 4), moved, border)
    return jnp.concatenate(out + [border], axis=0)


def unpack(rows, count, size_y):
    tiles = count * size_y
    border = rows[tiles + 8 * ((count + 1) // 2) :]
    out = []
    for p in range(count):
        tile = rows[tiles + 8 * (p // 2) : tiles + 8 * (p // 2) + 8]
        body = jnp.concatenate(
            [rows[p * size_y : (p + 1) * size_y], pltpu.roll(tile, 4, 0) if p % 2 else tile], axis=0
        )
        out.append(jnp.concatenate([body, pltpu.roll(border, 128 - (8 * p + 2), 1)], axis=1))
    return out


def second_kernel(dims, at, f_ref, ie_ref, ll_ref, zl_ref, zh_ref, yl_ref, yh_ref, state_ref, one_ref, two_ref):
    groups_x, groups_y, groups_z, size_x, size_y, size_z = dims
    zrows = zl_ref.shape[0]
    lane = lax.broadcasted_iota(jnp.int32, (8, 128), 1)
    high_lane = jnp.logical_and(lane < HALO, at[2] < groups_z - 1)
    low_lane = jnp.logical_and(lane >= 128 - HALO, at[2] > 0)
    y_high = (at[1] < groups_y - 1).astype(jnp.float32)
    y_low = (at[1] > 0).astype(jnp.float32)

    def flip(a):
        return jnp.concatenate([a, jnp.zeros((128 - zrows, a.shape[1]), jnp.float32)], axis=0).T

    own_low, own_high = flip(zl_ref[...]), flip(zh_ref[...])
    edge = HALO * size_x * len(FORWARD)
    after = edge if groups_z == 2 else edge + zrows
    yl_low, yl_high = flip(yl_ref[edge : edge + zrows]), flip(yl_ref[after : after + zrows])
    yh_low, yh_high = flip(yh_ref[edge : edge + zrows]), flip(yh_ref[after : after + zrows])

    def column(low, high, rows, at):
        reps = rows // 8
        hl = jnp.concatenate([high_lane] * reps, axis=0)
        ll = jnp.concatenate([low_lane] * reps, axis=0)
        moved_high = pltpu.roll(high, (128 - at) % 128, 1)
        moved_low = pltpu.roll(low, (128 - HALO - at) % 128, 1)
        return jnp.where(hl, moved_high, jnp.where(ll, moved_low, 0.0))

    def wide(m, x):
        t, q = place_of(m)
        at = (x * 3 + t) * HALO
        if m < 6:
            body = f_ref[m, x]
        else:
            body = ie_ref[x] if m == 12 else ll_ref[x].astype(jnp.float32)
        rows = slice(q * size_y, (q + 1) * size_y)
        body_z = column(own_low[rows], own_high[rows], size_y, at)
        start = (FORWARD.index(m) * size_x + x) * HALO
        blank = jnp.zeros((8 - 2 * HALO, 128), jnp.float32)
        first, last = q * size_y, (q + 1) * size_y
        tile = jnp.concatenate(
            [yh_ref[start : start + HALO] * y_high, blank, yl_ref[start : start + HALO] * y_low], axis=0
        )
        low = jnp.concatenate(
            [yh_low[first : first + HALO] * y_high, blank, yl_low[last - HALO : last] * y_low], axis=0
        )
        high = jnp.concatenate(
            [yh_high[first : first + HALO] * y_high, blank, yl_high[last - HALO : last] * y_low], axis=0
        )
        corner = column(low, high, 8, at)
        return jnp.concatenate(
            [jnp.concatenate([body, body_z], axis=1), jnp.concatenate([tile, corner], axis=1)], axis=0
        )

    half = wide_masks(dims, at)
    xs = range(size_x)
    ex, ey, ez, hx, hy, hz, ie, lv = ([wide(m, x) for x in xs] for m in FORWARD)
    pairs = [coefficients(ie[x], lv[x]) for x in xs]
    ca, cb = [p[0] for p in pairs], [p[1] for p in pairs]
    nothing = jnp.zeros_like(half)
    hx = [hx[x] - half * (forward_y(ez[x]) - forward_z(ey[x])) for x in xs]
    hy = [hy[x] - half * (forward_z(ex[x]) - ((ez[x + 1] if x + 1 < size_x else nothing) - ez[x])) for x in xs]
    hz = [hz[x] - half * (((ey[x + 1] if x + 1 < size_x else nothing) - ey[x]) - forward_y(ex[x])) for x in xs]
    first_ey, first_ez = ey[0], ez[0]
    ex = [ca[x] * ex[x] + cb[x] * (backward_y(hz[x]) - backward_z(hy[x])) for x in xs]
    ey = [ca[x] * ey[x] + cb[x] * (backward_z(hx[x]) - (hz[x] - (hz[x - 1] if x else nothing))) for x in xs]
    ez = [ca[x] * ez[x] + cb[x] * ((hy[x] - (hy[x - 1] if x else nothing)) - backward_y(hx[x])) for x in xs]
    state = [*ex, *ey, *ez, *hx, *hy, *hz, *ca, *cb, first_ey, first_ez]
    for i, a in enumerate(state):
        state_ref[i] = a
    next_hy = hy[-1] - half * (forward_z(ex[-1]) + ez[-1])
    next_hz = hz[-1] + half * (ey[-1] + forward_y(ex[-1]))
    up = pack([hy[-1], hz[-1], next_hy, next_hz, cb[-1]], size_y, size_z)
    down = pack([first_ey, first_ez, ey[0], ez[0], cb[0]], size_y, size_z)
    even = lax.rem(at[0], 2) == 0
    one_ref[...] = jnp.where(even, up, down)
    two_ref[...] = jnp.where(even, down, up)


def third_kernel(dims, at, state_ref, one_ref, two_ref, out_ref):
    groups_x, groups_y, groups_z, size_x, size_y, size_z = dims
    xs = range(size_x)
    half = wide_masks(dims, at)
    half_low = half * (at[0] > 0).astype(jnp.float32)
    state = [[state_ref[i * size_x + x] for x in xs] for i in range(8)]
    ex, ey, ez, hx, hy, hz, ca, cb = state
    first_ey, first_ez = state_ref[8 * size_x], state_ref[8 * size_x + 1]
    even = lax.rem(at[0], 2) == 0
    one, two = one_ref[...], two_ref[...]
    low_hy, low_hz, below_hy, below_hz, low_cb = unpack(jnp.where(even, two, one), 5, size_y)
    next_ey, next_ez, high_ey, high_ez, high_cb = unpack(jnp.where(even, one, two), 5, size_y)
    add_y, add_z = half * next_ez, -(half * next_ey)
    hy[-1], hz[-1] = hy[-1] + add_y, hz[-1] + add_z
    ex[-1] = ex[-1] + cb[-1] * (backward_y(add_z) - backward_z(add_y))
    ey[-1] = ey[-1] - cb[-1] * add_z
    ez[-1] = ez[-1] + cb[-1] * add_y
    add_y, add_z = half_low * first_ez, -(half_low * first_ey)
    low_hy, low_hz = low_hy + add_y, low_hz + add_z
    more_ex = low_cb * (backward_y(add_z) - backward_z(add_y))
    more_ey, more_ez = -(low_cb * add_z), low_cb * add_y
    ey[0] = ey[0] + cb[0] * low_hz
    ez[0] = ez[0] - cb[0] * low_hy
    high_ey = high_ey + high_cb * hz[-1]
    high_ez = high_ez - high_cb * hy[-1]
    low_hy = below_hy + add_y - half_low * (forward_z(more_ex) + more_ez - ez[0])
    low_hz = below_hz + add_z + half_low * (more_ey + forward_y(more_ex) - ey[0])
    after_ey, after_ez = ey[1:] + [high_ey], ez[1:] + [high_ez]
    hx = [hx[x] - half * (forward_y(ez[x]) - forward_z(ey[x])) for x in xs]
    hy = [hy[x] - half * (forward_z(ex[x]) - (after_ez[x] - ez[x])) for x in xs]
    hz = [hz[x] - half * ((after_ey[x] - ey[x]) - forward_y(ex[x])) for x in xs]
    before_hy, before_hz = [low_hy] + hy[:-1], [low_hz] + hz[:-1]
    for x in xs:
        new = (
            ca[x] * ex[x] + cb[x] * (backward_y(hz[x]) - backward_z(hy[x])),
            ca[x] * ey[x] + cb[x] * (backward_z(hx[x]) - (hz[x] - before_hz[x])),
            ca[x] * ez[x] + cb[x] * ((hy[x] - before_hy[x]) - backward_y(hx[x])),
            hx[x], hy[x], hz[x],
        )
        for m in range(6):
            out_ref[m, x] = new[m][:size_y, :size_z]


def halves_of_table(a):
    high = lax.reduce_precision(a, 8, 7)
    return jnp.concatenate([high, a - high], axis=0).astype(jnp.bfloat16)


def halves(a):
    high = a.astype(jnp.bfloat16)
    return high, (a - high.astype(jnp.float32)).astype(jnp.bfloat16)


def product(a, table_ref, contract):
    rows, size = a.shape[0], table_ref.shape[0] // 2
    high, low = halves(a)
    if contract == 0:
        nothing = jnp.zeros_like(low)
        left = jnp.concatenate(
            [jnp.concatenate([high, high], axis=1), jnp.concatenate([low, nothing], axis=1)], axis=0
        )
    else:
        left = jnp.concatenate([high, low], axis=0)
    dims = (((1,), (contract,)), ((), ()))
    both = lax.dot_general(left, table_ref[...], dims, preferred_element_type=jnp.float32)
    if contract == 0:
        return both[:rows] + both[rows:]
    return both[:rows, :size] + (both[rows:, :size] + both[:rows, size:])


def steering_x(count_x, direction, weight):
    phase = KAPPA * jnp.arange(count_x, dtype=jnp.float32)[:, None] * direction[0]
    return jnp.concatenate([jnp.cos(phase), jnp.sin(phase), jnp.broadcast_to(weight, phase.shape)], axis=1)


def steering_yz(count_y, groups_z, size_z, direction, own):
    ys = jnp.arange(count_y, dtype=jnp.float32)[None, :, None]
    core = (own - jnp.arange(groups_z, dtype=jnp.int32) + groups_z) % groups_z
    zval = (core * size_z + size_z // 2 + 2).astype(jnp.float32)[:, None, None]
    phase = (KAPPA * (ys * direction[1] + zval * direction[2])).reshape(groups_z * count_y, -1)
    return jnp.concatenate([jnp.cos(phase), jnp.sin(phase)], axis=1)


def main_kernel(slots, dims, at, *refs):
    groups_x, groups_y, groups_z, size_x, size_y, size_z = dims
    got_refs = refs[:groups_z]
    table_ref, x_ref, pattern_ref, elem_ref = refs[groups_z:]
    per_owner = NE // groups_x
    half = half_rows(groups_x * slots, size_y)
    count_x, count_y = groups_x * size_x, groups_y * size_y
    lanes = groups_z * count_y
    zs = size_z // 2 + 2

    def pick(c, start, size, stride):
        return got_refs[c][pl.ds(start, size, stride=stride), :]

    loaded = {}

    def plane(m, k):
        row, q = slab_place(m, k)
        if row not in loaded:
            loaded[row] = [
                pick(c, b * groups_x * size_x * half + row, count_x, half)
                for c in range(groups_z)
                for b in range(groups_y)
            ]
        return jnp.concatenate([p[:, q * size_y : (q + 1) * size_y] for p in loaded[row]], axis=1)

    row_id = lax.broadcasted_iota(jnp.int32, (count_x, lanes), 0)
    lane_id = lax.broadcasted_iota(jnp.int32, (count_x, lanes), 1) % count_y
    x_up, x_low = row_id < count_x - 1, row_id > 0
    y_up, y_low = lane_id < count_y - 1, lane_id > 0

    def dxp(a):
        return jnp.where(x_up, pltpu.roll(a, count_x - 1, 0), 0.0) - a

    def dyp(a):
        return jnp.where(y_up, pltpu.roll(a, lanes - 1, 1), 0.0) - a

    def dxm(a):
        return a - jnp.where(x_low, pltpu.roll(a, 1, 0), 0.0)

    def dym(a):
        return a - jnp.where(y_low, pltpu.roll(a, 1, 1), 0.0)

    ca, cb = {}, {}
    for k in range(-5, 2):
        ca[k], cb[k] = coefficients(plane(12, k), plane(13, k))

    def step(ex, ey, ez, hx, hy, hz, low, high):
        nhx = {k: hx[k] - 0.5 * (dyp(ez[k]) - (ey[k + 1] - ey[k])) for k in range(low - 1, high + 1)}
        nhy = {k: hy[k] - 0.5 * ((ex[k + 1] - ex[k]) - dxp(ez[k])) for k in range(low - 1, high + 1)}
        nhz = {k: hz[k] - 0.5 * (dxp(ey[k]) - dyp(ex[k])) for k in range(low, high + 1)}
        nex = {k: ca[k] * ex[k] + cb[k] * (dym(nhz[k]) - (nhy[k] - nhy[k - 1])) for k in range(low, high + 1)}
        ney = {k: ca[k] * ey[k] + cb[k] * ((nhx[k] - nhx[k - 1]) - dxm(nhz[k])) for k in range(low, high + 1)}
        nez = {k: ca[k] * ez[k] + cb[k] * (dxm(nhy[k]) - dym(nhx[k])) for k in range(low, high + 1)}
        return nex, ney, nez, nhx, nhy, nhz

    def arrays(first):
        return [
            {k: plane(m, k) for k in range(LOWEST[m], TOPMOST[m] + 1)} for m in range(first, first + 6)
        ]

    u1 = step(*arrays(0), -5, 1)
    u2 = step(*u1, -4, 0)
    rows = []
    for m in (0, 1, 3, 4):
        rows.append(u1[m][0] * math.cos(OMEGA) + u2[m][0] * math.cos(2 * OMEGA))
        rows.append(-u1[m][0] * math.sin(OMEGA) - u2[m][0] * math.sin(2 * OMEGA))
    dft = jnp.concatenate(rows, axis=0)

    nd = table_ref.shape[1] // 2
    cos_x, sin_x, weight = x_ref[:, :nd], x_ref[:, nd : 2 * nd], x_ref[:1, 2 * nd :]
    amp = 1.0 / math.sqrt(count_x * count_y * groups_z)
    prod = product(dft, table_ref, 0)
    pattern = jnp.zeros((1, nd), jnp.float32)
    weight = (2.0 * amp) * weight
    mixing = []
    for c in range(4):
        re = prod[2 * c * count_x : (2 * c + 1) * count_x]
        im = prod[(2 * c + 1) * count_x : (2 * c + 2) * count_x]
        real = re[:, :nd] - im[:, nd:]
        imag = re[:, nd:] + im[:, :nd]
        far_re = amp * jnp.sum(real * cos_x - imag * sin_x, axis=0, keepdims=True)
        far_im = amp * jnp.sum(real * sin_x + imag * cos_x, axis=0, keepdims=True)
        pattern = pattern + far_re * far_re + far_im * far_im
        out_re, out_im = weight * far_re, weight * far_im
        b_re = out_re * cos_x + out_im * sin_x
        b_im = out_im * cos_x - out_re * sin_x
        mixing.append(jnp.concatenate([b_re, b_im], axis=1))
        mixing.append(jnp.concatenate([b_im, -b_re], axis=1))
    pattern_ref[...] = pattern

    src = product(jnp.concatenate(mixing, axis=0), table_ref, 1)

    def with_sources(state, when):
        state = [dict(a) for a in state]
        for c, m in enumerate((0, 1, 3, 4)):
            gre = src[2 * c * count_x : (2 * c + 1) * count_x]
            gim = src[(2 * c + 1) * count_x : (2 * c + 2) * count_x]
            state[m][0] = state[m][0] + (gre * math.cos(OMEGA * when) - gim * math.sin(OMEGA * when))
        return state

    v1 = step(*with_sources(arrays(6), 2), -5, 0)
    v2 = step(*with_sources(v1, 1), -4, -1)
    sens = [
        sum(v1[m][k] * u2[m][k] for m in range(3)) + sum(v2[m][k] * u1[m][k] for m in range(3))
        for k in range(-4, 0)
    ]
    sens = jnp.concatenate(sens, axis=0)

    own = at[0]
    senders = groups_x * groups_y * groups_z
    total = senders * slots
    lists = groups_x * slots
    row, lane = (8, 2 * size_y) if half == BODY else (BODY, 0)
    pieces = range(-(-lists // (4 * size_y - lane)))

    def table(x):
        def piece(r):
            return jnp.concatenate(
                [pick(c, x * half + row + r, groups_x * groups_y, size_x * half)[:, lane:] for c in range(groups_z)], axis=0
            )

        return jnp.concatenate([piece(r) for r in pieces], axis=1)

    cell_tab, elem_tab = table(0), table(1)
    width = cell_tab.shape[1]
    at_lane = lax.broadcasted_iota(jnp.int32, (width, total), 0)
    slot = lax.broadcasted_iota(jnp.int32, (width, total), 1)
    spread_cell = (at_lane == own * slots + slot % slots).astype(jnp.float32).astype(jnp.bfloat16)
    spread_elem = (at_lane == slot % lists).astype(jnp.float32).astype(jnp.bfloat16)
    sender = lax.broadcasted_iota(jnp.int32, (senders, total), 0)
    slot = lax.broadcasted_iota(jnp.int32, (senders, total), 1)
    mine, owned = sender == slot // slots, sender == (slot // lists) * groups_x + own

    def spread(table, places, rows):
        moved = jnp.dot(table.astype(jnp.bfloat16), places, preferred_element_type=jnp.float32)
        return jnp.sum(jnp.where(rows, moved, 0.0), axis=0, keepdims=True)

    cell_tab = (cell_tab + 0.5).astype(jnp.int32)
    column = spread((cell_tab // size_z).astype(jnp.float32), spread_cell, mine)
    place_z = spread((cell_tab % size_z).astype(jnp.float32), spread_cell, mine)
    elems = spread(elem_tab, spread_elem, owned)
    column = (column + 0.5).astype(jnp.int32)
    place_z = (place_z + 0.5).astype(jnp.int32) - (zs - 4)
    elems = (elems + 1.5).astype(jnp.int32) - 1
    slot = lax.broadcasted_iota(jnp.int32, (1, total), 1)
    block = slot // lists
    place_x = (slot // slots % groups_x) * size_x + column // size_y
    place_y = column % size_y
    row_want = place_z * count_x + place_x
    lane_want = (block // groups_y) * count_y + (block % groups_y) * size_y + place_y
    hot_row = (lax.broadcasted_iota(jnp.int32, (4 * count_x, total), 0) == row_want).astype(jnp.float32)
    hot_row = hot_row.astype(jnp.bfloat16)
    hot_lane = lax.broadcasted_iota(jnp.int32, (lanes, total), 0) == lane_want
    picked = lax.dot_general(
        jnp.concatenate(halves(sens), axis=0), jnp.concatenate([hot_row, hot_row], axis=0),
        (((0,), (0,)), ((), ())), preferred_element_type=jnp.float32,
    )
    values = jnp.sum(jnp.where(hot_lane, picked, 0.0), axis=0, keepdims=True)
    hot_elem = (lax.broadcasted_iota(jnp.int32, (per_owner, total), 0) == elems).astype(jnp.float32)
    high = values.astype(jnp.bfloat16).astype(jnp.float32)
    both = jnp.where(lax.broadcasted_iota(jnp.int32, (8, total), 0) == 0, high, values - high)
    sums = lax.dot_general(
        both.astype(jnp.bfloat16), hot_elem.astype(jnp.bfloat16), (((1,), (1,)), ((), ())),
        preferred_element_type=jnp.float32,
    )
    sums = sums[:1] + sums[1:2]
    scale = 1.0 / math.sqrt(groups_x * groups_x * groups_y * groups_z * slots / NE)
    elem_ref[...] = sums * scale


def local(fields, adjoint, inv_eps, loss_level, direction, pattern_weight, voxel_cell, voxel_elem):
    size_x, size_y, size_z = inv_eps.shape
    groups_x, groups_y, groups_z = (lax.axis_size(a) for a in ("gx", "gy", "gz"))
    dims = (groups_x, groups_y, groups_z, size_x, size_y, size_z)
    slots = voxel_cell.shape[4]
    per_owner = NE // groups_x
    half = half_rows(groups_x * slots, size_y)
    nd = direction.shape[1]
    vmem = pl.BlockSpec(memory_space=pltpu.VMEM)
    hbm = pl.BlockSpec(memory_space=pltpu.HBM)

    def call(kernel, name, outs, *args, fetched=0, limit=48):
        scratch = [pltpu.VMEM(a.shape, a.dtype) for a in args[:fetched]]
        args = [
            pltpu.with_memory_space_constraint(a, pltpu.HBM) if i < fetched else a for i, a in enumerate(args)
        ]
        if fetched:
            scratch.append(pltpu.SemaphoreType.DMA((fetched,)))

        def located(*refs):
            kernel(dims, tuple(lax.axis_index(a) for a in ("gx", "gy", "gz")), *refs)

        return pl.pallas_call(
            located,
            out_shape=tuple(jax.ShapeDtypeStruct(o, jnp.float32) for o in outs),
            in_specs=[hbm] * fetched + [vmem] * (len(args) - fetched),
            out_specs=(vmem,) * len(outs),
            scratch_shapes=scratch,
            compiler_params=pltpu.CompilerParams(vmem_limit_bytes=limit * 1024 * 1024),
            name=name,
        )(*args)

    zrows = -(-(3 * HALO * size_x) // 8) * 8
    yrows = len(FORWARD) * size_x * HALO
    z_count, y_count = 1 if groups_z == 2 else 2, 1 if groups_y == 2 else 2
    send, *edges = call(
        first_kernel, "first",
        [(groups_x * groups_y, size_x * half, 4 * size_y)]
        + [(zrows, 4 * size_y)] * z_count + [(yrows, size_z)] * y_count,
        fields, adjoint, inv_eps, loss_level, voxel_cell.reshape(groups_x, slots),
        voxel_elem.reshape(groups_x, slots), fetched=6, limit=16,
    )
    z_top, z_bottom = edges[0], edges[z_count - 1]
    y_top, y_bottom = edges[z_count], edges[-1]
    z_low, z_high = neighbours("gz", z_top, z_bottom)
    z_sides = [z_low] if groups_z == 2 else [z_low, z_high]
    y_low, y_high = neighbours("gy", jnp.concatenate([y_top] + z_sides), jnp.concatenate([y_bottom] + z_sides))
    got = lax.all_to_all(send, ("gy", "gx"), split_axis=0, concat_axis=0, tiled=True)
    got = got.reshape(groups_x * groups_y * size_x * half, 4 * size_y)
    seen, _ = lax.optimization_barrier((direction, z_low))
    table_yz = halves_of_table(
        steering_yz(groups_y * size_y, groups_z, size_z, seen, lax.axis_index("gz"))
    )
    rows = size_y + 8
    state, one, two = call(
        second_kernel, "second",
        [(8 * size_x + 2, rows, size_z + 128)] + [(5 * size_y + 24 + rows, size_z)] * 2,
        fields, inv_eps, loss_level, z_low, z_high, y_low, y_high,
    )
    seen, seen_weight, _ = lax.optimization_barrier((direction, pattern_weight, one))
    table_x = steering_x(groups_x * size_x, seen, seen_weight)

    one_side, other_side = (
        lax.ppermute(sent, "gx", [p for i in range(first, groups_x - 1, 2) for p in ((i, i + 1), (i + 1, i))])
        for first, sent in ((0, one), (1, two))
    )

    got, _ = lax.optimization_barrier((got, one))
    gots = [got] + [
        lax.ppermute(got, "gz", [(i, (i + s) % groups_z) for i in range(groups_z)]) for s in range(1, groups_z)
    ]

    pattern, elem = call(
        functools.partial(main_kernel, slots), "main", [(1, nd), (1, per_owner)],
        *gots, table_yz, table_x,
    )
    state, pattern = lax.optimization_barrier((state, pattern))
    (fields_out,) = call(
        third_kernel, "third", [(6, size_x, size_y, size_z)], state, one_side, other_side
    )
    return (fields_out, pattern.reshape(nd), elem.reshape(per_owner))


def solution(mesh):
    in_specs = (
        P(None, ("groups", "gx"), "gy", "gz"),
        P(None, ("groups", "gx"), "gy", "gz"),
        P(("groups", "gx"), "gy", "gz"),
        P(("groups", "gx"), "gy", "gz"),
        P(),
        P(),
        P(("groups", "gx"), "gy", "gz", None, None),
        P(("groups", "gx"), "gy", "gz", None, None),
    )
    out_specs = (P(None, ("groups", "gx"), "gy", "gz"), P("groups"), P(("groups", "gx")))
    return jax.shard_map(local, mesh=mesh, in_specs=in_specs, out_specs=out_specs, check_vma=False)
```
